128 devices in a mesh: req: 4 (over z), exp: 32 (over y, x, core).
Axes of the slice: x: 4, y: 4, z: 4, core: 2. Of those that a mesh axis runs over, the one named last changes fastest.
Arguments:
- hidden: bfloat16 [16384, 1536], P(('req', 'exp')), may hold values from -6 to 6
- attn_gain: float32 [1536], replicated, may hold values from 0.5 to 1.5
- query_weight: bfloat16 [1536, 1536], replicated
- key_matrix: bfloat16 [1536, 512], replicated
- value_matrix: bfloat16 [1536, 512], replicated, may hold values from -0.15625 to 0.15625
- output_weight: bfloat16 [1536, 1536], replicated, may hold values from -0.15625 to 0.15625
- prompt_start: int32 [16384], P(('req', 'exp')), may hold values from 0 to 4095, as said below
- ffn_gain: float32 [1536], replicated, may hold values from 0.5 to 1.5
- routes: int32 [16384, 8], P(('req', 'exp')), may hold values from 0 to 31, all different within a row; in each aligned block of 128 rows (0 to 127, 128 to 255, ...) at most 64 rows name the same one
- route_weights: float32 [16384, 8], P(('req', 'exp')), may hold values from 0.02 to 0.3
- expert_weights: bfloat16 [32, 3, 1536, 512], P('exp', None, None, 'req'), may hold values from -0.15625 to 0.15625
Outputs:
- layer_out: bfloat16 [16384, 1536], P(('req', 'exp'))
- rotated_key_cache: bfloat16 [16384, 512], P(('req', 'exp'))
- value_cache: bfloat16 [16384, 512], P(('req', 'exp'))
The draws below stay inside these ranges and needn't reach their ends.
Inputs may be any that keep to these rules, and one draw needn't show every extreme that they name: prompt_start never falls along a stream, is at most the token's own position in it, is 0 at each stream's first position, and tokens of one stream with the same value form one prompt; each stream's last position begins a prompt of its own. `routes`: each row names 8 different experts; among the rows of one device no expert is named by more than 64 rows, a bound that some block reaches.
All inputs are finite; a program needn't handle non-finite values.
Results may differ from the reference program's by a relative error of at most 0.0096.
Values may be sent and summed in bfloat16 or wider, within the bound.
A program may use at most 192 MiB of HBM per device.

```python
import math
import jax
import jax.numpy as jnp
import numpy as np
from jax import lax

MODEL_WIDTH = 1536
QUERY_HEADS = 24
KEY_VALUE_HEADS = 8
HEAD_SIZE = 64
FF = 512
TOP = 8
TOK_DEV = 128
EXPERTS = 32
CAP = 64
STREAM = 4096
ALL_POSITIONS = 16384
N_REQ = 4


gap_odds = 64


def query_value_pair(key):
    inner = jax.random.fold_in(key, 11)
    base_values = jax.random.normal(inner, (MODEL_WIDTH, QUERY_HEADS * HEAD_SIZE), jnp.float32)
    return base_values * MODEL_WIDTH ** (-0.5)


def draw_query_weight(key, part):
    return query_value_pair(key).astype(jnp.bfloat16)


def draw_key_matrix(key, part):
    shard_values = jax.random.normal(jax.random.fold_in(key, 12), (MODEL_WIDTH, KEY_VALUE_HEADS, HEAD_SIZE), jnp.float32) * MODEL_WIDTH ** (-0.5)
    return shard_values.reshape(MODEL_WIDTH, KEY_VALUE_HEADS * HEAD_SIZE).astype(jnp.bfloat16)


def draw_prompt_start(key, part):
    first_key = jax.random.fold_in(key, 21)
    length_key = jax.random.fold_in(key, 22)
    gap_key = jax.random.fold_in(key, 23)
    lead = jax.random.randint(first_key, (N_REQ, 1), 0, TOK_DEV)
    long_len = jax.random.randint(length_key, (N_REQ, 1), STREAM // 2 + 2 * TOK_DEV, STREAM - TOK_DEV + 1)
    positions = jnp.arange(STREAM, dtype=jnp.int32)[None, :]
    inside = (positions > lead) & (positions < lead + long_len)
    random_cut = jax.random.randint(gap_key, (N_REQ, STREAM), 0, gap_odds) == 0
    boundary = (positions == 0) | (positions == STREAM - 1) | (positions == lead) | (positions == lead + long_len) | random_cut & jnp.logical_not(inside)
    marks = jnp.where(boundary, positions, 0)
    starts = lax.cummax(marks, axis=1)
    return starts.reshape(-1).astype(jnp.int32)


def steps_of(stream_key, extent, cuts, least, top_value):
    level = 1.0
    for position, shards_of in cuts:
        draws = jax.random.uniform(jax.random.fold_in(jax.random.fold_in(stream_key, 6), position), (shards_of,), jnp.float32, least / len(cuts), top_value / len(cuts))
        level = level * jnp.repeat(jnp.exp(draws), extent[position] // shards_of).reshape((-1,) + (1,) * (len(extent) - 1 - position))
    return level


def assign_block(key, own, number, rows, count, top, bound, slope):
    order = jax.random.permutation(key, count)
    crowded, common = load_shares(count, rows * top, bound, slope, True), load_shares(count, rows * top, bound, slope, False)
    places = jnp.arange(count)

    def named(tallies, rotation):
        used = int((tallies > 0).sum())
        fixed = max(1, used // 4)
        shifted = fixed + (places - fixed + rotation * (used - fixed)) % max(1, count - fixed)
        return jnp.zeros((count,), jnp.int32).at[order[jnp.where(places < fixed, places, shifted)]].set(jnp.asarray(tallies, jnp.int32))

    tallies = jnp.where(number % 4 == 0, named(crowded, number // 4), named(common, number - number // 4 - 1))
    mixed = jax.random.permutation(jax.random.fold_in(own, 3), count)
    giver, sink = mixed[0:count // 2 * 2:2], mixed[1:count // 2 * 2:2]
    room = jnp.minimum(tallies[giver] - 1, bound - tallies[sink]) // 2
    room = jnp.where((giver == order[0]) | (sink == order[0]) | (tallies[sink] == 0), 0, jnp.maximum(room, 0))
    shifted = jax.random.randint(jax.random.fold_in(own, 4), (count // 2,), 0, 1 << 20) % (room + 1)
    tallies = tallies.at[giver].add(-shifted).at[sink].add(shifted)
    items = jnp.searchsorted(jnp.cumsum(tallies), jnp.arange(rows * top), side="right").astype(jnp.int32)
    grid = items.reshape(top, rows).T
    grid = grid[jax.random.permutation(jax.random.fold_in(own, 1), rows)]
    rotation = jax.random.randint(jax.random.fold_in(own, 2), (rows, 1), 0, top)
    return jnp.take_along_axis(grid, (jnp.arange(top)[None, :] + rotation) % top, axis=1)


def load_shares(number_of, total, most, lean, full):
    loads = [(1 << 20) // math.isqrt(standing ** lean) + 1 for standing in range(1, number_of + 1)]
    largest = most if full else min(most, max(-(-total // number_of), total * loads[0] // sum(loads)))
    least = 1 if total - largest >= number_of - 1 else 0
    given, surplus = [largest] + [least] * (number_of - 1), total - largest - least * (number_of - 1)
    while surplus > 0:
        free = [i for i in range(1, number_of) if given[i] < largest] or [i for i in range(1, number_of) if given[i] < most]
        mass, left = sum([loads[i] for i in free]), surplus
        for i in free:
            more = min(most - given[i], max(1, left * loads[i] // mass), surplus)
            given[i] = given[i] + more
            surplus = surplus - more
    return np.array(given)


def scatter_about(own_key, extent, spread, reach, shards=(), kind=jnp.bfloat16):
    array = jax.random.normal(own_key, extent, jnp.float32) * spread
    if len(shards) > 0:
        array = steps_of(own_key, extent, shards, -0.22, 0.18) * array
    return jnp.clip(array, min=-reach, max=reach).astype(kind)


def setup_inputs(seed: int = 0) -> dict:
    seeds = jax.random.split(jax.random.key(seed), 12)
    hidden = scatter_about(seeds[0], (ALL_POSITIONS, MODEL_WIDTH), 1.0, 6.0, ((0, 128),))
    attn_gain = jnp.clip(1.0 + 0.1 * jax.random.normal(seeds[1], (MODEL_WIDTH,), jnp.float32), 0.5, 1.5)
    query_weight = draw_query_weight(jax.random.fold_in(seeds[11], 71), 0)
    key_matrix = draw_key_matrix(jax.random.fold_in(seeds[11], 71), 0)
    value_matrix = scatter_about(seeds[4], (MODEL_WIDTH, KEY_VALUE_HEADS * HEAD_SIZE), MODEL_WIDTH ** -0.5, 0.15625)
    output_weight = scatter_about(seeds[5], (QUERY_HEADS * HEAD_SIZE, MODEL_WIDTH), (QUERY_HEADS * HEAD_SIZE) ** -0.5, 0.15625)
    prompt_start = draw_prompt_start(jax.random.fold_in(seeds[11], 71), 0)
    ffn_gain = jnp.clip(1.0 + 0.1 * jax.random.normal(seeds[7], (MODEL_WIDTH,), jnp.float32), 0.5, 1.5)
    routes_keys = jax.random.split(jax.random.fold_in(seeds[8], 1), ALL_POSITIONS // TOK_DEV)
    routes_turns = jax.random.permutation(jax.random.fold_in(seeds[8], 3), ALL_POSITIONS // TOK_DEV)
    routes = jax.vmap(lambda own, number: assign_block(jax.random.fold_in(seeds[8], 2), own, number, TOK_DEV, EXPERTS, TOP, CAP, 1))(routes_keys, routes_turns).reshape((ALL_POSITIONS, TOP))
    route_weights = jnp.clip(jnp.exp(math.log(0.3) - 2.7080503 * jax.random.uniform(seeds[9], (ALL_POSITIONS, TOP), jnp.float32) ** steps_of(seeds[9], (ALL_POSITIONS, TOP), ((0, 128),), -0.2, 0.2)), 0.02, 0.3)
    expert_weights = scatter_about(seeds[10], (EXPERTS, 3, MODEL_WIDTH, FF), MODEL_WIDTH ** -0.5, 0.15625, ((0, 32), (3, 4)))
    return {"hidden": hidden, "attn_gain": attn_gain, "query_weight": query_weight, "key_matrix": key_matrix, "value_matrix": value_matrix, "output_weight": output_weight, "prompt_start": prompt_start, "ffn_gain": ffn_gain, "routes": routes, "route_weights": route_weights, "expert_weights": expert_weights}


epsilon = 1e-05
block_rows = 512

def rms_norm(values, gain):
    mean_square = lax.optimization_barrier(jnp.mean(values * values, axis=-1, keepdims=True))
    return values * lax.rsqrt(mean_square + epsilon) * gain

def rotary_embedding(heads_in, stream_offsets):
    half = heads_in.shape[-1] // 2
    freqs = 10000.0 ** (-jnp.arange(half, dtype=jnp.float32) / half)
    angle = stream_offsets.astype(jnp.float32)[:, None] * freqs[None, :]
    cosine = jnp.cos(angle)[:, None, :]
    sine = jnp.sin(angle)[:, None, :]
    first_half = heads_in[..., :half]
    second_half = heads_in[..., half:]
    return jnp.concatenate([first_half * cosine - second_half * sine, second_half * cosine + first_half * sine], axis=-1)

def reference(hidden, attn_gain, query_weight, key_matrix, value_matrix, output_weight, prompt_start, ffn_gain, routes, route_weights, expert_weights):
    heads_per_group = QUERY_HEADS // KEY_VALUE_HEADS
    inputs = hidden.astype(jnp.float32)
    positions = jnp.arange(ALL_POSITIONS, dtype=jnp.int32) % STREAM
    stream_offsets = positions - prompt_start
    normalized_input = rms_norm(inputs, attn_gain).astype(jnp.bfloat16)
    query_rows_all = jnp.dot(normalized_input, query_weight, preferred_element_type=jnp.float32).reshape(ALL_POSITIONS, QUERY_HEADS, HEAD_SIZE)
    query_rows_all = rotary_embedding(query_rows_all, stream_offsets).astype(jnp.bfloat16).reshape(ALL_POSITIONS, KEY_VALUE_HEADS, heads_per_group, HEAD_SIZE)
    gathered_keys = jnp.dot(normalized_input, key_matrix, preferred_element_type=jnp.float32).reshape(ALL_POSITIONS, KEY_VALUE_HEADS, HEAD_SIZE)
    gathered_keys = rotary_embedding(gathered_keys, stream_offsets).astype(jnp.bfloat16)
    gathered_values = jnp.dot(normalized_input, value_matrix, preferred_element_type=jnp.float32).astype(jnp.bfloat16)
    rotated_key_cache = gathered_keys.reshape(ALL_POSITIONS, KEY_VALUE_HEADS * HEAD_SIZE)
    value_cache = gathered_values
    value_per_head = gathered_values.reshape(ALL_POSITIONS, KEY_VALUE_HEADS, HEAD_SIZE)
    query_block = math.gcd(STREAM, 512)
    per_stream = STREAM // query_block
    block_count = ALL_POSITIONS // query_block

    def attend_block(block_index):
        group_index = block_index // per_stream
        query_rows = lax.dynamic_slice_in_dim(query_rows_all, block_index * query_block, query_block, 0).astype(jnp.float32)
        key_rows = lax.dynamic_slice_in_dim(gathered_keys, group_index * STREAM, STREAM, 0).astype(jnp.float32)
        value_rows = lax.dynamic_slice_in_dim(value_per_head, group_index * STREAM, STREAM, 0).astype(jnp.float32)
        query_pos = block_index % per_stream * query_block + jnp.arange(query_block, dtype=jnp.int32)
        starts = lax.dynamic_slice_in_dim(prompt_start, block_index * query_block, query_block, 0)
        key_pos = jnp.arange(STREAM, dtype=jnp.int32)
        scores = jnp.einsum('qgrd,kgd->qgrk', query_rows, key_rows) * HEAD_SIZE ** (-0.5)
        valid = (key_pos[None, :] >= starts[:, None]) & (key_pos[None, :] <= query_pos[:, None])
        valid = valid[:, None, None, :]
        masked = jnp.where(valid, scores, jnp.float32(-1e+30))
        row_max = lax.optimization_barrier(jnp.max(masked, axis=-1, keepdims=True))
        probs = jnp.where(valid, jnp.exp(masked - row_max), jnp.float32(0.0))
        totals = lax.optimization_barrier(jnp.sum(probs, axis=-1))
        attention_mixed = jnp.einsum('qgrk,kgd->qgrd', probs.astype(jnp.bfloat16).astype(jnp.float32), value_rows)
        attention_mixed = attention_mixed / totals[..., None]
        return attention_mixed.reshape(query_block, QUERY_HEADS * HEAD_SIZE).astype(jnp.bfloat16)
    attention = lax.map(attend_block, jnp.arange(block_count, dtype=jnp.int32)).reshape(ALL_POSITIONS, QUERY_HEADS * HEAD_SIZE)
    residual = inputs + jnp.dot(attention, output_weight, preferred_element_type=jnp.float32)
    moe_in = rms_norm(residual, ffn_gain).astype(jnp.bfloat16)
    flat_routes = routes.reshape(-1).astype(jnp.int32)
    pair_count = flat_routes.shape[0]
    order = jnp.argsort(flat_routes, stable=True).astype(jnp.int32)
    counts = lax.optimization_barrier(jnp.sum((flat_routes[:, None] == jnp.arange(EXPERTS, dtype=jnp.int32)[None, :]).astype(jnp.int32), axis=0))
    padded = (counts + block_rows - 1) // block_rows * block_rows
    offsets_pad = jnp.cumsum(padded) - padded
    starts_sorted = jnp.cumsum(counts) - counts
    sorted_experts = flat_routes[order]
    rank = jnp.arange(pair_count, dtype=jnp.int32) - starts_sorted[sorted_experts]
    dest_sorted = (offsets_pad[sorted_experts] + rank).astype(jnp.int32)
    group_blocks = -(-pair_count // block_rows) + EXPERTS
    slot_total = group_blocks * block_rows
    token_of = jnp.zeros((slot_total,), jnp.int32).at[dest_sorted].set(order // TOP)
    valid_slot = jnp.zeros((slot_total,), jnp.bfloat16).at[dest_sorted].set(jnp.bfloat16(1.0))
    ends = offsets_pad + padded
    block_start = jnp.arange(group_blocks, dtype=jnp.int32) * block_rows
    block_expert = lax.optimization_barrier(jnp.sum((ends[None, :] <= block_start[:, None]).astype(jnp.int32), axis=1))
    block_expert = jnp.minimum(block_expert, EXPERTS - 1)

    def expert_block(block_index):
        token_rows = lax.dynamic_slice_in_dim(token_of, block_index * block_rows, block_rows, 0)
        live = lax.dynamic_slice_in_dim(valid_slot, block_index * block_rows, block_rows, 0)
        rows_in = moe_in[token_rows] * live[:, None]
        weights = expert_weights[block_expert[block_index]]
        gate_out = jnp.dot(rows_in, weights[0], preferred_element_type=jnp.float32)
        up_out = jnp.dot(rows_in, weights[1], preferred_element_type=jnp.float32)
        hidden_units = (jax.nn.silu(gate_out) * up_out).astype(jnp.bfloat16)
        result = lax.dot_general(hidden_units, weights[2], (((1,), (1,)), ((), ())), preferred_element_type=jnp.float32)
        return result.astype(jnp.bfloat16)
    expert_rows = lax.map(expert_block, jnp.arange(group_blocks, dtype=jnp.int32)).reshape(slot_total, MODEL_WIDTH)
    dest_pair = jnp.zeros((pair_count,), jnp.int32).at[order].set(dest_sorted).reshape(ALL_POSITIONS, TOP)
    moe_sum = jnp.zeros((ALL_POSITIONS, MODEL_WIDTH), jnp.float32)
    for column in range(TOP):
        moe_sum = moe_sum + route_weights[:, column:column + 1] * expert_rows[dest_pair[:, column]].astype(jnp.float32)
    layer_out = (residual + moe_sum).astype(jnp.bfloat16)
    return (layer_out, rotated_key_cache, value_cache)
```

```python
import jax
import jax.numpy as jnp
from jax import lax
from jax.experimental import pallas as pl
from jax.experimental.pallas import tpu as pltpu
from jax.sharding import PartitionSpec as P

QUERY_HEADS = 24
KEY_VALUE_HEADS = 8
HEAD_SIZE = 64
TOP = 8
SIDE = 4
CHIPS = SIDE * SIDE
EXPERTS = 32
SLOTS = 64
FF = 512


epsilon = 1e-05


def rms_norm(values, gain):
    mean_square = jnp.mean(values * values, axis=-1, keepdims=True)
    return values * lax.rsqrt(mean_square + epsilon) * gain


def rotary_embedding(heads_in, stream_offsets):
    half = heads_in.shape[-1] // 2
    freqs = 10000.0 ** (-jnp.arange(half, dtype=jnp.float32) / half)
    angle = stream_offsets.astype(jnp.float32)[:, None] * freqs[None, :]
    cosine = jnp.cos(angle)[:, None, :]
    sine = jnp.sin(angle)[:, None, :]
    first_half = heads_in[..., :half]
    second_half = heads_in[..., half:]
    return jnp.concatenate(
        [first_half * cosine - second_half * sine, second_half * cosine + first_half * sine],
        axis=-1,
    )


class Plane:
    def __init__(self):
        me = lax.axis_index("exp")
        self.core = lax.rem(me, 2)
        chip = lax.div(me, 2)
        self.y = lax.div(chip, SIDE)
        self.x = lax.rem(chip, SIDE)

    def chip(self, dy, dx):
        return lax.rem(self.y + dy + SIDE, SIDE) * SIDE + lax.rem(self.x + dx + SIDE, SIDE)

    def device(self, dy, dx):
        return {"exp": self.chip(dy, dx) * 2 + self.core}

    def partner(self):
        return {"exp": self.chip(0, 0) * 2 + 1 - self.core}


def greet(plane, with_partner=False):
    barrier = pltpu.get_barrier_semaphore()
    for dy, dx in ((0, 1), (0, -1), (1, 0), (-1, 0)):
        pl.semaphore_signal(
            barrier, inc=1, device_id=plane.device(dy, dx), device_id_type=pl.DeviceIdType.MESH
        )
    if with_partner:
        pl.semaphore_signal(
            barrier, inc=1, device_id=plane.partner(), device_id_type=pl.DeviceIdType.MESH
        )
    pl.semaphore_wait(barrier, 5 if with_partner else 4)


def turn(h, a, b):
    return (b, a) if h == 0 else (a, b)


class Gather:
    COPIES = 20

    def __init__(self, plane, own, slots, send, recv, rows, slot_of):
        self.plane, self.own, self.slots = plane, own, slots
        self.send, self.recv, self.rows, self.slot_of = send, recv, rows, slot_of

    def span(self, h, part):
        half = self.rows // 2
        if part is None:
            return pl.ds(h * half, half)
        return pl.ds(h * half + part * (half // 2), half // 2)

    def step(self, k):
        if k < 4:
            return (
                ((0, 0), None, (1, 0)),
                ((0, 0), None, (-1, 0)),
                ((-1, 0), 0, (1, 0)),
                ((1, 0), 1, (-1, 0)),
            )[k]
        a = (0, -1, 1, 2)[(k - 4) // 4]
        return (
            ((a, 0), None, (0, 1)),
            ((a, 0), None, (0, -1)),
            ((a, -1), 0, (0, 1)),
            ((a, 1), 1, (0, -1)),
        )[(k - 4) % 4]

    def make(self, h, k, incoming):
        (a, b), part, (da, db) = self.step(k)
        span = self.span(h, part)
        if incoming:
            a, b = a - da, b - db
        slot = self.slot_of(self.plane.chip(*turn(h, a, b)))
        there = self.slots.at[slot, span]
        here = self.own.at[span] if (a, b) == (0, 0) else there
        return pltpu.make_async_remote_copy(
            src_ref=here,
            dst_ref=there,
            send_sem=self.send.at[h * self.COPIES + k],
            recv_sem=self.recv.at[h * self.COPIES + k],
            device_id=self.plane.device(*turn(h, da, db)),
            device_id_type=pl.DeviceIdType.MESH,
        )

    def start(self, *ks):
        for k in ks:
            for h in (0, 1):
                self.make(h, k, False).start()

    def arrive(self, k, *then):
        for h in (0, 1):
            self.make(h, k, True).wait_recv()
            for t in then:
                self.make(h, t, False).start()

    def run(self):
        self.start(0, 1)
        self.start(4, 5)
        self.arrive(0, 2, 8, 9)
        self.arrive(1, 3, 12, 13)
        self.arrive(4, 6)
        self.arrive(5, 7)
        self.arrive(2)
        self.arrive(3, 16, 17)
        for base in (8, 12, 16):
            self.arrive(base, base + 2)
            self.arrive(base + 1, base + 3)
        for base in (4, 8, 12, 16):
            self.arrive(base + 2)
            self.arrive(base + 3)

    def finish(self):
        for h in (0, 1):
            for k in range(self.COPIES):
                self.make(h, k, False).wait_send()


def gather_rows(block, collective_id):
    rows, width = block.shape

    def kernel(own, slots, send, recv, mine_sem):
        plane = Plane()
        greet(plane)
        gather = Gather(plane, own, slots, send, recv, rows, lambda chip: chip)
        mine = pltpu.make_async_copy(own, slots.at[plane.chip(0, 0)], mine_sem)
        mine.start()
        gather.run()
        gather.finish()
        mine.wait()

    return pl.pallas_call(
        kernel,
        out_shape=jax.ShapeDtypeStruct((CHIPS, rows, width), block.dtype),
        in_specs=[pl.BlockSpec(memory_space=pltpu.VMEM)],
        out_specs=pl.BlockSpec(memory_space=pl.ANY),
        scratch_shapes=[
            pltpu.SemaphoreType.DMA((2 * Gather.COPIES,)),
            pltpu.SemaphoreType.DMA((2 * Gather.COPIES,)),
            pltpu.SemaphoreType.DMA,
        ],
        compiler_params=pltpu.CompilerParams(collective_id=collective_id, has_side_effects=True),
        name="gather_rows",
    )(block)


class Scatter:
    COPIES = 20

    def __init__(self, plane, parts, hold, send, recv, rows):
        self.plane, self.parts, self.hold = plane, parts, hold
        self.send, self.recv, self.rows = send, recv, rows

    def span(self, h, part):
        half = self.rows // 2
        if part is None:
            return pl.ds(h * half, half)
        return pl.ds(h * half + part * (half // 2), half // 2)

    def step(self, k):
        if k < 16:
            q = (2, 1, 3, 0)[k // 4]
            return (
                ((2, q), 0, (1, 0)),
                ((2, q), 1, (-1, 0)),
                ((1, q), None, (1, 0)),
                ((3, q), None, (-1, 0)),
            )[k % 4]
        return (
            ((0, 2), 0, (0, 1)),
            ((0, 2), 1, (0, -1)),
            ((0, 1), None, (0, 1)),
            ((0, 3), None, (0, -1)),
        )[k % 4]

    def make(self, h, k):
        (a, b), part, (da, db) = self.step(k)
        span = self.span(h, part)
        size = self.rows // 2 if part is None else self.rows // 4
        return pltpu.make_async_remote_copy(
            src_ref=self.parts.at[self.plane.chip(*turn(h, a, b)), span],
            dst_ref=self.hold.at[h, k, pl.ds(0, size)],
            send_sem=self.send.at[h * self.COPIES + k],
            recv_sem=self.recv.at[h * self.COPIES + k],
            device_id=self.plane.device(*turn(h, da, db)),
            device_id_type=pl.DeviceIdType.MESH,
        )

    def start(self, k):
        for h in (0, 1):
            self.make(h, k).start()

    def add(self, h, k, place, part):
        size = self.rows // 4
        at = (self.plane.chip(*turn(h, *place)), self.span(h, part))
        self.parts[at] = (
            self.parts[at].astype(jnp.float32)
            + self.hold[h, k, pl.ds(0, size)].astype(jnp.float32)
        ).astype(jnp.bfloat16)

    def relay(self, base, near, far):
        for h in (0, 1):
            self.make(h, base).wait_recv()
            self.add(h, base, near, 0)
            self.make(h, base + 2).start()
        for h in (0, 1):
            self.make(h, base + 1).wait_recv()
            self.add(h, base + 1, far, 1)
            self.make(h, base + 3).start()

    def total(self, h, base, place):
        self.make(h, base + 2).wait_recv()
        self.make(h, base + 3).wait_recv()
        at = (self.plane.chip(*turn(h, *place)), self.span(h, None))
        return (
            self.parts[at].astype(jnp.float32)
            + self.hold[h, base + 2].astype(jnp.float32)
            + self.hold[h, base + 3].astype(jnp.float32)
        )

    def run(self, out):
        for i in range(4):
            self.start(4 * i)
            self.start(4 * i + 1)
        for i, q in enumerate((2, 1, 3, 0)):
            self.relay(4 * i, (1, q), (3, q))
        for i, q in enumerate((2, 1, 3, 0)):
            for h in (0, 1):
                at = (self.plane.chip(*turn(h, 0, q)), self.span(h, None))
                self.parts[at] = self.total(h, 4 * i, (0, q)).astype(jnp.bfloat16)
            if i == 0:
                self.start(16)
                self.start(17)
            if i == 2:
                self.relay(16, (0, 1), (0, 3))
        for h in (0, 1):
            out[self.span(h, None)] = self.total(h, 16, (0, 0))

    def finish(self):
        for h in (0, 1):
            for k in range(self.COPIES):
                self.make(h, k).wait_send()


def scatter_sums(parts, collective_id):
    _, rows, width = parts.shape

    def kernel(given, out, held, hold, send, recv, in_sem):
        load = pltpu.make_async_copy(given, held, in_sem)
        load.start()
        plane = Plane()
        greet(plane)
        load.wait()
        scatter = Scatter(plane, held, hold, send, recv, rows)
        scatter.run(out)
        scatter.finish()

    return pl.pallas_call(
        kernel,
        out_shape=jax.ShapeDtypeStruct((rows, width), jnp.float32),
        in_specs=[pl.BlockSpec(memory_space=pl.ANY)],
        out_specs=pl.BlockSpec(memory_space=pltpu.VMEM),
        scratch_shapes=[
            pltpu.VMEM((CHIPS, rows, width), jnp.bfloat16),
            pltpu.VMEM((2, Scatter.COPIES, rows // 2, width), jnp.bfloat16),
            pltpu.SemaphoreType.DMA((2 * Scatter.COPIES,)),
            pltpu.SemaphoreType.DMA((2 * Scatter.COPIES,)),
            pltpu.SemaphoreType.DMA,
        ],
        compiler_params=pltpu.CompilerParams(
            collective_id=collective_id, has_side_effects=True, vmem_limit_bytes=60 << 20
        ),
        name="scatter_sums",
    )(parts)


BLOCKS = 4


def expert_kernel(ranks, gains, rows_in, own, other, out, weights, picked, made, sems):
    step = pl.program_id(0)

    def loads():
        for e, source in enumerate((own, other)):
            for r in range(4):
                yield pltpu.make_async_copy(
                    source.at[r],
                    weights.at[e, :, :, pl.ds(r * 128, 128)],
                    sems.at[e * 4 + r],
                )

    @pl.when(step == 0)
    def _():
        for load in loads():
            load.start()

    tokens = rows_in.shape[1]
    slot = lax.broadcasted_iota(jnp.int32, (SLOTS, tokens), 0).astype(jnp.float32)

    def hits(j):
        return jnp.concatenate([ranks[j, e : e + 1, :] == slot for e in (0, 1)], axis=0)

    for j in range(BLOCKS):
        choose = jnp.where(hits(j), 1.0, 0.0).astype(jnp.bfloat16)
        picked[j] = jnp.dot(choose, rows_in[j], preferred_element_type=jnp.float32).astype(
            jnp.bfloat16
        )

    @pl.when(step == 0)
    def _():
        for load in loads():
            load.wait()

    width = rows_in.shape[2]
    for e in (0, 1):
        rows = picked[:, e * SLOTS : (e + 1) * SLOTS, :].reshape(BLOCKS * SLOTS, width)
        gate = jnp.dot(rows, weights[e, 0], preferred_element_type=jnp.float32)
        up = jnp.dot(rows, weights[e, 1], preferred_element_type=jnp.float32)
        units = (gate / (1.0 + jnp.exp(-gate)) * up).astype(jnp.bfloat16)
        result = lax.dot_general(
            units, weights[e, 2], (((1,), (1,)), ((), ())), preferred_element_type=jnp.float32
        )
        for j in range(BLOCKS):
            gain = jnp.sum(
                jnp.where(ranks[j, e : e + 1, :] == slot, gains[j, e : e + 1, :], 0.0),
                axis=1,
                keepdims=True,
            )
            made[j, e * SLOTS : (e + 1) * SLOTS, :] = (
                result[j * SLOTS : (j + 1) * SLOTS, :] * gain
            ).astype(jnp.bfloat16)

    for j in range(BLOCKS):
        choose = jnp.where(hits(j), 1.0, 0.0).astype(jnp.bfloat16)
        out[j] = lax.dot_general(
            choose, made[j], (((0,), (0,)), ((), ())), preferred_element_type=jnp.float32
        ).astype(jnp.bfloat16)


def run_experts(ranks, gains, rows_in, own, other):
    chips, tokens, width = rows_in.shape
    return pl.pallas_call(
        expert_kernel,
        grid=(chips // BLOCKS,),
        out_shape=jax.ShapeDtypeStruct(rows_in.shape, jnp.bfloat16),
        in_specs=[
            pl.BlockSpec((BLOCKS, 2, tokens), lambda i: (i, 0, 0)),
            pl.BlockSpec((BLOCKS, 2, tokens), lambda i: (i, 0, 0)),
            pl.BlockSpec((BLOCKS, tokens, width), lambda i: (i, 0, 0)),
            pl.BlockSpec(memory_space=pl.ANY),
            pl.BlockSpec(memory_space=pl.ANY),
        ],
        out_specs=pl.BlockSpec((BLOCKS, tokens, width), lambda i: (i, 0, 0)),
        scratch_shapes=[
            pltpu.VMEM((2, 3, width, FF), jnp.bfloat16),
            pltpu.VMEM((BLOCKS, 2 * SLOTS, width), jnp.bfloat16),
            pltpu.VMEM((BLOCKS, 2 * SLOTS, width), jnp.bfloat16),
            pltpu.SemaphoreType.DMA((8,)),
        ],
        compiler_params=pltpu.CompilerParams(vmem_limit_bytes=60 << 20),
        name="experts",
    )(ranks, gains, rows_in, own, other)


def slot_tables(routes, route_weights):
    tokens = routes.shape[0]
    hit = routes[None] == jnp.arange(EXPERTS, dtype=jnp.int32)[:, None, None]
    gains = jnp.sum(jnp.where(hit, route_weights[None], 0.0), axis=2)
    named = jnp.any(hit, axis=2)
    earlier = jnp.triu(jnp.ones((tokens, tokens), jnp.bfloat16), 1)
    ranks = jnp.dot(named.astype(jnp.bfloat16), earlier, preferred_element_type=jnp.float32)
    return jnp.where(named, ranks, -1.0), gains


def shards(
    hidden,
    attn_gain,
    query_weight,
    key_matrix,
    value_matrix,
    output_weight,
    prompt_start,
    ffn_gain,
    routes,
    route_weights,
    expert_weights,
):
    total_row_count = hidden.shape[0]
    lane_index = lax.axis_index("exp")
    heads_per_group = QUERY_HEADS // KEY_VALUE_HEADS

    tables = jnp.stack(slot_tables(routes, route_weights))
    tables = lax.all_gather(tables, "exp", axis=0)
    weight_piece = lax.all_gather(expert_weights[0], "req", axis=0)
    weight_other = lax.ppermute(weight_piece, "exp", [(i, i ^ 1) for i in range(EXPERTS)])
    tables = lax.dynamic_index_in_dim(
        tables.reshape(CHIPS, 2, 2, CHIPS, 2, total_row_count),
        lax.rem(lane_index, 2),
        1,
        keepdims=False,
    )
    tables = lax.dynamic_index_in_dim(tables, lax.div(lane_index, 2), 2, keepdims=False)
    tables = jnp.where(lax.rem(lane_index, 2) == 0, tables, tables[:, :, ::-1])

    positions = lane_index * total_row_count + jnp.arange(total_row_count, dtype=jnp.int32)
    stream_offsets = positions - prompt_start
    inputs = hidden.astype(jnp.float32)
    normalized_input = rms_norm(inputs, attn_gain).astype(jnp.bfloat16)
    query_rows_all = jnp.dot(
        normalized_input, query_weight, preferred_element_type=jnp.float32
    ).reshape(total_row_count, QUERY_HEADS, HEAD_SIZE)
    query_rows_all = (
        rotary_embedding(query_rows_all, stream_offsets)
        .astype(jnp.bfloat16)
        .reshape(total_row_count, KEY_VALUE_HEADS, heads_per_group, HEAD_SIZE)
    )
    shard_keys = jnp.dot(normalized_input, key_matrix, preferred_element_type=jnp.float32).reshape(
        total_row_count, KEY_VALUE_HEADS, HEAD_SIZE
    )
    shard_keys = (
        rotary_embedding(shard_keys, stream_offsets)
        .astype(jnp.bfloat16)
        .reshape(total_row_count, KEY_VALUE_HEADS * HEAD_SIZE)
    )
    values_local = jnp.dot(
        normalized_input, value_matrix, preferred_element_type=jnp.float32
    ).astype(jnp.bfloat16)
    stacked = jnp.stack([shard_keys, values_local])
    key_value_slice = lax.all_gather(stacked, "exp", axis=1, tiled=True)
    feature_width = key_value_slice.shape[1]
    key_tile = key_value_slice[0].reshape(feature_width, KEY_VALUE_HEADS, HEAD_SIZE)
    value_tile = key_value_slice[1].reshape(feature_width, KEY_VALUE_HEADS, HEAD_SIZE)
    key_pos = jnp.arange(feature_width, dtype=jnp.int32)
    scores = jnp.einsum(
        "tgrd,sgd->tgrs", query_rows_all, key_tile, preferred_element_type=jnp.float32
    ) * HEAD_SIZE ** (-0.5)
    valid = (key_pos[None, :] >= prompt_start[:, None]) & (key_pos[None, :] <= positions[:, None])
    valid = valid[:, None, None, :]
    masked = jnp.where(valid, scores, jnp.float32(-1e30))
    new_max = jnp.max(masked, axis=-1)
    probs = jnp.where(valid, jnp.exp(masked - new_max[..., None]), jnp.float32(0.0))
    totals = jnp.sum(probs, axis=-1)
    attention_mixed = jnp.einsum(
        "tgrs,sgd->tgrd", probs.astype(jnp.bfloat16), value_tile, preferred_element_type=jnp.float32
    )
    attention = (
        (attention_mixed / totals[..., None])
        .reshape(total_row_count, QUERY_HEADS * HEAD_SIZE)
        .astype(jnp.bfloat16)
    )
    residual = inputs + jnp.dot(attention, output_weight, preferred_element_type=jnp.float32)
    moe_in = rms_norm(residual, ffn_gain).astype(jnp.bfloat16)

    rows_in = gather_rows(moe_in, 1)
    parts = run_experts(tables[:, 0], tables[:, 1], rows_in, weight_piece, weight_other)
    moe_sum = scatter_sums(parts, 2)
    layer_out = (residual + moe_sum).astype(jnp.bfloat16)
    return (layer_out, stacked[0], stacked[1])


def solution(mesh):
    in_specs = (
        P(("req", "exp"), None),
        P(),
        P(),
        P(),
        P(),
        P(),
        P(("req", "exp")),
        P(),
        P(("req", "exp"), None),
        P(("req", "exp"), None),
        P("exp", None, None, "req"),
    )
    out_specs = (P(("req", "exp"), None), P(("req", "exp"), None), P(("req", "exp"), None))
    return jax.shard_map(shards, mesh=mesh, in_specs=in_specs, out_specs=out_specs, check_vma=False)
```

```python
import jax
import jax.numpy as jnp
from jax import lax
from jax.experimental import pallas as pl
from jax.experimental.pallas import tpu as pltpu
from jax.sharding import PartitionSpec as P

QUERY_HEADS = 24
KEY_VALUE_HEADS = 8
HEAD_SIZE = 64
TOP = 8
SIDE = 4
CHIPS = SIDE * SIDE
EXPERTS = 32
SLOTS = 64
FF = 512


epsilon = 1e-05


def rms_norm(values, gain):
    mean_square = jnp.mean(values * values, axis=-1, keepdims=True)
    return values * lax.rsqrt(mean_square + epsilon) * gain


def rotary_embedding(heads_in, stream_offsets):
    half = heads_in.shape[-1] // 2
    freqs = 10000.0 ** (-jnp.arange(half, dtype=jnp.float32) / half)
    angle = stream_offsets.astype(jnp.float32)[:, None] * freqs[None, :]
    cosine = jnp.cos(angle)[:, None, :]
    sine = jnp.sin(angle)[:, None, :]
    first_half = heads_in[..., :half]
    second_half = heads_in[..., half:]
    return jnp.concatenate(
        [first_half * cosine - second_half * sine, second_half * cosine + first_half * sine],
        axis=-1,
    )


class Plane:
    def __init__(self):
        me = lax.axis_index("exp")
        self.core = lax.rem(me, 2)
        chip = lax.div(me, 2)
        self.y = lax.div(chip, SIDE)
        self.x = lax.rem(chip, SIDE)

    def chip(self, dy, dx):
        return lax.rem(self.y + dy + SIDE, SIDE) * SIDE + lax.rem(self.x + dx + SIDE, SIDE)

    def device(self, dy, dx):
        return {"exp": self.chip(dy, dx) * 2 + self.core}

    def partner(self):
        return {"exp": self.chip(0, 0) * 2 + 1 - self.core}


NEXT = ((0, 1), (0, -1), (1, 0), (-1, 0))
OTHERS = tuple((dy, dx) for dy in range(SIDE) for dx in range(SIDE) if dy or dx)


def greet(plane, places=NEXT, with_partner=False):
    barrier = pltpu.get_barrier_semaphore()
    for dy, dx in places:
        pl.semaphore_signal(
            barrier, inc=1, device_id=plane.device(dy, dx), device_id_type=pl.DeviceIdType.MESH
        )
    if with_partner:
        pl.semaphore_signal(
            barrier, inc=1, device_id=plane.partner(), device_id_type=pl.DeviceIdType.MESH
        )
    pl.semaphore_wait(barrier, len(places) + int(with_partner))


def turn(h, a, b):
    return (b, a) if h == 0 else (a, b)


class Gather:
    COPIES = 20

    def __init__(self, plane, own, slots, send, recv, rows, slot_of, ready=None):
        self.plane, self.own, self.slots = plane, own, slots
        self.send, self.recv, self.rows, self.slot_of = send, recv, rows, slot_of
        self.ready = ready or (lambda h, a, b: None)

    def span(self, h, part):
        half = self.rows // 2
        if part is None:
            return pl.ds(h * half, half)
        return pl.ds(h * half + part * (half // 2), half // 2)

    def step(self, k):
        if k < 4:
            return (
                ((0, 0), None, (1, 0)),
                ((0, 0), None, (-1, 0)),
                ((-1, 0), 0, (1, 0)),
                ((1, 0), 1, (-1, 0)),
            )[k]
        a = (0, -1, 1, 2)[(k - 4) // 4]
        return (
            ((a, 0), None, (0, 1)),
            ((a, 0), None, (0, -1)),
            ((a, -1), 0, (0, 1)),
            ((a, 1), 1, (0, -1)),
        )[(k - 4) % 4]

    def make(self, h, k, incoming):
        (a, b), part, (da, db) = self.step(k)
        span = self.span(h, part)
        if incoming:
            a, b = a - da, b - db
        slot = self.slot_of(self.plane.chip(*turn(h, a, b)))
        there = self.slots.at[slot, span]
        here = self.own.at[span] if (a, b) == (0, 0) else there
        return pltpu.make_async_remote_copy(
            src_ref=here,
            dst_ref=there,
            send_sem=self.send.at[h * self.COPIES + k],
            recv_sem=self.recv.at[h * self.COPIES + k],
            device_id=self.plane.device(*turn(h, da, db)),
            device_id_type=pl.DeviceIdType.MESH,
        )

    def start(self, *ks):
        for k in ks:
            for h in (0, 1):
                self.make(h, k, False).start()

    def arrive(self, k, *then):
        for h in (0, 1):
            self.make(h, k, True).wait_recv()
            for t in then:
                self.make(h, t, False).start()
            (a, b), part, (da, db) = self.step(k)
            if part != 0:
                self.ready(h, a - da, b - db)

    def run(self):
        self.start(0, 1)
        self.start(4, 5)
        self.ready(0, 0, 0)
        self.ready(1, 0, 0)
        self.arrive(0, 2, 8, 9)
        self.arrive(1, 3, 12, 13)
        self.arrive(4, 6)
        self.arrive(5, 7)
        self.arrive(2)
        self.arrive(3, 16, 17)
        for base in (8, 12, 16):
            self.arrive(base, base + 2)
            self.arrive(base + 1, base + 3)
        for base in (4, 8, 12, 16):
            self.arrive(base + 2)
            self.arrive(base + 3)

    def finish(self):
        for h in (0, 1):
            for k in range(self.COPIES):
                self.make(h, k, False).wait_send()


def gather_rows(block, collective_id):
    rows, width = block.shape

    def kernel(own, slots, send, recv, mine_sem):
        plane = Plane()
        greet(plane)
        gather = Gather(plane, own, slots, send, recv, rows, lambda chip: chip)
        mine = pltpu.make_async_copy(own, slots.at[plane.chip(0, 0)], mine_sem)
        mine.start()
        gather.run()
        gather.finish()
        mine.wait()

    return pl.pallas_call(
        kernel,
        out_shape=jax.ShapeDtypeStruct((CHIPS, rows, width), block.dtype),
        in_specs=[pl.BlockSpec(memory_space=pltpu.VMEM)],
        out_specs=pl.BlockSpec(memory_space=pl.ANY),
        scratch_shapes=[
            pltpu.SemaphoreType.DMA((2 * Gather.COPIES,)),
            pltpu.SemaphoreType.DMA((2 * Gather.COPIES,)),
            pltpu.SemaphoreType.DMA,
        ],
        compiler_params=pltpu.CompilerParams(collective_id=collective_id, has_side_effects=True),
        name="gather_rows",
    )(block)


def gather_keys_values(block, tables, collective_id):
    rows, width = block.shape

    def kernel(own, given, slots, held, send, recv, give, take, lend, borrow, sems):
        plane = Plane()
        greet(plane, OTHERS, True)
        here = plane.chip(0, 0)

        def share(h, a, b, incoming=False):
            place = turn(h, a, b)
            half = pl.ds(h * (rows // 2), rows // 2)
            core = 1 - plane.core if incoming else plane.core
            there = slots.at[plane.chip(*place) * 2 + core, half]
            at = h * CHIPS + (a % SIDE) * SIDE + b % SIDE
            return pltpu.make_async_remote_copy(
                src_ref=own.at[half] if (a, b) == (0, 0) and not incoming else there,
                dst_ref=there,
                send_sem=lend.at[at],
                recv_sem=borrow.at[at],
                device_id=plane.partner(),
                device_id_type=pl.DeviceIdType.MESH,
            )

        def table(n, incoming):
            dy, dx = OTHERS[n]
            return pltpu.make_async_remote_copy(
                src_ref=given.at[plane.chip(dy, dx)],
                dst_ref=held.at[plane.chip(-dy, -dx) if incoming else here],
                send_sem=give.at[n],
                recv_sem=take.at[n],
                device_id=plane.device(dy, dx),
                device_id_type=pl.DeviceIdType.MESH,
            )

        gather = Gather(
            plane,
            own,
            slots,
            send,
            recv,
            rows,
            lambda chip: chip * 2 + plane.core,
            lambda h, a, b: share(h, a, b).start(),
        )
        mine = pltpu.make_async_copy(own, slots.at[here * 2 + plane.core], sems.at[0])
        mine.start()
        row = pltpu.make_async_copy(given.at[here], held.at[here], sems.at[1])
        row.start()
        gather.run()
        for n in range(len(OTHERS)):
            table(n, False).start()
        gather.finish()
        mine.wait()
        row.wait()
        for n in range(len(OTHERS)):
            table(n, True).wait_recv()
            table(n, False).wait_send()
        for h in (0, 1):
            for a in range(SIDE):
                for b in range(SIDE):
                    share(h, a, b, True).wait_recv()
                    share(h, a, b).wait_send()

    return pl.pallas_call(
        kernel,
        out_shape=(
            jax.ShapeDtypeStruct((2 * CHIPS, rows, width), block.dtype),
            jax.ShapeDtypeStruct(tables.shape, tables.dtype),
        ),
        in_specs=[pl.BlockSpec(memory_space=pltpu.VMEM)] * 2,
        out_specs=(pl.BlockSpec(memory_space=pl.ANY), pl.BlockSpec(memory_space=pltpu.VMEM)),
        scratch_shapes=[
            pltpu.SemaphoreType.DMA((2 * Gather.COPIES,)),
            pltpu.SemaphoreType.DMA((2 * Gather.COPIES,)),
            pltpu.SemaphoreType.DMA((len(OTHERS),)),
            pltpu.SemaphoreType.DMA((len(OTHERS),)),
            pltpu.SemaphoreType.DMA((2 * CHIPS,)),
            pltpu.SemaphoreType.DMA((2 * CHIPS,)),
            pltpu.SemaphoreType.DMA((2,)),
        ],
        compiler_params=pltpu.CompilerParams(collective_id=collective_id, has_side_effects=True),
        name="gather_keys_values",
    )(block, tables)


KEYS = 512
PAIR = 6
LOW = -1e30
SCALE = HEAD_SIZE**-0.5 * 1.4426950408889634


def attention_kernel(bounds, queries, keys, values, starts, out, packed, peak, total):
    rows = queries.shape[0]
    lane = lax.broadcasted_iota(jnp.int32, (rows, 128), 1)
    low_half = lane < HEAD_SIZE
    for n in range(PAIR):
        tile = queries[:, (n // 2) * 128 : (n // 2 + 1) * 128].astype(jnp.float32)
        group = n // 3
        if n % 2 != group:
            tile = pltpu.roll(tile, HEAD_SIZE, axis=1)
        keep = low_half if group == 0 else jnp.logical_not(low_half)
        packed[n * rows : (n + 1) * rows, :] = jnp.where(keep, tile, 0.0).astype(jnp.bfloat16)
    peak[...] = jnp.full_like(peak, LOW)
    total[...] = jnp.zeros_like(total)
    first, last, inner, base = bounds[0], bounds[1], bounds[2], bounds[3]
    half = PAIR // 2 * rows

    def block(at, masked):
        at = pl.multiple_of(at * KEYS, KEYS)
        key = keys[pl.ds(at, KEYS), :]
        value = values[pl.ds(at, KEYS), :]
        key_lane = lax.broadcasted_iota(jnp.int32, (KEYS, 128), 1)
        if masked:
            key_pos = at + lax.broadcasted_iota(jnp.int32, (rows, KEYS), 1)
            own_pos = base + lax.broadcasted_iota(jnp.int32, (rows, KEYS), 0)
            valid = (key_pos >= starts[...]) & (key_pos <= own_pos)
        for group in (0, 1):
            span = pl.ds(group * half, half)
            scores = lax.dot_general(
                packed[span, :], key, (((1,), (1,)), ((), ())), preferred_element_type=jnp.float32
            )
            if masked:
                scores = jnp.where(
                    valid[None], scores.reshape(PAIR // 2, rows, KEYS), LOW
                ).reshape(half, KEYS)
            before = peak[span, :]
            now = jnp.maximum(before, jnp.max(scores, axis=1, keepdims=True))
            peak[span, :] = now
            fade = jnp.exp2((before - now) * SCALE)
            probs = jnp.exp2((scores - now[:, :1]) * SCALE).astype(jnp.bfloat16)
            own_half = (key_lane < HEAD_SIZE) == (group == 0)
            beside = jnp.where(own_half, value, jnp.ones_like(value))
            total[span, :] = total[span, :] * fade + jnp.dot(
                probs, beside, preferred_element_type=jnp.float32
            )

    def visit(at, carry):
        edge = (at == last) | (at * KEYS < inner)

        @pl.when(edge)
        def _():
            block(at, True)

        @pl.when(jnp.logical_not(edge))
        def _():
            block(at, False)

        return carry

    lax.fori_loop(first, last + 1, visit, 0)

    def head(n):
        sums = total[n * rows : (n + 1) * rows, :]
        result = sums / pltpu.roll(sums, HEAD_SIZE, axis=1)
        if n % 2 != n // 3:
            result = pltpu.roll(result, HEAD_SIZE, axis=1)
        return result

    for i in range(PAIR // 2):
        out[:, i * 128 : (i + 1) * 128] = jnp.where(low_half, head(2 * i), head(2 * i + 1)).astype(
            out.dtype
        )


def attend(queries, keys_values, prompt_start, base):
    rows, width = queries.shape
    span = PAIR * HEAD_SIZE
    pairs = width // span
    keys_values = keys_values.reshape(-1, keys_values.shape[-1])
    length = keys_values.shape[0]
    bounds = jnp.stack([prompt_start[0] // KEYS, base // KEYS, prompt_start[rows - 1], base])
    return pl.pallas_call(
        attention_kernel,
        out_shape=jax.ShapeDtypeStruct((rows, width), jnp.bfloat16),
        grid_spec=pltpu.PrefetchScalarGridSpec(
            num_scalar_prefetch=1,
            grid=(pairs,),
            in_specs=[
                pl.BlockSpec((rows, span), lambda p, _: (0, p)),
                pl.BlockSpec((length, 128), lambda p, _: (0, p)),
                pl.BlockSpec((length, 128), lambda p, _: (0, p + pairs)),
                pl.BlockSpec((rows, 1), lambda p, _: (0, 0)),
            ],
            out_specs=pl.BlockSpec((rows, span), lambda p, _: (0, p)),
            scratch_shapes=[
                pltpu.VMEM((PAIR * rows, 128), jnp.bfloat16),
                pltpu.VMEM((PAIR * rows, 128), jnp.float32),
                pltpu.VMEM((PAIR * rows, 128), jnp.float32),
            ],
        ),
        compiler_params=pltpu.CompilerParams(vmem_limit_bytes=60 << 20),
        name="attention",
    )(bounds.astype(jnp.int32), queries, keys_values, keys_values, prompt_start[:, None])


class Scatter:
    COPIES = 20

    def __init__(self, plane, parts, hold, send, recv, rows):
        self.plane, self.parts, self.hold = plane, parts, hold
        self.send, self.recv, self.rows = send, recv, rows

    def span(self, h, part):
        half = self.rows // 2
        if part is None:
            return pl.ds(h * half, half)
        return pl.ds(h * half + part * (half // 2), half // 2)

    def step(self, k):
        if k < 16:
            q = (2, 1, 3, 0)[k // 4]
            return (
                ((2, q), 0, (1, 0)),
                ((2, q), 1, (-1, 0)),
                ((1, q), None, (1, 0)),
                ((3, q), None, (-1, 0)),
            )[k % 4]
        return (
            ((0, 2), 0, (0, 1)),
            ((0, 2), 1, (0, -1)),
            ((0, 1), None, (0, 1)),
            ((0, 3), None, (0, -1)),
        )[k % 4]

    def make(self, h, k):
        (a, b), part, (da, db) = self.step(k)
        span = self.span(h, part)
        size = self.rows // 2 if part is None else self.rows // 4
        return pltpu.make_async_remote_copy(
            src_ref=self.parts.at[self.plane.chip(*turn(h, a, b)), span],
            dst_ref=self.hold.at[h, k, pl.ds(0, size)],
            send_sem=self.send.at[h * self.COPIES + k],
            recv_sem=self.recv.at[h * self.COPIES + k],
            device_id=self.plane.device(*turn(h, da, db)),
            device_id_type=pl.DeviceIdType.MESH,
        )

    def start(self, k):
        for h in (0, 1):
            self.make(h, k).start()

    def add(self, h, k, place, part):
        size = self.rows // 4
        at = (self.plane.chip(*turn(h, *place)), self.span(h, part))
        self.parts[at] = (
            self.parts[at].astype(jnp.float32)
            + self.hold[h, k, pl.ds(0, size)].astype(jnp.float32)
        ).astype(jnp.bfloat16)

    def relay(self, base, near, far):
        for h in (0, 1):
            self.make(h, base).wait_recv()
            self.add(h, base, near, 0)
            self.make(h, base + 2).start()
        for h in (0, 1):
            self.make(h, base + 1).wait_recv()
            self.add(h, base + 1, far, 1)
            self.make(h, base + 3).start()

    def total(self, h, base, place):
        self.make(h, base + 2).wait_recv()
        self.make(h, base + 3).wait_recv()
        at = (self.plane.chip(*turn(h, *place)), self.span(h, None))
        return (
            self.parts[at].astype(jnp.float32)
            + self.hold[h, base + 2].astype(jnp.float32)
            + self.hold[h, base + 3].astype(jnp.float32)
        )

    def run(self, out):
        for i in range(4):
            self.start(4 * i)
            self.start(4 * i + 1)
        for i, q in enumerate((2, 1, 3, 0)):
            self.relay(4 * i, (1, q), (3, q))
        for i, q in enumerate((2, 1, 3, 0)):
            for h in (0, 1):
                at = (self.plane.chip(*turn(h, 0, q)), self.span(h, None))
                self.parts[at] = self.total(h, 4 * i, (0, q)).astype(jnp.bfloat16)
            if i == 0:
                self.start(16)
                self.start(17)
            if i == 2:
                self.relay(16, (0, 1), (0, 3))
        for h in (0, 1):
            out[self.span(h, None)] = self.total(h, 16, (0, 0))

    def finish(self):
        for h in (0, 1):
            for k in range(self.COPIES):
                self.make(h, k).wait_send()


def scatter_sums(parts, collective_id):
    _, rows, width = parts.shape

    def kernel(given, out, held, hold, send, recv, in_sem):
        load = pltpu.make_async_copy(given, held, in_sem)
        load.start()
        plane = Plane()
        greet(plane)
        load.wait()
        scatter = Scatter(plane, held, hold, send, recv, rows)
        scatter.run(out)
        scatter.finish()

    return pl.pallas_call(
        kernel,
        out_shape=jax.ShapeDtypeStruct((rows, width), jnp.float32),
        in_specs=[pl.BlockSpec(memory_space=pl.ANY)],
        out_specs=pl.BlockSpec(memory_space=pltpu.VMEM),
        scratch_shapes=[
            pltpu.VMEM((CHIPS, rows, width), jnp.bfloat16),
            pltpu.VMEM((2, Scatter.COPIES, rows // 2, width), jnp.bfloat16),
            pltpu.SemaphoreType.DMA((2 * Scatter.COPIES,)),
            pltpu.SemaphoreType.DMA((2 * Scatter.COPIES,)),
            pltpu.SemaphoreType.DMA,
        ],
        compiler_params=pltpu.CompilerParams(
            collective_id=collective_id, has_side_effects=True, vmem_limit_bytes=60 << 20
        ),
        name="scatter_sums",
    )(parts)


BLOCKS = 4


def expert_kernel(tables, rows_in, own, other, out, weights, picked, made, sems):
    step = pl.program_id(0)
    core = lax.rem(lax.axis_index("exp"), 2)

    def loads():
        for e, source in enumerate((own, other)):
            for r in range(4):
                yield pltpu.make_async_copy(
                    source.at[r],
                    weights.at[core if e == 0 else 1 - core, :, :, pl.ds(r * 128, 128)],
                    sems.at[e * 4 + r],
                )

    @pl.when(step == 0)
    def _():
        for load in loads():
            load.start()

    tokens = rows_in.shape[1]
    slot = lax.broadcasted_iota(jnp.int32, (SLOTS, tokens), 0).astype(jnp.float32)

    def hits(j):
        return jnp.concatenate([tables[j, 2 + e : 3 + e, :] == slot for e in (0, 1)], axis=0)

    for j in range(BLOCKS):
        choose = jnp.where(hits(j), 1.0, 0.0).astype(jnp.bfloat16)
        picked[j] = jnp.dot(choose, rows_in[j], preferred_element_type=jnp.float32).astype(
            jnp.bfloat16
        )

    @pl.when(step == 0)
    def _():
        for load in loads():
            load.wait()

    width = rows_in.shape[2]
    for e in (0, 1):
        rows = picked[:, e * SLOTS : (e + 1) * SLOTS, :].reshape(BLOCKS * SLOTS, width)
        gate = jnp.dot(rows, weights[e, 0], preferred_element_type=jnp.float32)
        up = jnp.dot(rows, weights[e, 1], preferred_element_type=jnp.float32)
        units = (gate / (1.0 + jnp.exp(-gate)) * up).astype(jnp.bfloat16)
        result = lax.dot_general(
            units, weights[e, 2], (((1,), (1,)), ((), ())), preferred_element_type=jnp.float32
        )
        for j in range(BLOCKS):
            gain = jnp.sum(
                jnp.where(tables[j, 2 + e : 3 + e, :] == slot, tables[j, e : e + 1, :], 0.0),
                axis=1,
                keepdims=True,
            )
            made[j, e * SLOTS : (e + 1) * SLOTS, :] = (
                result[j * SLOTS : (j + 1) * SLOTS, :] * gain
            ).astype(jnp.bfloat16)

    for j in range(BLOCKS):
        choose = jnp.where(hits(j), 1.0, 0.0).astype(jnp.bfloat16)
        out[j] = lax.dot_general(
            choose, made[j], (((0,), (0,)), ((), ())), preferred_element_type=jnp.float32
        ).astype(jnp.bfloat16)


def run_experts(tables, rows_in, own, other):
    chips, tokens, width = rows_in.shape
    return pl.pallas_call(
        expert_kernel,
        grid=(chips // BLOCKS,),
        out_shape=jax.ShapeDtypeStruct(rows_in.shape, jnp.bfloat16),
        in_specs=[
            pl.BlockSpec((BLOCKS, 8, tokens), lambda i: (i, 0, 0)),
            pl.BlockSpec((BLOCKS, tokens, width), lambda i: (i, 0, 0)),
            pl.BlockSpec(memory_space=pl.ANY),
            pl.BlockSpec(memory_space=pl.ANY),
        ],
        out_specs=pl.BlockSpec((BLOCKS, tokens, width), lambda i: (i, 0, 0)),
        scratch_shapes=[
            pltpu.VMEM((2, 3, width, FF), jnp.bfloat16),
            pltpu.VMEM((BLOCKS, 2 * SLOTS, width), jnp.bfloat16),
            pltpu.VMEM((BLOCKS, 2 * SLOTS, width), jnp.bfloat16),
            pltpu.SemaphoreType.DMA((8,)),
        ],
        compiler_params=pltpu.CompilerParams(vmem_limit_bytes=60 << 20),
        name="experts",
    )(tables, rows_in, own, other)


def slot_tables(routes, route_weights):
    tokens = routes.shape[0]
    hit = routes[None] == jnp.arange(EXPERTS, dtype=jnp.int32)[:, None, None]
    gains = jnp.sum(jnp.where(hit, route_weights[None], 0.0), axis=2)
    named = jnp.any(hit, axis=2)
    earlier = jnp.triu(jnp.ones((tokens, tokens), jnp.bfloat16), 1)
    ranks = jnp.dot(named.astype(jnp.bfloat16), earlier, preferred_element_type=jnp.float32)
    ranks = jnp.where(named, ranks, -1.0)
    pairs = [t.reshape(CHIPS, 2, tokens) for t in (gains, ranks)]
    return jnp.concatenate(pairs + [jnp.zeros((CHIPS, 4, tokens), jnp.float32)], axis=1)


def shards(
    hidden,
    attn_gain,
    query_weight,
    key_matrix,
    value_matrix,
    output_weight,
    prompt_start,
    ffn_gain,
    routes,
    route_weights,
    expert_weights,
):
    total_row_count = hidden.shape[0]
    lane_index = lax.axis_index("exp")
    weight_piece = lax.all_gather(expert_weights[0], "req", axis=0)
    weight_other = lax.ppermute(weight_piece, "exp", [(i, i ^ 1) for i in range(EXPERTS)])
    positions = lane_index * total_row_count + jnp.arange(total_row_count, dtype=jnp.int32)
    stream_offsets = positions - prompt_start
    inputs = hidden.astype(jnp.float32)
    normalized_input = rms_norm(inputs, attn_gain).astype(jnp.bfloat16)
    query_rows_all = jnp.dot(
        normalized_input, query_weight, preferred_element_type=jnp.float32
    ).reshape(total_row_count, QUERY_HEADS, HEAD_SIZE)
    query_rows_all = (
        rotary_embedding(query_rows_all, stream_offsets)
        .astype(jnp.bfloat16)
        .reshape(total_row_count, QUERY_HEADS * HEAD_SIZE)
    )
    shard_keys = jnp.dot(normalized_input, key_matrix, preferred_element_type=jnp.float32).reshape(
        total_row_count, KEY_VALUE_HEADS, HEAD_SIZE
    )
    shard_keys = (
        rotary_embedding(shard_keys, stream_offsets)
        .astype(jnp.bfloat16)
        .reshape(total_row_count, KEY_VALUE_HEADS * HEAD_SIZE)
    )
    values_local = jnp.dot(
        normalized_input, value_matrix, preferred_element_type=jnp.float32
    ).astype(jnp.bfloat16)
    keys_values, tables = gather_keys_values(
        jnp.concatenate([shard_keys, values_local], axis=1), slot_tables(routes, route_weights), 0
    )
    attention = attend(
        query_rows_all, keys_values, prompt_start, lane_index * total_row_count
    )
    residual = inputs + jnp.dot(attention, output_weight, preferred_element_type=jnp.float32)
    moe_in = rms_norm(residual, ffn_gain).astype(jnp.bfloat16)

    rows_in = gather_rows(moe_in, 1)
    parts = run_experts(tables, rows_in, weight_piece, weight_other)
    moe_sum = scatter_sums(parts, 2)
    layer_out = (residual + moe_sum).astype(jnp.bfloat16)
    return (layer_out, shard_keys, values_local)


def solution(mesh):
    in_specs = (
        P(("req", "exp"), None),
        P(),
        P(),
        P(),
        P(),
        P(),
        P(("req", "exp")),
        P(),
        P(("req", "exp"), None),
        P(("req", "exp"), None),
        P("exp", None, None, "req"),
    )
    out_specs = (P(("req", "exp"), None), P(("req", "exp"), None), P(("req", "exp"), None))
    return jax.shard_map(shards, mesh=mesh, in_specs=in_specs, out_specs=out_specs, check_vma=False)
```

```python
import jax
import jax.numpy as jnp
from jax import lax
from jax.experimental import pallas as pl
from jax.experimental.pallas import tpu as pltpu
from jax.sharding import PartitionSpec as P

QUERY_HEADS = 24
KEY_VALUE_HEADS = 8
HEAD_SIZE = 64
TOP = 8
SIDE = 4
CHIPS = SIDE * SIDE
EXPERTS = 32
SLOTS = 64
FF = 512


epsilon = 1e-05


def rms_norm(values, gain):
    mean_square = jnp.mean(values * values, axis=-1, keepdims=True)
    return values * lax.rsqrt(mean_square + epsilon) * gain


def rotary_embedding(heads_in, stream_offsets):
    half = heads_in.shape[-1] // 2
    freqs = 10000.0 ** (-jnp.arange(half, dtype=jnp.float32) / half)
    angle = stream_offsets.astype(jnp.float32)[:, None] * freqs[None, :]
    cosine = jnp.cos(angle)[:, None, :]
    sine = jnp.sin(angle)[:, None, :]
    first_half = heads_in[..., :half]
    second_half = heads_in[..., half:]
    return jnp.concatenate(
        [first_half * cosine - second_half * sine, second_half * cosine + first_half * sine],
        axis=-1,
    )


class Plane:
    def __init__(self):
        me = lax.axis_index("exp")
        self.core = lax.rem(me, 2)
        chip = lax.div(me, 2)
        self.y = lax.div(chip, SIDE)
        self.x = lax.rem(chip, SIDE)

    def chip(self, dy, dx):
        return lax.rem(self.y + dy + SIDE, SIDE) * SIDE + lax.rem(self.x + dx + SIDE, SIDE)

    def device(self, dy, dx):
        return {"exp": self.chip(dy, dx) * 2 + self.core}

    def partner(self):
        return {"exp": self.chip(0, 0) * 2 + 1 - self.core}

    def mirror(self, same_core):
        core = self.core if same_core else 1 - self.core
        return {"exp": (CHIPS - 1 - self.chip(0, 0)) * 2 + core}


NEXT = ((0, 1), (0, -1), (1, 0), (-1, 0))
OTHERS = tuple((dy, dx) for dy in range(SIDE) for dx in range(SIDE) if dy or dx)


def greet(plane, places=NEXT, devices=()):
    barrier = pltpu.get_barrier_semaphore()
    for device in [plane.device(dy, dx) for dy, dx in places] + list(devices):
        pl.semaphore_signal(
            barrier, inc=1, device_id=device, device_id_type=pl.DeviceIdType.MESH
        )
    pl.semaphore_wait(barrier, len(places) + len(devices))


def remote(src, dst, send, recv, device):
    return pltpu.make_async_remote_copy(
        src_ref=src,
        dst_ref=dst,
        send_sem=send,
        recv_sem=recv,
        device_id=device,
        device_id_type=pl.DeviceIdType.MESH,
    )


def turn(h, a, b):
    return (b, a) if h == 0 else (a, b)


class Gather:
    COPIES = 20

    def __init__(self, plane, own, slots, send, recv, rows, slot_of):
        self.plane, self.own, self.slots = plane, own, slots
        self.send, self.recv, self.rows, self.slot_of = send, recv, rows, slot_of

    def span(self, h, part):
        half = self.rows // 2
        if part is None:
            return pl.ds(h * half, half)
        return pl.ds(h * half + part * (half // 2), half // 2)

    def step(self, k):
        if k < 4:
            return (
                ((0, 0), None, (1, 0)),
                ((0, 0), None, (-1, 0)),
                ((-1, 0), 0, (1, 0)),
                ((1, 0), 1, (-1, 0)),
            )[k]
        a = (0, -1, 1, 2)[(k - 4) // 4]
        return (
            ((a, 0), None, (0, 1)),
            ((a, 0), None, (0, -1)),
            ((a, -1), 0, (0, 1)),
            ((a, 1), 1, (0, -1)),
        )[(k - 4) % 4]

    def make(self, h, k, incoming):
        (a, b), part, (da, db) = self.step(k)
        span = self.span(h, part)
        if incoming:
            a, b = a - da, b - db
        slot = self.slot_of(self.plane.chip(*turn(h, a, b)))
        there = self.slots.at[slot, span]
        here = self.own.at[span] if (a, b) == (0, 0) else there
        return pltpu.make_async_remote_copy(
            src_ref=here,
            dst_ref=there,
            send_sem=self.send.at[h * self.COPIES + k],
            recv_sem=self.recv.at[h * self.COPIES + k],
            device_id=self.plane.device(*turn(h, da, db)),
            device_id_type=pl.DeviceIdType.MESH,
        )

    def start(self, *ks):
        for k in ks:
            for h in (0, 1):
                self.make(h, k, False).start()

    def arrive(self, k, *then):
        for h in (0, 1):
            self.make(h, k, True).wait_recv()
            for t in then:
                self.make(h, t, False).start()

    def run(self):
        self.start(0, 1)
        self.start(4, 5)
        self.arrive(0, 2, 8, 9)
        self.arrive(1, 3, 12, 13)
        self.arrive(4, 6)
        self.arrive(5, 7)
        self.arrive(2)
        self.arrive(3, 16, 17)
        for base in (8, 12, 16):
            self.arrive(base, base + 2)
            self.arrive(base + 1, base + 3)
        for base in (4, 8, 12, 16):
            self.arrive(base + 2)
            self.arrive(base + 3)

    def finish(self):
        for h in (0, 1):
            for k in range(self.COPIES):
                self.make(h, k, False).wait_send()


def gather_rows(block, weights, collective_id):
    rows, width = block.shape

    def kernel(own, given, slots, other, send, recv, sems):
        plane = Plane()
        greet(plane, NEXT, [plane.partner()])
        swap = remote(given, other, sems.at[1], sems.at[2], plane.partner())
        gather = Gather(plane, own, slots, send, recv, rows, lambda chip: chip)
        mine = pltpu.make_async_copy(own, slots.at[plane.chip(0, 0)], sems.at[0])
        mine.start()
        swap.start()
        gather.run()
        gather.finish()
        mine.wait()
        swap.wait()

    return pl.pallas_call(
        kernel,
        out_shape=(
            jax.ShapeDtypeStruct((CHIPS, rows, width), block.dtype),
            jax.ShapeDtypeStruct(weights.shape, weights.dtype),
        ),
        in_specs=[
            pl.BlockSpec(memory_space=pltpu.VMEM),
            pl.BlockSpec(memory_space=pl.ANY),
        ],
        out_specs=(pl.BlockSpec(memory_space=pl.ANY), pl.BlockSpec(memory_space=pl.ANY)),
        scratch_shapes=[
            pltpu.SemaphoreType.DMA((2 * Gather.COPIES,)),
            pltpu.SemaphoreType.DMA((2 * Gather.COPIES,)),
            pltpu.SemaphoreType.DMA((3,)),
        ],
        compiler_params=pltpu.CompilerParams(collective_id=collective_id, has_side_effects=True),
        name="gather_rows",
    )(block, weights)


KEYS = 512
PAIR = 6
PAIR_WIDTH = PAIR * HEAD_SIZE
LOW = -1e30
SCALE = HEAD_SIZE**-0.5 * 1.4426950408889634
ACROSS = (0, -1, 1, 2)


def attention_kernel(
    queries, pairs, starts, given,
    out, held,
    near, store, asked, begin, packed, peak, total, bias, done,
    give, take, x_send, x_recv, y_send, y_recv, q_send, q_recv, o_send, o_recv, sems,
):
    plane = Plane()
    core, odd = plane.core, lax.rem(plane.x, 2)
    here = plane.chip(0, 0)
    rows = queries.shape[0]
    friends = [plane.partner(), plane.mirror(True), plane.mirror(False)]
    greet(plane, OTHERS, [friends[0], friends[2]])

    mine = 2 * core + odd
    theirs = [2 * (1 - core) + odd, 2 * core + 1 - odd, 2 * (1 - core) + 1 - odd]
    slots = [core, 2 + core, 2 + core]
    from_slots = [1 - core, 2 + core, 2 + 1 - core]

    def lanes(at, size):
        return pl.ds(pl.multiple_of(at * size, size), size)

    swap = remote(
        pairs.at[:, lanes(1 - core, 512)], near, sems.at[0], sems.at[1], friends[0]
    )

    def source(h, parity):
        if h == 0:
            return pairs.at[:, lanes(2 * core + parity, 256)]
        return near.at[:, lanes(parity, 256)]

    def slot(h, dy, dx, part=None):
        low = (core if h == 0 else 1 - core) * rows
        size = rows
        if part is not None:
            size = rows // 2
            low = low + part * size
        return store.at[plane.chip(dy, dx), pl.ds(pl.multiple_of(low, size), size)]

    def keep(h):
        return pltpu.make_async_copy(source(h, odd), slot(h, 0, 0), sems.at[2 + h])

    def across(h, n, incoming=False):
        dx = (1, -1, 2)[n]
        return remote(
            source(h, odd if n == 2 else 1 - odd),
            slot(h, 0, -dx if incoming else 0),
            x_send.at[3 * h + n],
            x_recv.at[3 * h + n],
            plane.device(0, dx),
        )

    def along(h, i, n, incoming=False):
        dx = ACROSS[i]
        at, part, dy = ((0, None, 1), (0, None, -1), (-1, 0, 1), (1, 1, -1))[n]
        place = slot(h, at - dy if incoming else at, dx, part)
        src = source(h, odd) if (i == 0 and n < 2) else place
        if i == 0 and n < 2 and not incoming:
            place = slot(h, 0, 0)
        k = (h * 4 + i) * 4 + n
        return remote(src, place, y_send.at[k], y_recv.at[k], plane.device(dy, 0))

    def ask(n, incoming=False):
        at = from_slots[n] if incoming else slots[n]
        return remote(
            queries.at[:, lanes(theirs[n], PAIR_WIDTH)],
            asked.at[at],
            q_send.at[n],
            q_recv.at[n],
            friends[n],
        )

    def tell(n, incoming=False):
        at = from_slots[n] if incoming else slots[n]
        return remote(starts, begin.at[at], q_send.at[3 + n], q_recv.at[3 + n], friends[n])

    def table(n, incoming=False):
        dy, dx = OTHERS[n]
        return remote(
            given.at[plane.chip(dy, dx)],
            held.at[plane.chip(-dy, -dx) if incoming else here],
            give.at[n],
            take.at[n],
            plane.device(dy, dx),
        )

    own_asked = pltpu.make_async_copy(
        queries.at[:, lanes(mine, PAIR_WIDTH)], asked.at[core], sems.at[4]
    )
    own_begin = pltpu.make_async_copy(starts, begin.at[core], sems.at[5])
    own_table = pltpu.make_async_copy(given.at[here], held.at[here], sems.at[6])

    swap.start()
    for h in (0, 1):
        if h == 1:
            ask(0).start()
            tell(0).start()
            own_asked.start()
            own_begin.start()
            own_table.start()
            swap.wait_recv()
        keep(h).start()
        for n in range(3):
            across(h, n).start()
        along(h, 0, 0).start()
        along(h, 0, 1).start()
    for n in (1, 2):
        ask(n).start()
        tell(n).start()
    for n in range(3):
        i = (1, 2, 3)[n]
        for h in (0, 1):
            across(h, n, True).wait_recv()
            along(h, i, 0).start()
            along(h, i, 1).start()
    for n in range(len(OTHERS)):
        table(n).start()

    own_asked.wait()
    own_begin.wait()
    for n in range(3):
        ask(n, True).wait_recv()
        tell(n, True).wait_recv()
    for h in (0, 1):
        keep(h).wait()

    lane = lax.broadcasted_iota(jnp.int32, (rows, 128), 1)
    low_half = lane < HEAD_SIZE
    for which in (0, 1):
        for side in (0, 1):
            for n in range(PAIR):
                tile = asked[2 * which + side, :, (n // 2) * 128 : (n // 2 + 1) * 128].astype(
                    jnp.float32
                )
                group = n // 3
                if n % 2 != group:
                    tile = pltpu.roll(tile, HEAD_SIZE, axis=1)
                own_half = low_half if group == 0 else jnp.logical_not(low_half)
                at = (n * 2 + side) * rows
                packed[which, at : at + rows, :] = jnp.where(own_half, tile, 0.0).astype(
                    jnp.bfloat16
                )
    peak[...] = jnp.full_like(peak, LOW)
    total[...] = jnp.zeros_like(total)
    half = PAIR * rows

    def visit(which, chip):
        stream_chip = jnp.where(which == 0, here, CHIPS - 1 - here)
        at = chip * (2 * rows)
        for side in (0, 1):
            first = jnp.broadcast_to(begin[2 * which + side, 0:1, :], (rows, rows)).T
            first = jnp.concatenate([first] * (KEYS // rows), axis=1).astype(jnp.int32)
            key_pos = at + lax.broadcasted_iota(jnp.int32, (rows, KEYS), 1)
            own_pos = (2 * stream_chip + side) * rows + lax.broadcasted_iota(
                jnp.int32, (rows, KEYS), 0
            )
            bias[side * rows : (side + 1) * rows, :] = jnp.where(
                (key_pos >= first) & (key_pos <= own_pos), 0.0, LOW
            )
        tile = store[pl.ds(chip, 2)].reshape(KEYS, 256)
        key, value = tile[:, :128], tile[:, 128:]
        key_lane = lax.broadcasted_iota(jnp.int32, (KEYS, 128), 1)
        for group in (0, 1):
            span = pl.ds(group * half, half)
            scores = lax.dot_general(
                packed[which, span, :],
                key,
                (((1,), (1,)), ((), ())),
                preferred_element_type=jnp.float32,
            )
            scores = (scores.reshape(PAIR // 2, 2 * rows, KEYS) + bias[...][None]).reshape(
                half, KEYS
            )
            before = peak[which, span, :]
            now = jnp.maximum(before, jnp.max(scores, axis=1, keepdims=True))
            peak[which, span, :] = now
            fade = jnp.exp2((before - now) * SCALE)
            wide = jnp.concatenate([now] * (KEYS // 128), axis=1)
            probs = jnp.exp2((scores - wide) * SCALE).astype(jnp.bfloat16)
            own_half = (key_lane < HEAD_SIZE) == (group == 0)
            beside = jnp.where(own_half, value, jnp.ones_like(value))
            total[which, span, :] = total[which, span, :] * fade + jnp.dot(
                probs, beside, preferred_element_type=jnp.float32
            )

    def phase(step, carry):
        @pl.when(step == 1)
        def _():
            for i in range(4):
                for n in (0, 1):
                    for h in (0, 1):
                        along(h, i, n, True).wait_recv()
                        along(h, i, n + 2).start()

        @pl.when(step == 3)
        def _():
            for i in range(4):
                for n in (2, 3):
                    for h in (0, 1):
                        along(h, i, n, True).wait_recv()

        dy = jnp.where(step == 0, 0, jnp.where(step == 1, SIDE - 1, step - 1))
        dy = jnp.where(step == 3, 2, dy)
        row = lax.rem(plane.y + dy, SIDE) * SIDE

        def one(t, carry):
            which = lax.div(t, 2)
            chip = row + 2 * lax.rem(t, 2)
            limit = jnp.where(which == 0, here, CHIPS - 1 - here)

            @pl.when(chip <= limit)
            def _():
                visit(which, chip)

            return carry

        return lax.fori_loop(0, 4, one, carry)

    lax.fori_loop(0, 4, phase, 0)

    def answer(which, side):
        def head(n):
            at = (n * 2 + side) * rows
            sums = total[which, at : at + rows, :]
            result = sums / pltpu.roll(sums, HEAD_SIZE, axis=1)
            if n % 2 != n // 3:
                result = pltpu.roll(result, HEAD_SIZE, axis=1)
            return result

        return [
            jnp.where(low_half, head(2 * i), head(2 * i + 1)).astype(out.dtype)
            for i in range(PAIR // 2)
        ]

    for which in (1, 0):
        for side in (0, 1):
            for i, piece in enumerate(answer(which, side)):
                done[2 * which + side, :, i * 128 : (i + 1) * 128] = piece

    def reply(n, incoming=False):
        return remote(
            done.at[from_slots[n]],
            out.at[:, lanes(theirs[n] if incoming else mine, PAIR_WIDTH)],
            o_send.at[n],
            o_recv.at[n],
            friends[n],
        )

    for n in (1, 2, 0):
        reply(n).start()
    own_reply = pltpu.make_async_copy(
        done.at[core], out.at[:, lanes(mine, PAIR_WIDTH)], sems.at[7]
    )
    own_reply.start()

    swap.wait_send()
    own_table.wait()
    for h in (0, 1):
        for n in range(3):
            across(h, n).wait_send()
        for i in range(4):
            for n in range(4):
                along(h, i, n).wait_send()
    for n in range(3):
        ask(n).wait_send()
        tell(n).wait_send()
    for n in range(len(OTHERS)):
        table(n, True).wait_recv()
        table(n).wait_send()
    own_reply.wait()
    for n in range(3):
        reply(n, True).wait_recv()
        reply(n).wait_send()


def attend(queries, pairs, starts, tables, collective_id):
    rows, width = queries.shape
    dma = pltpu.SemaphoreType.DMA
    return pl.pallas_call(
        attention_kernel,
        out_shape=(
            jax.ShapeDtypeStruct((rows, width), jnp.bfloat16),
            jax.ShapeDtypeStruct(tables.shape, tables.dtype),
        ),
        in_specs=[pl.BlockSpec(memory_space=pltpu.VMEM)] * 4,
        out_specs=(pl.BlockSpec(memory_space=pltpu.VMEM),) * 2,
        scratch_shapes=[
            pltpu.VMEM((rows, 512), jnp.bfloat16),
            pltpu.VMEM((CHIPS, 2 * rows, 256), jnp.bfloat16),
            pltpu.VMEM((4, rows, PAIR_WIDTH), jnp.bfloat16),
            pltpu.VMEM((4, 8, rows), jnp.float32),
            pltpu.VMEM((2, 2 * PAIR * rows, 128), jnp.bfloat16),
            pltpu.VMEM((2, 2 * PAIR * rows, 128), jnp.float32),
            pltpu.VMEM((2, 2 * PAIR * rows, 128), jnp.float32),
            pltpu.VMEM((2 * rows, KEYS), jnp.float32),
            pltpu.VMEM((4, rows, PAIR_WIDTH), jnp.bfloat16),
            dma((len(OTHERS),)),
            dma((len(OTHERS),)),
            dma((6,)),
            dma((6,)),
            dma((32,)),
            dma((32,)),
            dma((6,)),
            dma((6,)),
            dma((3,)),
            dma((3,)),
            dma((8,)),
        ],
        compiler_params=pltpu.CompilerParams(
            collective_id=collective_id, has_side_effects=True, vmem_limit_bytes=60 << 20
        ),
        name="attention",
    )(queries, pairs, starts, tables)


class Scatter:
    COPIES = 20

    def __init__(self, plane, parts, hold, send, recv, rows):
        self.plane, self.parts, self.hold = plane, parts, hold
        self.send, self.recv, self.rows = send, recv, rows

    def span(self, h, part):
        half = self.rows // 2
        if part is None:
            return pl.ds(h * half, half)
        return pl.ds(h * half + part * (half // 2), half // 2)

    def step(self, k):
        if k < 16:
            q = (2, 1, 3, 0)[k // 4]
            return (
                ((2, q), 0, (1, 0)),
                ((2, q), 1, (-1, 0)),
                ((1, q), None, (1, 0)),
                ((3, q), None, (-1, 0)),
            )[k % 4]
        return (
            ((0, 2), 0, (0, 1)),
            ((0, 2), 1, (0, -1)),
            ((0, 1), None, (0, 1)),
            ((0, 3), None, (0, -1)),
        )[k % 4]

    def make(self, h, k):
        (a, b), part, (da, db) = self.step(k)
        span = self.span(h, part)
        size = self.rows // 2 if part is None else self.rows // 4
        return pltpu.make_async_remote_copy(
            src_ref=self.parts.at[self.plane.chip(*turn(h, a, b)), span],
            dst_ref=self.hold.at[h, k, pl.ds(0, size)],
            send_sem=self.send.at[h * self.COPIES + k],
            recv_sem=self.recv.at[h * self.COPIES + k],
            device_id=self.plane.device(*turn(h, da, db)),
            device_id_type=pl.DeviceIdType.MESH,
        )

    def start(self, k):
        for h in (0, 1):
            self.make(h, k).start()

    def add(self, h, k, place, part):
        size = self.rows // 4
        at = (self.plane.chip(*turn(h, *place)), self.span(h, part))
        self.parts[at] = (
            self.parts[at].astype(jnp.float32)
            + self.hold[h, k, pl.ds(0, size)].astype(jnp.float32)
        ).astype(jnp.bfloat16)

    def relay(self, base, near, far):
        for h in (0, 1):
            self.make(h, base).wait_recv()
            self.add(h, base, near, 0)
            self.make(h, base + 2).start()
        for h in (0, 1):
            self.make(h, base + 1).wait_recv()
            self.add(h, base + 1, far, 1)
            self.make(h, base + 3).start()

    def total(self, h, base, place):
        self.make(h, base + 2).wait_recv()
        self.make(h, base + 3).wait_recv()
        at = (self.plane.chip(*turn(h, *place)), self.span(h, None))
        return (
            self.parts[at].astype(jnp.float32)
            + self.hold[h, base + 2].astype(jnp.float32)
            + self.hold[h, base + 3].astype(jnp.float32)
        )

    def run(self, out):
        for i in range(4):
            self.start(4 * i)
            self.start(4 * i + 1)
        for i, q in enumerate((2, 1, 3, 0)):
            self.relay(4 * i, (1, q), (3, q))
        for i, q in enumerate((2, 1, 3, 0)):
            for h in (0, 1):
                at = (self.plane.chip(*turn(h, 0, q)), self.span(h, None))
                self.parts[at] = self.total(h, 4 * i, (0, q)).astype(jnp.bfloat16)
            if i == 0:
                self.start(16)
                self.start(17)
            if i == 2:
                self.relay(16, (0, 1), (0, 3))
        for h in (0, 1):
            out[self.span(h, None)] = self.total(h, 16, (0, 0))

    def finish(self):
        for h in (0, 1):
            for k in range(self.COPIES):
                self.make(h, k).wait_send()


def scatter_sums(parts, collective_id):
    _, rows, width = parts.shape

    def kernel(given, out, held, hold, send, recv, in_sem):
        load = pltpu.make_async_copy(given, held, in_sem)
        load.start()
        plane = Plane()
        greet(plane)
        load.wait()
        scatter = Scatter(plane, held, hold, send, recv, rows)
        scatter.run(out)
        scatter.finish()

    return pl.pallas_call(
        kernel,
        out_shape=jax.ShapeDtypeStruct((rows, width), jnp.float32),
        in_specs=[pl.BlockSpec(memory_space=pl.ANY)],
        out_specs=pl.BlockSpec(memory_space=pltpu.VMEM),
        scratch_shapes=[
            pltpu.VMEM((CHIPS, rows, width), jnp.bfloat16),
            pltpu.VMEM((2, Scatter.COPIES, rows // 2, width), jnp.bfloat16),
            pltpu.SemaphoreType.DMA((2 * Scatter.COPIES,)),
            pltpu.SemaphoreType.DMA((2 * Scatter.COPIES,)),
            pltpu.SemaphoreType.DMA,
        ],
        compiler_params=pltpu.CompilerParams(
            collective_id=collective_id, has_side_effects=True, vmem_limit_bytes=60 << 20
        ),
        name="scatter_sums",
    )(parts)


BLOCKS = 4


def expert_kernel(tables, rows_in, own, other, out, weights, picked, made, sems):
    step = pl.program_id(0)
    core = lax.rem(lax.axis_index("exp"), 2)

    def loads():
        for e, source in enumerate((own, other)):
            for r in range(4):
                yield pltpu.make_async_copy(
                    source.at[r],
                    weights.at[core if e == 0 else 1 - core, :, :, pl.ds(r * 128, 128)],
                    sems.at[e * 4 + r],
                )

    @pl.when(step == 0)
    def _():
        for load in loads():
            load.start()

    tokens = rows_in.shape[1]
    slot = lax.broadcasted_iota(jnp.int32, (SLOTS, tokens), 0).astype(jnp.float32)

    def hits(j):
        return jnp.concatenate([tables[j, 2 + e : 3 + e, :] == slot for e in (0, 1)], axis=0)

    for j in range(BLOCKS):
        choose = jnp.where(hits(j), 1.0, 0.0).astype(jnp.bfloat16)
        picked[j] = jnp.dot(choose, rows_in[j], preferred_element_type=jnp.float32).astype(
            jnp.bfloat16
        )

    @pl.when(step == 0)
    def _():
        for load in loads():
            load.wait()

    width = rows_in.shape[2]
    for e in (0, 1):
        rows = picked[:, e * SLOTS : (e + 1) * SLOTS, :].reshape(BLOCKS * SLOTS, width)
        gate = jnp.dot(rows, weights[e, 0], preferred_element_type=jnp.float32)
        up = jnp.dot(rows, weights[e, 1], preferred_element_type=jnp.float32)
        units = (gate / (1.0 + jnp.exp(-gate)) * up).astype(jnp.bfloat16)
        result = lax.dot_general(
            units, weights[e, 2], (((1,), (1,)), ((), ())), preferred_element_type=jnp.float32
        )
        for j in range(BLOCKS):
            gain = jnp.sum(
                jnp.where(tables[j, 2 + e : 3 + e, :] == slot, tables[j, e : e + 1, :], 0.0),
                axis=1,
                keepdims=True,
            )
            made[j, e * SLOTS : (e + 1) * SLOTS, :] = (
                result[j * SLOTS : (j + 1) * SLOTS, :] * gain
            ).astype(jnp.bfloat16)

    for j in range(BLOCKS):
        choose = jnp.where(hits(j), 1.0, 0.0).astype(jnp.bfloat16)
        out[j] = lax.dot_general(
            choose, made[j], (((0,), (0,)), ((), ())), preferred_element_type=jnp.float32
        ).astype(jnp.bfloat16)


def run_experts(tables, rows_in, own, other):
    chips, tokens, width = rows_in.shape
    return pl.pallas_call(
        expert_kernel,
        grid=(chips // BLOCKS,),
        out_shape=jax.ShapeDtypeStruct(rows_in.shape, jnp.bfloat16),
        in_specs=[
            pl.BlockSpec((BLOCKS, 8, tokens), lambda i: (i, 0, 0)),
            pl.BlockSpec((BLOCKS, tokens, width), lambda i: (i, 0, 0)),
            pl.BlockSpec(memory_space=pl.ANY),
            pl.BlockSpec(memory_space=pl.ANY),
        ],
        out_specs=pl.BlockSpec((BLOCKS, tokens, width), lambda i: (i, 0, 0)),
        scratch_shapes=[
            pltpu.VMEM((2, 3, width, FF), jnp.bfloat16),
            pltpu.VMEM((BLOCKS, 2 * SLOTS, width), jnp.bfloat16),
            pltpu.VMEM((BLOCKS, 2 * SLOTS, width), jnp.bfloat16),
            pltpu.SemaphoreType.DMA((8,)),
        ],
        compiler_params=pltpu.CompilerParams(vmem_limit_bytes=60 << 20),
        name="experts",
    )(tables, rows_in, own, other)


def slot_tables(routes, route_weights):
    tokens = routes.shape[0]
    hit = routes[None] == jnp.arange(EXPERTS, dtype=jnp.int32)[:, None, None]
    gains = jnp.sum(jnp.where(hit, route_weights[None], 0.0), axis=2)
    named = jnp.any(hit, axis=2)
    earlier = jnp.triu(jnp.ones((tokens, tokens), jnp.bfloat16), 1)
    ranks = jnp.dot(named.astype(jnp.bfloat16), earlier, preferred_element_type=jnp.float32)
    ranks = jnp.where(named, ranks, -1.0)
    pairs = [t.reshape(CHIPS, 2, tokens) for t in (gains, ranks)]
    return jnp.concatenate(pairs + [jnp.zeros((CHIPS, 4, tokens), jnp.float32)], axis=1)


def shards(
    hidden,
    attn_gain,
    query_weight,
    key_matrix,
    value_matrix,
    output_weight,
    prompt_start,
    ffn_gain,
    routes,
    route_weights,
    expert_weights,
):
    total_row_count = hidden.shape[0]
    lane_index = lax.axis_index("exp")
    weight_piece = lax.all_gather(expert_weights[0], "req", axis=0)
    positions = lane_index * total_row_count + jnp.arange(total_row_count, dtype=jnp.int32)
    stream_offsets = positions - prompt_start
    inputs = hidden.astype(jnp.float32)
    normalized_input = rms_norm(inputs, attn_gain).astype(jnp.bfloat16)
    query_rows_all = jnp.dot(
        normalized_input, query_weight, preferred_element_type=jnp.float32
    ).reshape(total_row_count, QUERY_HEADS, HEAD_SIZE)
    query_rows_all = (
        rotary_embedding(query_rows_all, stream_offsets)
        .astype(jnp.bfloat16)
        .reshape(total_row_count, QUERY_HEADS * HEAD_SIZE)
    )
    shard_keys = jnp.dot(normalized_input, key_matrix, preferred_element_type=jnp.float32).reshape(
        total_row_count, KEY_VALUE_HEADS, HEAD_SIZE
    )
    shard_keys = (
        rotary_embedding(shard_keys, stream_offsets)
        .astype(jnp.bfloat16)
        .reshape(total_row_count, KEY_VALUE_HEADS * HEAD_SIZE)
    )
    values_local = jnp.dot(
        normalized_input, value_matrix, preferred_element_type=jnp.float32
    ).astype(jnp.bfloat16)
    pairs = jnp.concatenate(
        [
            side[:, p * 128 : (p + 1) * 128]
            for p in range(KEY_VALUE_HEADS // 2)
            for side in (shard_keys, values_local)
        ],
        axis=1,
    )
    starts = jnp.broadcast_to(prompt_start.astype(jnp.float32)[None], (8, total_row_count))
    attention, tables = attend(
        query_rows_all, pairs, starts, slot_tables(routes, route_weights), 0
    )
    residual = inputs + jnp.dot(attention, output_weight, preferred_element_type=jnp.float32)
    moe_in = rms_norm(residual, ffn_gain).astype(jnp.bfloat16)

    rows_in, weight_other = gather_rows(moe_in, weight_piece, 1)
    parts = run_experts(tables, rows_in, weight_piece, weight_other)
    moe_sum = scatter_sums(parts, 2)
    layer_out = (residual + moe_sum).astype(jnp.bfloat16)
    return (layer_out, shard_keys, values_local)


def solution(mesh):
    in_specs = (
        P(("req", "exp"), None),
        P(),
        P(),
        P(),
        P(),
        P(),
        P(("req", "exp")),
        P(),
        P(("req", "exp"), None),
        P(("req", "exp"), None),
        P("exp", None, None, "req"),
    )
    out_specs = (P(("req", "exp"), None), P(("req", "exp"), None), P(("req", "exp"), None))
    return jax.shard_map(shards, mesh=mesh, in_specs=in_specs, out_specs=out_specs, check_vma=False)
```

```python
import jax
import jax.numpy as jnp
from jax import lax
from jax.experimental import pallas as pl
from jax.experimental.pallas import tpu as pltpu
from jax.sharding import PartitionSpec as P

QUERY_HEADS = 24
KEY_VALUE_HEADS = 8
HEAD_SIZE = 64
TOP = 8
SIDE = 4
CHIPS = SIDE * SIDE
EXPERTS = 32
SLOTS = 64
FF = 512


epsilon = 1e-05


def rms_norm(values, gain):
    mean_square = jnp.mean(values * values, axis=-1, keepdims=True)
    return values * lax.rsqrt(mean_square + epsilon) * gain


def rotary_embedding(heads_in, stream_offsets):
    half = heads_in.shape[-1] // 2
    freqs = 10000.0 ** (-jnp.arange(half, dtype=jnp.float32) / half)
    angle = stream_offsets.astype(jnp.float32)[:, None] * freqs[None, :]
    cosine = jnp.cos(angle)[:, None, :]
    sine = jnp.sin(angle)[:, None, :]
    first_half = heads_in[..., :half]
    second_half = heads_in[..., half:]
    return jnp.concatenate(
        [first_half * cosine - second_half * sine, second_half * cosine + first_half * sine],
        axis=-1,
    )


class Plane:
    def __init__(self):
        me = lax.axis_index("exp")
        self.core = lax.rem(me, 2)
        chip = lax.div(me, 2)
        self.y = lax.div(chip, SIDE)
        self.x = lax.rem(chip, SIDE)

    def chip(self, dy, dx):
        return lax.rem(self.y + dy + SIDE, SIDE) * SIDE + lax.rem(self.x + dx + SIDE, SIDE)

    def device(self, dy, dx):
        return {"exp": self.chip(dy, dx) * 2 + self.core}

    def level(self, dz):
        return {"req": lax.rem(lax.axis_index("req") + dz + SIDE, SIDE)}

    def partner(self):
        return {"exp": self.chip(0, 0) * 2 + 1 - self.core}

    def mirror(self, same_core):
        core = self.core if same_core else 1 - self.core
        return {"exp": (CHIPS - 1 - self.chip(0, 0)) * 2 + core}


NEXT = ((0, 1), (0, -1), (1, 0), (-1, 0))
OTHERS = tuple((dy, dx) for dy in range(SIDE) for dx in range(SIDE) if dy or dx)


def greet(plane, places=NEXT, devices=()):
    barrier = pltpu.get_barrier_semaphore()
    for device in [plane.device(dy, dx) for dy, dx in places] + list(devices):
        pl.semaphore_signal(
            barrier, inc=1, device_id=device, device_id_type=pl.DeviceIdType.MESH
        )
    pl.semaphore_wait(barrier, len(places) + len(devices))


def remote(src, dst, send, recv, device):
    return pltpu.make_async_remote_copy(
        src_ref=src,
        dst_ref=dst,
        send_sem=send,
        recv_sem=recv,
        device_id=device,
        device_id_type=pl.DeviceIdType.MESH,
    )


def turn(h, a, b):
    return (b, a) if h == 0 else (a, b)


class Gather:
    COPIES = 20

    def __init__(self, plane, own, slots, send, recv, rows, slot_of):
        self.plane, self.own, self.slots = plane, own, slots
        self.send, self.recv, self.rows, self.slot_of = send, recv, rows, slot_of

    def span(self, h, part):
        half = self.rows // 2
        if part is None:
            return pl.ds(h * half, half)
        return pl.ds(h * half + part * (half // 2), half // 2)

    def step(self, k):
        if k < 4:
            return (
                ((0, 0), None, (1, 0)),
                ((0, 0), None, (-1, 0)),
                ((-1, 0), 0, (1, 0)),
                ((1, 0), 1, (-1, 0)),
            )[k]
        a = (0, -1, 1, 2)[(k - 4) // 4]
        return (
            ((a, 0), None, (0, 1)),
            ((a, 0), None, (0, -1)),
            ((a, -1), 0, (0, 1)),
            ((a, 1), 1, (0, -1)),
        )[(k - 4) % 4]

    def make(self, h, k, incoming):
        (a, b), part, (da, db) = self.step(k)
        span = self.span(h, part)
        if incoming:
            a, b = a - da, b - db
        slot = self.slot_of(self.plane.chip(*turn(h, a, b)))
        there = self.slots.at[slot, span]
        here = self.own.at[span] if (a, b) == (0, 0) else there
        return pltpu.make_async_remote_copy(
            src_ref=here,
            dst_ref=there,
            send_sem=self.send.at[h * self.COPIES + k],
            recv_sem=self.recv.at[h * self.COPIES + k],
            device_id=self.plane.device(*turn(h, da, db)),
            device_id_type=pl.DeviceIdType.MESH,
        )

    def start(self, *ks):
        for k in ks:
            for h in (0, 1):
                self.make(h, k, False).start()

    def arrive(self, k, *then):
        for h in (0, 1):
            self.make(h, k, True).wait_recv()
            for t in then:
                self.make(h, t, False).start()

    def run(self):
        self.start(0, 1)
        self.start(4, 5)
        self.arrive(0, 2, 8, 9)
        self.arrive(1, 3, 12, 13)
        self.arrive(4, 6)
        self.arrive(5, 7)
        self.arrive(2)
        self.arrive(3, 16, 17)
        for base in (8, 12, 16):
            self.arrive(base, base + 2)
            self.arrive(base + 1, base + 3)
        for base in (4, 8, 12, 16):
            self.arrive(base + 2)
            self.arrive(base + 3)

    def finish(self):
        for h in (0, 1):
            for k in range(self.COPIES):
                self.make(h, k, False).wait_send()


def gather_rows(block, weights, collective_id):
    rows, width = block.shape

    def kernel(own, given, slots, other, send, recv, sems):
        plane = Plane()
        greet(plane, NEXT, [plane.partner()])
        swap = remote(given, other, sems.at[1], sems.at[2], plane.partner())
        gather = Gather(plane, own, slots, send, recv, rows, lambda chip: chip)
        mine = pltpu.make_async_copy(own, slots.at[plane.chip(0, 0)], sems.at[0])
        mine.start()
        swap.start()
        gather.run()
        gather.finish()
        mine.wait()
        swap.wait()

    return pl.pallas_call(
        kernel,
        out_shape=(
            jax.ShapeDtypeStruct((CHIPS, rows, width), block.dtype),
            jax.ShapeDtypeStruct(weights.shape, weights.dtype),
        ),
        in_specs=[
            pl.BlockSpec(memory_space=pltpu.VMEM),
            pl.BlockSpec(memory_space=pl.ANY),
        ],
        out_specs=(pl.BlockSpec(memory_space=pl.ANY), pl.BlockSpec(memory_space=pl.ANY)),
        scratch_shapes=[
            pltpu.SemaphoreType.DMA((2 * Gather.COPIES,)),
            pltpu.SemaphoreType.DMA((2 * Gather.COPIES,)),
            pltpu.SemaphoreType.DMA((3,)),
        ],
        compiler_params=pltpu.CompilerParams(collective_id=collective_id, has_side_effects=True),
        name="gather_rows",
    )(block, weights)


KEYS = 512
PAIR = 6
PAIR_WIDTH = PAIR * HEAD_SIZE
LOW = -1e30
SCALE = HEAD_SIZE**-0.5 * 1.4426950408889634
ACROSS = (0, -1, 1, 2)


def attention_kernel(
    queries, pairs, starts, given, weights,
    out, held, gathered, partners,
    near, store, asked, begin, packed, peak, total, bias, done,
    give, take, x_send, x_recv, y_send, y_recv, q_send, q_recv, o_send, o_recv, w_send, w_recv, sems,
):
    plane = Plane()
    core, odd = plane.core, lax.rem(plane.x, 2)
    here = plane.chip(0, 0)
    rows = queries.shape[0]
    friends = [plane.partner(), plane.mirror(True), plane.mirror(False)]
    greet(plane, OTHERS, [friends[0], friends[2], plane.level(1), plane.level(-1)])

    mine = 2 * core + odd
    theirs = [2 * (1 - core) + odd, 2 * core + 1 - odd, 2 * (1 - core) + 1 - odd]
    slots = [core, 2 + core, 2 + core]
    from_slots = [1 - core, 2 + core, 2 + 1 - core]

    def lanes(at, size):
        return pl.ds(pl.multiple_of(at * size, size), size)

    swap = remote(
        pairs.at[:, lanes(1 - core, 512)], near, sems.at[0], sems.at[1], friends[0]
    )

    def source(h, parity):
        if h == 0:
            return pairs.at[:, lanes(2 * core + parity, 256)]
        return near.at[:, lanes(parity, 256)]

    def slot(h, dy, dx, part=None):
        low = (core if h == 0 else 1 - core) * rows
        size = rows
        if part is not None:
            size = rows // 2
            low = low + part * size
        return store.at[plane.chip(dy, dx), pl.ds(pl.multiple_of(low, size), size)]

    def keep(h):
        return pltpu.make_async_copy(source(h, odd), slot(h, 0, 0), sems.at[2 + h])

    def across(h, n, incoming=False):
        dx = (1, -1, 2)[n]
        return remote(
            source(h, odd if n == 2 else 1 - odd),
            slot(h, 0, -dx if incoming else 0),
            x_send.at[3 * h + n],
            x_recv.at[3 * h + n],
            plane.device(0, dx),
        )

    def along(h, i, n, incoming=False):
        dx = ACROSS[i]
        at, part, dy = ((0, None, 1), (0, None, -1), (-1, 0, 1), (1, 1, -1))[n]
        place = slot(h, at - dy if incoming else at, dx, part)
        src = source(h, odd) if (i == 0 and n < 2) else place
        if i == 0 and n < 2 and not incoming:
            place = slot(h, 0, 0)
        k = (h * 4 + i) * 4 + n
        return remote(src, place, y_send.at[k], y_recv.at[k], plane.device(dy, 0))

    def ask(n, incoming=False):
        at = from_slots[n] if incoming else slots[n]
        return remote(
            queries.at[:, lanes(theirs[n], PAIR_WIDTH)],
            asked.at[at],
            q_send.at[n],
            q_recv.at[n],
            friends[n],
        )

    def tell(n, incoming=False):
        at = from_slots[n] if incoming else slots[n]
        return remote(starts, begin.at[at], q_send.at[3 + n], q_recv.at[3 + n], friends[n])

    def table(n, incoming=False):
        dy, dx = OTHERS[n]
        return remote(
            given.at[plane.chip(dy, dx)],
            held.at[plane.chip(-dy, -dx) if incoming else here],
            give.at[n],
            take.at[n],
            plane.device(dy, dx),
        )

    def slice_copy(n):
        if n < 2:
            return remote(
                weights, gathered.at[n], w_send.at[n], w_recv.at[n], plane.level((1, -1)[n])
            )
        if n < 4:
            size = weights.shape[1] // 2
            part = pl.ds((n - 2) * size, size)
            return remote(
                gathered.at[n - 2, :, part],
                gathered.at[2, :, part],
                w_send.at[n],
                w_recv.at[n],
                plane.level((1, -1)[n - 2]),
            )
        return remote(weights, partners, w_send.at[n], w_recv.at[n], friends[0])

    own_asked = pltpu.make_async_copy(
        queries.at[:, lanes(mine, PAIR_WIDTH)], asked.at[core], sems.at[4]
    )
    own_begin = pltpu.make_async_copy(starts, begin.at[core], sems.at[5])
    own_table = pltpu.make_async_copy(given.at[here], held.at[here], sems.at[6])

    swap.start()
    for h in (0, 1):
        if h == 1:
            ask(0).start()
            tell(0).start()
            own_asked.start()
            own_begin.start()
            own_table.start()
            swap.wait_recv()
        keep(h).start()
        for n in range(3):
            across(h, n).start()
        along(h, 0, 0).start()
        along(h, 0, 1).start()
    for n in (1, 2):
        ask(n).start()
        tell(n).start()
    for n in range(3):
        i = (1, 2, 3)[n]
        for h in (0, 1):
            across(h, n, True).wait_recv()
            along(h, i, 0).start()
            along(h, i, 1).start()
    for n in range(len(OTHERS)):
        table(n).start()
    for n in (0, 1, 4):
        slice_copy(n).start()

    own_asked.wait()
    own_begin.wait()
    for n in range(3):
        ask(n, True).wait_recv()
        tell(n, True).wait_recv()
    for h in (0, 1):
        keep(h).wait()

    lane = lax.broadcasted_iota(jnp.int32, (rows, 128), 1)
    low_half = lane < HEAD_SIZE
    for which in (0, 1):
        for side in (0, 1):
            for n in range(PAIR):
                tile = asked[2 * which + side, :, (n // 2) * 128 : (n // 2 + 1) * 128].astype(
                    jnp.float32
                )
                group = n // 3
                if n % 2 != group:
                    tile = pltpu.roll(tile, HEAD_SIZE, axis=1)
                own_half = low_half if group == 0 else jnp.logical_not(low_half)
                at = (n * 2 + side) * rows
                packed[which, at : at + rows, :] = jnp.where(own_half, tile, 0.0).astype(
                    jnp.bfloat16
                )
    peak[...] = jnp.full_like(peak, LOW)
    total[...] = jnp.zeros_like(total)
    half = PAIR * rows

    def visit(which, chip):
        stream_chip = jnp.where(which == 0, here, CHIPS - 1 - here)
        at = chip * (2 * rows)
        for side in (0, 1):
            first = jnp.broadcast_to(begin[2 * which + side, 0:1, :], (rows, rows)).T
            first = jnp.concatenate([first] * (KEYS // rows), axis=1).astype(jnp.int32)
            key_pos = at + lax.broadcasted_iota(jnp.int32, (rows, KEYS), 1)
            own_pos = (2 * stream_chip + side) * rows + lax.broadcasted_iota(
                jnp.int32, (rows, KEYS), 0
            )
            bias[side * rows : (side + 1) * rows, :] = jnp.where(
                (key_pos >= first) & (key_pos <= own_pos), 0.0, LOW
            )
        tile = store[pl.ds(chip, 2)].reshape(KEYS, 256)
        key, value = tile[:, :128], tile[:, 128:]
        key_lane = lax.broadcasted_iota(jnp.int32, (KEYS, 128), 1)
        for group in (0, 1):
            span = pl.ds(group * half, half)
            scores = lax.dot_general(
                packed[which, span, :],
                key,
                (((1,), (1,)), ((), ())),
                preferred_element_type=jnp.float32,
            )
            scores = (scores.reshape(PAIR // 2, 2 * rows, KEYS) + bias[...][None]).reshape(
                half, KEYS
            )
            before = peak[which, span, :]
            now = jnp.maximum(before, jnp.max(scores, axis=1, keepdims=True))
            peak[which, span, :] = now
            fade = jnp.exp2((before - now) * SCALE)
            wide = jnp.concatenate([now] * (KEYS // 128), axis=1)
            probs = jnp.exp2((scores - wide) * SCALE).astype(jnp.bfloat16)
            own_half = (key_lane < HEAD_SIZE) == (group == 0)
            beside = jnp.where(own_half, value, jnp.ones_like(value))
            total[which, span, :] = total[which, span, :] * fade + jnp.dot(
                probs, beside, preferred_element_type=jnp.float32
            )

    def phase(step, carry):
        @pl.when(step == 1)
        def _():
            for i in range(4):
                for n in (0, 1):
                    for h in (0, 1):
                        along(h, i, n, True).wait_recv()
                        along(h, i, n + 2).start()

        @pl.when(step == 3)
        def _():
            for i in range(4):
                for n in (2, 3):
                    for h in (0, 1):
                        along(h, i, n, True).wait_recv()
            for n in (0, 1):
                slice_copy(n).wait_recv()
                slice_copy(n + 2).start()

        dy = jnp.where(step == 0, 0, jnp.where(step == 1, SIDE - 1, step - 1))
        dy = jnp.where(step == 3, 2, dy)
        row = lax.rem(plane.y + dy, SIDE) * SIDE

        def one(t, carry):
            which = lax.div(t, 2)
            chip = row + 2 * lax.rem(t, 2)
            limit = jnp.where(which == 0, here, CHIPS - 1 - here)

            @pl.when(chip <= limit)
            def _():
                visit(which, chip)

            return carry

        return lax.fori_loop(0, 4, one, carry)

    lax.fori_loop(0, 4, phase, 0)

    def answer(which, side):
        def head(n):
            at = (n * 2 + side) * rows
            sums = total[which, at : at + rows, :]
            result = sums / pltpu.roll(sums, HEAD_SIZE, axis=1)
            if n % 2 != n // 3:
                result = pltpu.roll(result, HEAD_SIZE, axis=1)
            return result

        return [
            jnp.where(low_half, head(2 * i), head(2 * i + 1)).astype(out.dtype)
            for i in range(PAIR // 2)
        ]

    for which in (1, 0):
        for side in (0, 1):
            for i, piece in enumerate(answer(which, side)):
                done[2 * which + side, :, i * 128 : (i + 1) * 128] = piece

    def reply(n, incoming=False):
        return remote(
            done.at[from_slots[n]],
            out.at[:, lanes(theirs[n] if incoming else mine, PAIR_WIDTH)],
            o_send.at[n],
            o_recv.at[n],
            friends[n],
        )

    for n in (1, 2, 0):
        reply(n).start()
    own_reply = pltpu.make_async_copy(
        done.at[core], out.at[:, lanes(mine, PAIR_WIDTH)], sems.at[7]
    )
    own_reply.start()

    swap.wait_send()
    own_table.wait()
    for h in (0, 1):
        for n in range(3):
            across(h, n).wait_send()
        for i in range(4):
            for n in range(4):
                along(h, i, n).wait_send()
    for n in range(3):
        ask(n).wait_send()
        tell(n).wait_send()
    for n in range(len(OTHERS)):
        table(n, True).wait_recv()
        table(n).wait_send()
    own_reply.wait()
    for n in range(3):
        reply(n, True).wait_recv()
        reply(n).wait_send()
    for n in (2, 3, 4):
        slice_copy(n).wait_recv()
    for n in range(5):
        slice_copy(n).wait_send()


def attend(queries, pairs, starts, tables, weights, collective_id):
    rows, width = queries.shape
    dma = pltpu.SemaphoreType.DMA
    return pl.pallas_call(
        attention_kernel,
        out_shape=(
            jax.ShapeDtypeStruct((rows, width), jnp.bfloat16),
            jax.ShapeDtypeStruct(tables.shape, tables.dtype),
            jax.ShapeDtypeStruct((3, *weights.shape), weights.dtype),
            jax.ShapeDtypeStruct(weights.shape, weights.dtype),
        ),
        in_specs=[pl.BlockSpec(memory_space=pltpu.VMEM)] * 4 + [pl.BlockSpec(memory_space=pl.ANY)],
        out_specs=(pl.BlockSpec(memory_space=pltpu.VMEM),) * 2
        + (pl.BlockSpec(memory_space=pl.ANY),) * 2,
        scratch_shapes=[
            pltpu.VMEM((rows, 512), jnp.bfloat16),
            pltpu.VMEM((CHIPS, 2 * rows, 256), jnp.bfloat16),
            pltpu.VMEM((4, rows, PAIR_WIDTH), jnp.bfloat16),
            pltpu.VMEM((4, 8, rows), jnp.float32),
            pltpu.VMEM((2, 2 * PAIR * rows, 128), jnp.bfloat16),
            pltpu.VMEM((2, 2 * PAIR * rows, 128), jnp.float32),
            pltpu.VMEM((2, 2 * PAIR * rows, 128), jnp.float32),
            pltpu.VMEM((2 * rows, KEYS), jnp.float32),
            pltpu.VMEM((4, rows, PAIR_WIDTH), jnp.bfloat16),
            dma((len(OTHERS),)),
            dma((len(OTHERS),)),
            dma((6,)),
            dma((6,)),
            dma((32,)),
            dma((32,)),
            dma((6,)),
            dma((6,)),
            dma((3,)),
            dma((3,)),
            dma((5,)),
            dma((5,)),
            dma((8,)),
        ],
        compiler_params=pltpu.CompilerParams(
            collective_id=collective_id, has_side_effects=True, vmem_limit_bytes=60 << 20
        ),
        name="attention",
    )(queries, pairs, starts, tables, weights)


class Scatter:
    COPIES = 20

    def __init__(self, plane, parts, hold, send, recv, rows):
        self.plane, self.parts, self.hold = plane, parts, hold
        self.send, self.recv, self.rows = send, recv, rows

    def span(self, h, part):
        half = self.rows // 2
        if part is None:
            return pl.ds(h * half, half)
        return pl.ds(h * half + part * (half // 2), half // 2)

    def step(self, k):
        if k < 16:
            q = (2, 1, 3, 0)[k // 4]
            return (
                ((2, q), 0, (1, 0)),
                ((2, q), 1, (-1, 0)),
                ((1, q), None, (1, 0)),
                ((3, q), None, (-1, 0)),
            )[k % 4]
        return (
            ((0, 2), 0, (0, 1)),
            ((0, 2), 1, (0, -1)),
            ((0, 1), None, (0, 1)),
            ((0, 3), None, (0, -1)),
        )[k % 4]

    def make(self, h, k):
        (a, b), part, (da, db) = self.step(k)
        span = self.span(h, part)
        size = self.rows // 2 if part is None else self.rows // 4
        return pltpu.make_async_remote_copy(
            src_ref=self.parts.at[self.plane.chip(*turn(h, a, b)), span],
            dst_ref=self.hold.at[h, k, pl.ds(0, size)],
            send_sem=self.send.at[h * self.COPIES + k],
            recv_sem=self.recv.at[h * self.COPIES + k],
            device_id=self.plane.device(*turn(h, da, db)),
            device_id_type=pl.DeviceIdType.MESH,
        )

    def start(self, k):
        for h in (0, 1):
            self.make(h, k).start()

    def add(self, h, k, place, part):
        size = self.rows // 4
        at = (self.plane.chip(*turn(h, *place)), self.span(h, part))
        self.parts[at] = (
            self.parts[at].astype(jnp.float32)
            + self.hold[h, k, pl.ds(0, size)].astype(jnp.float32)
        ).astype(jnp.bfloat16)

    def relay(self, base, near, far):
        for h in (0, 1):
            self.make(h, base).wait_recv()
            self.add(h, base, near, 0)
            self.make(h, base + 2).start()
        for h in (0, 1):
            self.make(h, base + 1).wait_recv()
            self.add(h, base + 1, far, 1)
            self.make(h, base + 3).start()

    def total(self, h, base, place):
        self.make(h, base + 2).wait_recv()
        self.make(h, base + 3).wait_recv()
        at = (self.plane.chip(*turn(h, *place)), self.span(h, None))
        return (
            self.parts[at].astype(jnp.float32)
            + self.hold[h, base + 2].astype(jnp.float32)
            + self.hold[h, base + 3].astype(jnp.float32)
        )

    def run(self, out):
        for i in range(4):
            self.start(4 * i)
            self.start(4 * i + 1)
        for i, q in enumerate((2, 1, 3, 0)):
            self.relay(4 * i, (1, q), (3, q))
        for i, q in enumerate((2, 1, 3, 0)):
            for h in (0, 1):
                at = (self.plane.chip(*turn(h, 0, q)), self.span(h, None))
                self.parts[at] = self.total(h, 4 * i, (0, q)).astype(jnp.bfloat16)
            if i == 0:
                self.start(16)
                self.start(17)
            if i == 2:
                self.relay(16, (0, 1), (0, 3))
        for h in (0, 1):
            out[self.span(h, None)] = self.total(h, 16, (0, 0))

    def finish(self):
        for h in (0, 1):
            for k in range(self.COPIES):
                self.make(h, k).wait_send()


def scatter_sums(parts, collective_id):
    _, rows, width = parts.shape

    def kernel(given, out, held, hold, send, recv, in_sem):
        load = pltpu.make_async_copy(given, held, in_sem)
        load.start()
        plane = Plane()
        greet(plane)
        load.wait()
        scatter = Scatter(plane, held, hold, send, recv, rows)
        scatter.run(out)
        scatter.finish()

    return pl.pallas_call(
        kernel,
        out_shape=jax.ShapeDtypeStruct((rows, width), jnp.float32),
        in_specs=[pl.BlockSpec(memory_space=pl.ANY)],
        out_specs=pl.BlockSpec(memory_space=pltpu.VMEM),
        scratch_shapes=[
            pltpu.VMEM((CHIPS, rows, width), jnp.bfloat16),
            pltpu.VMEM((2, Scatter.COPIES, rows // 2, width), jnp.bfloat16),
            pltpu.SemaphoreType.DMA((2 * Scatter.COPIES,)),
            pltpu.SemaphoreType.DMA((2 * Scatter.COPIES,)),
            pltpu.SemaphoreType.DMA,
        ],
        compiler_params=pltpu.CompilerParams(
            collective_id=collective_id, has_side_effects=True, vmem_limit_bytes=60 << 20
        ),
        name="scatter_sums",
    )(parts)


BLOCKS = 4


def expert_kernel(tables, rows_in, own, own_rest, other, other_rest, out, weights, picked, made, sems):
    step = pl.program_id(0)
    core = lax.rem(lax.axis_index("exp"), 2)

    def loads():
        for e, (first, rest) in enumerate(((own, own_rest), (other, other_rest))):
            for r in range(4):
                yield pltpu.make_async_copy(
                    first if r == 0 else rest.at[r - 1],
                    weights.at[core if e == 0 else 1 - core, :, :, pl.ds(r * 128, 128)],
                    sems.at[e * 4 + r],
                )

    @pl.when(step == 0)
    def _():
        for load in loads():
            load.start()

    tokens = rows_in.shape[1]
    slot = lax.broadcasted_iota(jnp.int32, (SLOTS, tokens), 0).astype(jnp.float32)

    def hits(j):
        return jnp.concatenate([tables[j, 2 + e : 3 + e, :] == slot for e in (0, 1)], axis=0)

    for j in range(BLOCKS):
        choose = jnp.where(hits(j), 1.0, 0.0).astype(jnp.bfloat16)
        picked[j] = jnp.dot(choose, rows_in[j], preferred_element_type=jnp.float32).astype(
            jnp.bfloat16
        )

    @pl.when(step == 0)
    def _():
        for load in loads():
            load.wait()

    width = rows_in.shape[2]
    for e in (0, 1):
        rows = picked[:, e * SLOTS : (e + 1) * SLOTS, :].reshape(BLOCKS * SLOTS, width)
        gate = jnp.dot(rows, weights[e, 0], preferred_element_type=jnp.float32)
        up = jnp.dot(rows, weights[e, 1], preferred_element_type=jnp.float32)
        units = (gate / (1.0 + jnp.exp(-gate)) * up).astype(jnp.bfloat16)
        result = lax.dot_general(
            units, weights[e, 2], (((1,), (1,)), ((), ())), preferred_element_type=jnp.float32
        )
        for j in range(BLOCKS):
            gain = jnp.sum(
                jnp.where(tables[j, 2 + e : 3 + e, :] == slot, tables[j, e : e + 1, :], 0.0),
                axis=1,
                keepdims=True,
            )
            made[j, e * SLOTS : (e + 1) * SLOTS, :] = (
                result[j * SLOTS : (j + 1) * SLOTS, :] * gain
            ).astype(jnp.bfloat16)

    for j in range(BLOCKS):
        choose = jnp.where(hits(j), 1.0, 0.0).astype(jnp.bfloat16)
        out[j] = lax.dot_general(
            choose, made[j], (((0,), (0,)), ((), ())), preferred_element_type=jnp.float32
        ).astype(jnp.bfloat16)


def run_experts(tables, rows_in, *weights):
    chips, tokens, width = rows_in.shape
    return pl.pallas_call(
        expert_kernel,
        grid=(chips // BLOCKS,),
        out_shape=jax.ShapeDtypeStruct(rows_in.shape, jnp.bfloat16),
        in_specs=[
            pl.BlockSpec((BLOCKS, 8, tokens), lambda i: (i, 0, 0)),
            pl.BlockSpec((BLOCKS, tokens, width), lambda i: (i, 0, 0)),
        ]
        + [pl.BlockSpec(memory_space=pl.ANY)] * 4,
        out_specs=pl.BlockSpec((BLOCKS, tokens, width), lambda i: (i, 0, 0)),
        scratch_shapes=[
            pltpu.VMEM((2, 3, width, FF), jnp.bfloat16),
            pltpu.VMEM((BLOCKS, 2 * SLOTS, width), jnp.bfloat16),
            pltpu.VMEM((BLOCKS, 2 * SLOTS, width), jnp.bfloat16),
            pltpu.SemaphoreType.DMA((8,)),
        ],
        compiler_params=pltpu.CompilerParams(vmem_limit_bytes=60 << 20),
        name="experts",
    )(tables, rows_in, *weights)


def slot_tables(routes, route_weights):
    tokens = routes.shape[0]
    hit = routes[None] == jnp.arange(EXPERTS, dtype=jnp.int32)[:, None, None]
    gains = jnp.sum(jnp.where(hit, route_weights[None], 0.0), axis=2)
    named = jnp.any(hit, axis=2)
    earlier = jnp.triu(jnp.ones((tokens, tokens), jnp.bfloat16), 1)
    ranks = jnp.dot(named.astype(jnp.bfloat16), earlier, preferred_element_type=jnp.float32)
    ranks = jnp.where(named, ranks, -1.0)
    pairs = [t.reshape(CHIPS, 2, tokens) for t in (gains, ranks)]
    return jnp.concatenate(pairs + [jnp.zeros((CHIPS, 4, tokens), jnp.float32)], axis=1)


def shards(
    hidden,
    attn_gain,
    query_weight,
    key_matrix,
    value_matrix,
    output_weight,
    prompt_start,
    ffn_gain,
    routes,
    route_weights,
    expert_weights,
):
    total_row_count = hidden.shape[0]
    lane_index = lax.axis_index("exp")
    positions = lane_index * total_row_count + jnp.arange(total_row_count, dtype=jnp.int32)
    stream_offsets = positions - prompt_start
    inputs = hidden.astype(jnp.float32)
    normalized_input = rms_norm(inputs, attn_gain).astype(jnp.bfloat16)
    query_rows_all = jnp.dot(
        normalized_input, query_weight, preferred_element_type=jnp.float32
    ).reshape(total_row_count, QUERY_HEADS, HEAD_SIZE)
    query_rows_all = (
        rotary_embedding(query_rows_all, stream_offsets)
        .astype(jnp.bfloat16)
        .reshape(total_row_count, QUERY_HEADS * HEAD_SIZE)
    )
    shard_keys = jnp.dot(normalized_input, key_matrix, preferred_element_type=jnp.float32).reshape(
        total_row_count, KEY_VALUE_HEADS, HEAD_SIZE
    )
    shard_keys = (
        rotary_embedding(shard_keys, stream_offsets)
        .astype(jnp.bfloat16)
        .reshape(total_row_count, KEY_VALUE_HEADS * HEAD_SIZE)
    )
    values_local = jnp.dot(
        normalized_input, value_matrix, preferred_element_type=jnp.float32
    ).astype(jnp.bfloat16)
    pairs = jnp.concatenate(
        [
            side[:, p * 128 : (p + 1) * 128]
            for p in range(KEY_VALUE_HEADS // 2)
            for side in (shard_keys, values_local)
        ],
        axis=1,
    )
    starts = jnp.broadcast_to(prompt_start.astype(jnp.float32)[None], (8, total_row_count))
    own = expert_weights[0]
    attention, tables, own_rest, other = attend(
        query_rows_all, pairs, starts, slot_tables(routes, route_weights), own, 0
    )
    residual = inputs + jnp.dot(attention, output_weight, preferred_element_type=jnp.float32)
    moe_in = rms_norm(residual, ffn_gain).astype(jnp.bfloat16)

    rows_in, other_rest = gather_rows(moe_in, own_rest, 1)
    parts = run_experts(tables, rows_in, own, own_rest, other, other_rest)
    moe_sum = scatter_sums(parts, 2)
    layer_out = (residual + moe_sum).astype(jnp.bfloat16)
    return (layer_out, shard_keys, values_local)


def solution(mesh):
    in_specs = (
        P(("req", "exp"), None),
        P(),
        P(),
        P(),
        P(),
        P(),
        P(("req", "exp")),
        P(),
        P(("req", "exp"), None),
        P(("req", "exp"), None),
        P("exp", None, None, "req"),
    )
    out_specs = (P(("req", "exp"), None), P(("req", "exp"), None), P(("req", "exp"), None))
    return jax.shard_map(shards, mesh=mesh, in_specs=in_specs, out_specs=out_specs, check_vma=False)
```

```python
import jax
import jax.numpy as jnp
from jax import lax
from jax.experimental import pallas as pl
from jax.experimental.pallas import tpu as pltpu
from jax.sharding import PartitionSpec as P

QUERY_HEADS = 24
KEY_VALUE_HEADS = 8
HEAD_SIZE = 64
TOP = 8
SIDE = 4
CHIPS = SIDE * SIDE
EXPERTS = 32
SLOTS = 64
FF = 512


epsilon = 1e-05


def rms_norm(values, gain):
    mean_square = jnp.mean(values * values, axis=-1, keepdims=True)
    return values * lax.rsqrt(mean_square + epsilon) * gain


def rotary_embedding(heads_in, stream_offsets):
    half = heads_in.shape[-1] // 2
    freqs = 10000.0 ** (-jnp.arange(half, dtype=jnp.float32) / half)
    angle = stream_offsets.astype(jnp.float32)[:, None] * freqs[None, :]
    cosine = jnp.cos(angle)[:, None, :]
    sine = jnp.sin(angle)[:, None, :]
    first_half = heads_in[..., :half]
    second_half = heads_in[..., half:]
    return jnp.concatenate(
        [first_half * cosine - second_half * sine, second_half * cosine + first_half * sine],
        axis=-1,
    )


class Plane:
    def __init__(self):
        me = lax.axis_index("exp")
        self.core = lax.rem(me, 2)
        chip = lax.div(me, 2)
        self.y = lax.div(chip, SIDE)
        self.x = lax.rem(chip, SIDE)

    def chip(self, dy, dx):
        return lax.rem(self.y + dy + SIDE, SIDE) * SIDE + lax.rem(self.x + dx + SIDE, SIDE)

    def device(self, dy, dx):
        return {"exp": self.chip(dy, dx) * 2 + self.core}

    def level(self, dz):
        return {"req": lax.rem(lax.axis_index("req") + dz + SIDE, SIDE)}

    def partner(self):
        return {"exp": self.chip(0, 0) * 2 + 1 - self.core}

    def mirror(self, same_core):
        core = self.core if same_core else 1 - self.core
        return {"exp": (CHIPS - 1 - self.chip(0, 0)) * 2 + core}


NEXT = ((0, 1), (0, -1), (1, 0), (-1, 0))
OTHERS = tuple((dy, dx) for dy in range(SIDE) for dx in range(SIDE) if dy or dx)


def greet(plane, places=NEXT, devices=()):
    barrier = pltpu.get_barrier_semaphore()
    for device in [plane.device(dy, dx) for dy, dx in places] + list(devices):
        pl.semaphore_signal(
            barrier, inc=1, device_id=device, device_id_type=pl.DeviceIdType.MESH
        )
    pl.semaphore_wait(barrier, len(places) + len(devices))


def remote(src, dst, send, recv, device):
    return pltpu.make_async_remote_copy(
        src_ref=src,
        dst_ref=dst,
        send_sem=send,
        recv_sem=recv,
        device_id=device,
        device_id_type=pl.DeviceIdType.MESH,
    )


KEYS = 512
PAIR = 6
PAIR_WIDTH = PAIR * HEAD_SIZE
LOW = -1e30
SCALE = HEAD_SIZE**-0.5 * 1.4426950408889634
ACROSS = (0, -1, 1, 2)


def attention_kernel(
    queries, pairs, starts, given, weights,
    out, held, gathered, partners,
    near, store, asked, begin, packed, peak, total, bias, done,
    give, take, x_send, x_recv, y_send, y_recv, q_send, q_recv, o_send, o_recv, w_send, w_recv, sems,
):
    plane = Plane()
    core, odd = plane.core, lax.rem(plane.x, 2)
    here = plane.chip(0, 0)
    rows = queries.shape[0]
    friends = [plane.partner(), plane.mirror(True), plane.mirror(False)]
    greet(plane, OTHERS, [friends[0], friends[2], plane.level(1), plane.level(-1)])

    mine = 2 * core + odd
    theirs = [2 * (1 - core) + odd, 2 * core + 1 - odd, 2 * (1 - core) + 1 - odd]
    slots = [core, 2 + core, 2 + core]
    from_slots = [1 - core, 2 + core, 2 + 1 - core]

    def lanes(at, size):
        return pl.ds(pl.multiple_of(at * size, size), size)

    swap = remote(
        pairs.at[:, lanes(1 - core, 512)], near, sems.at[0], sems.at[1], friends[0]
    )

    def source(h, parity):
        if h == 0:
            return pairs.at[:, lanes(2 * core + parity, 256)]
        return near.at[:, lanes(parity, 256)]

    def slot(h, dy, dx, part=None):
        low = (core if h == 0 else 1 - core) * rows
        size = rows
        if part is not None:
            size = rows // 2
            low = low + part * size
        return store.at[plane.chip(dy, dx), pl.ds(pl.multiple_of(low, size), size)]

    def keep(h):
        return pltpu.make_async_copy(source(h, odd), slot(h, 0, 0), sems.at[2 + h])

    def across(h, n, incoming=False):
        dx = (1, -1, 2)[n]
        return remote(
            source(h, odd if n == 2 else 1 - odd),
            slot(h, 0, -dx if incoming else 0),
            x_send.at[3 * h + n],
            x_recv.at[3 * h + n],
            plane.device(0, dx),
        )

    def along(h, i, n, incoming=False):
        dx = ACROSS[i]
        at, part, dy = ((0, None, 1), (0, None, -1), (-1, 0, 1), (1, 1, -1))[n]
        place = slot(h, at - dy if incoming else at, dx, part)
        src = source(h, odd) if (i == 0 and n < 2) else place
        if i == 0 and n < 2 and not incoming:
            place = slot(h, 0, 0)
        k = (h * 4 + i) * 4 + n
        return remote(src, place, y_send.at[k], y_recv.at[k], plane.device(dy, 0))

    def ask(n, incoming=False):
        at = from_slots[n] if incoming else slots[n]
        return remote(
            queries.at[:, lanes(theirs[n], PAIR_WIDTH)],
            asked.at[at],
            q_send.at[n],
            q_recv.at[n],
            friends[n],
        )

    def tell(n, incoming=False):
        at = from_slots[n] if incoming else slots[n]
        return remote(starts, begin.at[at], q_send.at[3 + n], q_recv.at[3 + n], friends[n])

    def table(n, incoming=False):
        dy, dx = OTHERS[n]
        return remote(
            given.at[plane.chip(dy, dx)],
            held.at[plane.chip(-dy, -dx) if incoming else here],
            give.at[n],
            take.at[n],
            plane.device(dy, dx),
        )

    def slice_copy(n):
        if n < 2:
            return remote(
                weights, gathered.at[n], w_send.at[n], w_recv.at[n], plane.level((1, -1)[n])
            )
        if n < 4:
            size = weights.shape[1] // 2
            part = pl.ds((n - 2) * size, size)
            return remote(
                gathered.at[n - 2, :, part],
                gathered.at[2, :, part],
                w_send.at[n],
                w_recv.at[n],
                plane.level((1, -1)[n - 2]),
            )
        return remote(weights, partners, w_send.at[n], w_recv.at[n], friends[0])

    own_asked = pltpu.make_async_copy(
        queries.at[:, lanes(mine, PAIR_WIDTH)], asked.at[core], sems.at[4]
    )
    own_begin = pltpu.make_async_copy(starts, begin.at[core], sems.at[5])
    own_table = pltpu.make_async_copy(given.at[here], held.at[here], sems.at[6])

    swap.start()
    for n in (0, 1, 4):
        slice_copy(n).start()
    for h in (0, 1):
        if h == 1:
            ask(0).start()
            tell(0).start()
            own_asked.start()
            own_begin.start()
            own_table.start()
            swap.wait_recv()
        keep(h).start()
        for n in range(3):
            across(h, n).start()
        along(h, 0, 0).start()
        along(h, 0, 1).start()
    for n in (1, 2):
        ask(n).start()
        tell(n).start()
    for n in range(3):
        i = (1, 2, 3)[n]
        for h in (0, 1):
            across(h, n, True).wait_recv()
            along(h, i, 0).start()
            along(h, i, 1).start()
    for n in range(len(OTHERS)):
        table(n).start()

    own_asked.wait()
    own_begin.wait()
    for n in range(3):
        ask(n, True).wait_recv()
        tell(n, True).wait_recv()
    for h in (0, 1):
        keep(h).wait()

    lane = lax.broadcasted_iota(jnp.int32, (rows, 128), 1)
    low_half = lane < HEAD_SIZE
    for which in (0, 1):
        for side in (0, 1):
            for n in range(PAIR):
                tile = asked[2 * which + side, :, (n // 2) * 128 : (n // 2 + 1) * 128].astype(
                    jnp.float32
                )
                group = n // 3
                if n % 2 != group:
                    tile = pltpu.roll(tile, HEAD_SIZE, axis=1)
                own_half = low_half if group == 0 else jnp.logical_not(low_half)
                at = (n * 2 + side) * rows
                packed[which, at : at + rows, :] = jnp.where(own_half, tile, 0.0).astype(
                    jnp.bfloat16
                )
    peak[...] = jnp.full_like(peak, LOW)
    total[...] = jnp.zeros_like(total)
    half = PAIR * rows

    def visit(which, chip):
        stream_chip = jnp.where(which == 0, here, CHIPS - 1 - here)
        at = chip * (2 * rows)
        for side in (0, 1):
            first = jnp.broadcast_to(begin[2 * which + side, 0:1, :], (rows, rows)).T
            first = jnp.concatenate([first] * (KEYS // rows), axis=1).astype(jnp.int32)
            key_pos = at + lax.broadcasted_iota(jnp.int32, (rows, KEYS), 1)
            own_pos = (2 * stream_chip + side) * rows + lax.broadcasted_iota(
                jnp.int32, (rows, KEYS), 0
            )
            bias[side * rows : (side + 1) * rows, :] = jnp.where(
                (key_pos >= first) & (key_pos <= own_pos), 0.0, LOW
            )
        tile = store[pl.ds(chip, 2)].reshape(KEYS, 256)
        key, value = tile[:, :128], tile[:, 128:]
        key_lane = lax.broadcasted_iota(jnp.int32, (KEYS, 128), 1)
        for group in (0, 1):
            span = pl.ds(group * half, half)
            scores = lax.dot_general(
                packed[which, span, :],
                key,
                (((1,), (1,)), ((), ())),
                preferred_element_type=jnp.float32,
            )
            scores = (scores.reshape(PAIR // 2, 2 * rows, KEYS) + bias[...][None]).reshape(
                half, KEYS
            )
            before = peak[which, span, :]
            now = jnp.maximum(before, jnp.max(scores, axis=1, keepdims=True))
            peak[which, span, :] = now
            fade = jnp.exp2((before - now) * SCALE)
            wide = jnp.concatenate([now] * (KEYS // 128), axis=1)
            probs = jnp.exp2((scores - wide) * SCALE).astype(jnp.bfloat16)
            own_half = (key_lane < HEAD_SIZE) == (group == 0)
            beside = jnp.where(own_half, value, jnp.ones_like(value))
            total[which, span, :] = total[which, span, :] * fade + jnp.dot(
                probs, beside, preferred_element_type=jnp.float32
            )

    def phase(step, carry):
        @pl.when(step == 1)
        def _():
            for i in range(4):
                for n in (0, 1):
                    for h in (0, 1):
                        along(h, i, n, True).wait_recv()
                        along(h, i, n + 2).start()

        @pl.when(step == 2)
        def _():
            for n in (0, 1):
                slice_copy(n).wait_recv()
                slice_copy(n + 2).start()

        @pl.when(step == 3)
        def _():
            for i in range(4):
                for n in (2, 3):
                    for h in (0, 1):
                        along(h, i, n, True).wait_recv()

        dy = jnp.where(step == 0, 0, jnp.where(step == 1, SIDE - 1, step - 1))
        dy = jnp.where(step == 3, 2, dy)
        row = lax.rem(plane.y + dy, SIDE) * SIDE

        def one(t, carry):
            which = lax.div(t, 2)
            chip = row + 2 * lax.rem(t, 2)
            limit = jnp.where(which == 0, here, CHIPS - 1 - here)

            @pl.when(chip <= limit)
            def _():
                visit(which, chip)

            return carry

        return lax.fori_loop(0, 4, one, carry)

    lax.fori_loop(0, 4, phase, 0)

    def answer(which, side):
        def head(n):
            at = (n * 2 + side) * rows
            sums = total[which, at : at + rows, :]
            result = sums / pltpu.roll(sums, HEAD_SIZE, axis=1)
            if n % 2 != n // 3:
                result = pltpu.roll(result, HEAD_SIZE, axis=1)
            return result

        return [
            jnp.where(low_half, head(2 * i), head(2 * i + 1)).astype(out.dtype)
            for i in range(PAIR // 2)
        ]

    for which in (1, 0):
        for side in (0, 1):
            for i, piece in enumerate(answer(which, side)):
                done[2 * which + side, :, i * 128 : (i + 1) * 128] = piece

    def reply(n, incoming=False):
        return remote(
            done.at[from_slots[n]],
            out.at[:, lanes(theirs[n] if incoming else mine, PAIR_WIDTH)],
            o_send.at[n],
            o_recv.at[n],
            friends[n],
        )

    for n in (1, 2, 0):
        reply(n).start()
    own_reply = pltpu.make_async_copy(
        done.at[core], out.at[:, lanes(mine, PAIR_WIDTH)], sems.at[7]
    )
    own_reply.start()

    swap.wait_send()
    own_table.wait()
    for h in (0, 1):
        for n in range(3):
            across(h, n).wait_send()
        for i in range(4):
            for n in range(4):
                along(h, i, n).wait_send()
    for n in range(3):
        ask(n).wait_send()
        tell(n).wait_send()
    for n in range(len(OTHERS)):
        table(n, True).wait_recv()
        table(n).wait_send()
    own_reply.wait()
    for n in range(3):
        reply(n, True).wait_recv()
        reply(n).wait_send()
    for n in (2, 3, 4):
        slice_copy(n).wait_recv()
    for n in range(5):
        slice_copy(n).wait_send()


def attend(queries, pairs, starts, tables, weights, collective_id):
    rows, width = queries.shape
    dma = pltpu.SemaphoreType.DMA
    return pl.pallas_call(
        attention_kernel,
        out_shape=(
            jax.ShapeDtypeStruct((rows, width), jnp.bfloat16),
            jax.ShapeDtypeStruct(tables.shape, tables.dtype),
            jax.ShapeDtypeStruct((3, *weights.shape), weights.dtype),
            jax.ShapeDtypeStruct(weights.shape, weights.dtype),
        ),
        in_specs=[pl.BlockSpec(memory_space=pltpu.VMEM)] * 4 + [pl.BlockSpec(memory_space=pl.ANY)],
        out_specs=(pl.BlockSpec(memory_space=pltpu.VMEM),) * 2
        + (pl.BlockSpec(memory_space=pl.ANY),) * 2,
        scratch_shapes=[
            pltpu.VMEM((rows, 512), jnp.bfloat16),
            pltpu.VMEM((CHIPS, 2 * rows, 256), jnp.bfloat16),
            pltpu.VMEM((4, rows, PAIR_WIDTH), jnp.bfloat16),
            pltpu.VMEM((4, 8, rows), jnp.float32),
            pltpu.VMEM((2, 2 * PAIR * rows, 128), jnp.bfloat16),
            pltpu.VMEM((2, 2 * PAIR * rows, 128), jnp.float32),
            pltpu.VMEM((2, 2 * PAIR * rows, 128), jnp.float32),
            pltpu.VMEM((2 * rows, KEYS), jnp.float32),
            pltpu.VMEM((4, rows, PAIR_WIDTH), jnp.bfloat16),
            dma((len(OTHERS),)),
            dma((len(OTHERS),)),
            dma((6,)),
            dma((6,)),
            dma((32,)),
            dma((32,)),
            dma((6,)),
            dma((6,)),
            dma((3,)),
            dma((3,)),
            dma((5,)),
            dma((5,)),
            dma((8,)),
        ],
        compiler_params=pltpu.CompilerParams(
            collective_id=collective_id, has_side_effects=True, vmem_limit_bytes=60 << 20
        ),
        name="attention",
    )(queries, pairs, starts, tables, weights)


BLOCKS = 4
GROUPS = (
    ((0, 0), (2, 0), (0, -1), (0, 1)),
    ((-1, 0), (1, 0), (-1, -1), (-1, 1)),
    ((-1, 2), (1, 2), (1, -1), (1, 1)),
    ((0, 2), (2, 2), (2, -1), (2, 1)),
)
TWO = (0, 2)
ENDS = (-1, 1)


def experts_kernel(
    own, residual, tables, first, rest, other,
    out,
    rows_in, sums, weights, picked, made, hold_q, hold_r, hold_p, hold_d,
    g_send, g_recv, q_send, q_recv, r_send, r_recv, p_send, p_recv, d_send, d_recv,
    w_send, w_recv, load_sems,
):
    plane = Plane()
    core = plane.core
    rows, width = own.shape
    part_rows = rows // 2
    even = lax.rem(plane.y + plane.x, 2) == 0

    def turned(o, t):
        return jnp.where(even, t, o), jnp.where(even, o, t)

    def place(at):
        return plane.chip(*turned(*at))

    def device(o, t):
        return plane.device(*turned(o, t))

    def part(n):
        return pl.ds(n * part_rows, part_rows)

    greet(plane, NEXT, [plane.partner()])

    def gather(k, src, dst, to):
        return remote(src, dst, g_send.at[k], g_recv.at[k], to)

    def emit(n, incoming=False):
        d = (1, -1)[n]
        at = (0, -d) if incoming else (0, 0)
        return gather(n, own, rows_in.at[place(at)], device(d, 0))

    def pass_on(n, incoming=False):
        at = (2, 0) if incoming else (0, ENDS[n])
        ref = rows_in.at[place(at), part(n)]
        return gather(2 + n, ref, ref, device(0, -ENDS[n]))

    def spread(group, j, n, incoming=False):
        d = (1, -1)[n]
        if group == 0:
            at = (-d, TWO[j]) if incoming else (TWO[j], 0)
            to = device(0, d)
        else:
            at = (ENDS[j], -d) if incoming else (0, ENDS[j])
            to = device(d, 0)
        ref = rows_in.at[place(at)]
        src = own if at == (0, 0) else ref
        return gather(4 + group * 8 + j * 4 + n, src, ref, to)

    def relay(group, j, n, incoming=False):
        if group == 0:
            at = (TWO[j], 2) if incoming else (ENDS[n], TWO[j])
            to = device(-ENDS[n], 0)
        else:
            at = (2, ENDS[j]) if incoming else (ENDS[j], ENDS[n])
            to = device(0, -ENDS[n])
        ref = rows_in.at[place(at), part(n)]
        return gather(4 + group * 8 + j * 4 + 2 + n, ref, ref, to)

    def lanes(r):
        return pl.ds(r * 128, 128)

    def loads():
        sources = [(first, core, 0), (other, 1 - core, 0)]
        sources += [(rest.at[r], core, r + 1) for r in range(3)]
        for n, (src, e, r) in enumerate(sources):
            yield pltpu.make_async_copy(src, weights.at[e, :, :, lanes(r)], load_sems.at[n])
        yield pltpu.make_async_copy(own, rows_in.at[place((0, 0))], load_sems.at[5])

    def swap(r, incoming=False):
        e = 1 - core if incoming else core
        return remote(
            rest.at[r],
            weights.at[e, :, :, lanes(r + 1)],
            w_send.at[r],
            w_recv.at[r],
            plane.partner(),
        )

    for n in (0, 1):
        emit(n).start()
    for r in range(3):
        swap(r).start()
    for n in (0, 1):
        spread(0, 0, n).start()
    for load in loads():
        load.start()
    for j in (0, 1):
        emit(j, True).wait_recv()
        pass_on(j).start()
        for n in (0, 1):
            spread(1, j, n).start()
    for n in (0, 1):
        pass_on(n, True).wait_recv()
    for n in (0, 1):
        spread(0, 1, n).start()
    for load in loads():
        load.wait()
    for r in range(3):
        swap(r, True).wait_recv()

    def far(group, j):
        return (TWO[j], 2) if group == 0 else (2, ENDS[j])

    def near(group, j, side):
        return (ENDS[side], TWO[j]) if group == 0 else (ENDS[j], ENDS[side])

    def line(group, along_first):
        return (lambda d: device(d, 0)) if (group == 0) == along_first else (lambda d: device(0, d))

    def give_far(group, j, n):
        k = group * 4 + j * 2 + n
        return remote(
            sums.at[place(far(group, j)), part(n)],
            hold_q.at[k],
            q_send.at[k],
            q_recv.at[k],
            line(group, False)(ENDS[n]),
        )

    def give_near(group, j, side, late):
        k = group * 4 + j * 2 + side
        span = part(side if late else 1 - side)
        return remote(
            sums.at[place(near(group, j, side)), span],
            hold_r.at[k, span],
            r_send.at[2 * k + late],
            r_recv.at[2 * k + late],
            line(group, True)(ENDS[side]),
        )

    def give_across(n):
        return remote(
            sums.at[place((2, 0)), part(n)],
            hold_p.at[n],
            p_send.at[n],
            p_recv.at[n],
            device(ENDS[n], 0),
        )

    def give_back(side, late):
        span = part(side if late else 1 - side)
        return remote(
            sums.at[place((0, ENDS[side])), span],
            hold_d.at[side, span],
            d_send.at[2 * side + late],
            d_recv.at[2 * side + late],
            device(0, ENDS[side]),
        )

    PAIRS = [(group, j) for j in (0, 1) for group in (0, 1)]
    slot = lax.broadcasted_iota(jnp.int32, (SLOTS, rows), 0).astype(jnp.float32)

    def group_step(g, carry):
        for when, j in ((1, 0), (2, 1)):

            @pl.when(g == when)
            def _():
                for n in (0, 1):
                    for group in (0, 1):
                        spread(group, j, n, True).wait_recv()
                        relay(group, j, n).start()

        @pl.when(g == 3)
        def _():
            for group, j in PAIRS:
                for n in (0, 1):
                    relay(group, j, n, True).wait_recv()
            for group, j in PAIRS:
                for side in (0, 1):
                    give_near(group, j, side, 0).start()

        ids = []
        for j in range(BLOCKS):
            at = place(GROUPS[3][j])
            for k in range(3):
                at = jnp.where(g == k, place(GROUPS[k][j]), at)
            ids.append(at)

        def hits(j, e):
            return tables[ids[j], 2 + e : 3 + e, :] == slot

        def choice(j):
            both = jnp.concatenate([hits(j, 0), hits(j, 1)], axis=0)
            return jnp.where(both, 1.0, 0.0).astype(jnp.bfloat16)

        for j in range(BLOCKS):
            picked[j] = jnp.dot(
                choice(j), rows_in[ids[j]], preferred_element_type=jnp.float32
            ).astype(jnp.bfloat16)
        for e in (0, 1):
            chosen = picked[:, e * SLOTS : (e + 1) * SLOTS, :].reshape(BLOCKS * SLOTS, width)
            gate = jnp.dot(chosen, weights[e, 0], preferred_element_type=jnp.float32)
            up = jnp.dot(chosen, weights[e, 1], preferred_element_type=jnp.float32)
            units = (gate / (1.0 + jnp.exp(-gate)) * up).astype(jnp.bfloat16)
            result = lax.dot_general(
                units, weights[e, 2], (((1,), (1,)), ((), ())), preferred_element_type=jnp.float32
            )
            for j in range(BLOCKS):
                gain = jnp.sum(
                    jnp.where(hits(j, e), tables[ids[j], e : e + 1, :], 0.0),
                    axis=1,
                    keepdims=True,
                )
                made[j, e * SLOTS : (e + 1) * SLOTS, :] = (
                    result[j * SLOTS : (j + 1) * SLOTS, :] * gain
                ).astype(jnp.bfloat16)
        for j in range(BLOCKS):
            sums[ids[j]] = lax.dot_general(
                choice(j), made[j], (((0,), (0,)), ((), ())), preferred_element_type=jnp.float32
            ).astype(jnp.bfloat16)
        return carry

    lax.fori_loop(0, len(GROUPS), group_step, 0)

    for group, j in PAIRS:
        for n in (0, 1):
            give_far(group, j, n).start()

    def add(at, held):
        sums[at] = (sums[at].astype(jnp.float32) + held.astype(jnp.float32)).astype(jnp.bfloat16)

    for group, j in PAIRS:
        for side in (0, 1):
            k = group * 4 + j * 2 + side
            give_far(group, j, side).wait_recv()
            add((place(near(group, j, side)), part(side)), hold_q[k])
            give_near(group, j, side, 1).start()

    def total(group, j):
        for side in (0, 1):
            for late in (0, 1):
                give_near(group, j, side, late).wait_recv()
        at = place((TWO[j], 0) if group == 0 else (0, ENDS[j]))
        k = group * 4 + j * 2
        return at, (
            sums[at].astype(jnp.float32)
            + hold_r[k].astype(jnp.float32)
            + hold_r[k + 1].astype(jnp.float32)
        )

    at, value = total(0, 1)
    sums[at] = value.astype(jnp.bfloat16)
    for n in (0, 1):
        give_across(n).start()
    for side in (0, 1):
        at, value = total(1, side)
        sums[at] = value.astype(jnp.bfloat16)
        give_back(side, 0).start()
    _, value = total(0, 0)
    out_sum = value + residual[...]
    for side in (0, 1):
        give_across(side).wait_recv()
        add((place((0, ENDS[side])), part(side)), hold_p[side])
        give_back(side, 1).start()
    for side in (0, 1):
        for late in (0, 1):
            give_back(side, late).wait_recv()
    out[...] = (
        out_sum + hold_d[0].astype(jnp.float32) + hold_d[1].astype(jnp.float32)
    ).astype(out.dtype)

    for n in (0, 1):
        emit(n).wait_send()
        pass_on(n).wait_send()
        give_across(n).wait_send()
        for late in (0, 1):
            give_back(n, late).wait_send()
    for r in range(3):
        swap(r).wait_send()
    for group, j in PAIRS:
        for n in (0, 1):
            spread(group, j, n).wait_send()
            relay(group, j, n).wait_send()
            give_far(group, j, n).wait_send()
            for late in (0, 1):
                give_near(group, j, n, late).wait_send()


def run_experts(block, residual, tables, weights, collective_id):
    rows, width = block.shape
    dma = pltpu.SemaphoreType.DMA
    vmem = pl.BlockSpec(memory_space=pltpu.VMEM)
    pairs = [dma((n,)) for n in (20, 8, 16, 2, 4, 3) for _ in (0, 1)]
    return pl.pallas_call(
        experts_kernel,
        out_shape=jax.ShapeDtypeStruct(block.shape, block.dtype),
        in_specs=[vmem] * 3 + [pl.BlockSpec(memory_space=pl.ANY)] * 3,
        out_specs=vmem,
        scratch_shapes=[
            pltpu.VMEM((CHIPS, rows, width), jnp.bfloat16),
            pltpu.VMEM((CHIPS, rows, width), jnp.bfloat16),
            pltpu.VMEM((2, 3, width, FF), jnp.bfloat16),
            pltpu.VMEM((BLOCKS, 2 * SLOTS, width), jnp.bfloat16),
            pltpu.VMEM((BLOCKS, 2 * SLOTS, width), jnp.bfloat16),
            pltpu.VMEM((8, rows // 2, width), jnp.bfloat16),
            pltpu.VMEM((8, rows, width), jnp.bfloat16),
            pltpu.VMEM((2, rows // 2, width), jnp.bfloat16),
            pltpu.VMEM((2, rows, width), jnp.bfloat16),
            *pairs,
            dma((6,)),
        ],
        compiler_params=pltpu.CompilerParams(
            collective_id=collective_id, has_side_effects=True, vmem_limit_bytes=60 << 20
        ),
        name="experts",
    )(block, residual, tables, *weights)


def slot_tables(routes, route_weights):
    tokens = routes.shape[0]
    hit = routes[None] == jnp.arange(EXPERTS, dtype=jnp.int32)[:, None, None]
    gains = jnp.sum(jnp.where(hit, route_weights[None], 0.0), axis=2)
    named = jnp.any(hit, axis=2)
    earlier = jnp.triu(jnp.ones((tokens, tokens), jnp.bfloat16), 1)
    ranks = jnp.dot(named.astype(jnp.bfloat16), earlier, preferred_element_type=jnp.float32)
    ranks = jnp.where(named, ranks, -1.0)
    pairs = [t.reshape(CHIPS, 2, tokens) for t in (gains, ranks)]
    return jnp.concatenate(pairs + [jnp.zeros((CHIPS, 4, tokens), jnp.float32)], axis=1)


def shards(
    hidden,
    attn_gain,
    query_weight,
    key_matrix,
    value_matrix,
    output_weight,
    prompt_start,
    ffn_gain,
    routes,
    route_weights,
    expert_weights,
):
    total_row_count = hidden.shape[0]
    lane_index = lax.axis_index("exp")
    positions = lane_index * total_row_count + jnp.arange(total_row_count, dtype=jnp.int32)
    stream_offsets = positions - prompt_start
    inputs = hidden.astype(jnp.float32)
    normalized_input = rms_norm(inputs, attn_gain).astype(jnp.bfloat16)
    query_rows_all = jnp.dot(
        normalized_input, query_weight, preferred_element_type=jnp.float32
    ).reshape(total_row_count, QUERY_HEADS, HEAD_SIZE)
    query_rows_all = (
        rotary_embedding(query_rows_all, stream_offsets)
        .astype(jnp.bfloat16)
        .reshape(total_row_count, QUERY_HEADS * HEAD_SIZE)
    )
    shard_keys = jnp.dot(normalized_input, key_matrix, preferred_element_type=jnp.float32).reshape(
        total_row_count, KEY_VALUE_HEADS, HEAD_SIZE
    )
    shard_keys = (
        rotary_embedding(shard_keys, stream_offsets)
        .astype(jnp.bfloat16)
        .reshape(total_row_count, KEY_VALUE_HEADS * HEAD_SIZE)
    )
    values_local = jnp.dot(
        normalized_input, value_matrix, preferred_element_type=jnp.float32
    ).astype(jnp.bfloat16)
    pairs = jnp.concatenate(
        [
            side[:, p * 128 : (p + 1) * 128]
            for p in range(KEY_VALUE_HEADS // 2)
            for side in (shard_keys, values_local)
        ],
        axis=1,
    )
    starts = jnp.broadcast_to(prompt_start.astype(jnp.float32)[None], (8, total_row_count))
    own = expert_weights[0]
    attention, tables, own_rest, other = attend(
        query_rows_all, pairs, starts, slot_tables(routes, route_weights), own, 0
    )
    residual = inputs + jnp.dot(attention, output_weight, preferred_element_type=jnp.float32)
    moe_in = rms_norm(residual, ffn_gain).astype(jnp.bfloat16)

    layer_out = run_experts(moe_in, residual, tables, (own, own_rest, other), 1)
    return (layer_out, shard_keys, values_local)


def solution(mesh):
    in_specs = (
        P(("req", "exp"), None),
        P(),
        P(),
        P(),
        P(),
        P(),
        P(("req", "exp")),
        P(),
        P(("req", "exp"), None),
        P(("req", "exp"), None),
        P("exp", None, None, "req"),
    )
    out_specs = (P(("req", "exp"), None), P(("req", "exp"), None), P(("req", "exp"), None))
    return jax.shard_map(shards, mesh=mesh, in_specs=in_specs, out_specs=out_specs, check_vma=False)
```

```python
import jax
import jax.numpy as jnp
from jax import lax
from jax.experimental import pallas as pl
from jax.experimental.pallas import tpu as pltpu
from jax.sharding import PartitionSpec as P

QUERY_HEADS = 24
KEY_VALUE_HEADS = 8
HEAD_SIZE = 64
TOP = 8
SIDE = 4
CHIPS = SIDE * SIDE
EXPERTS = 32
SLOTS = 64
FF = 512


epsilon = 1e-05


class Plane:
    def __init__(self):
        me = lax.axis_index("exp")
        self.core = lax.rem(me, 2)
        chip = lax.div(me, 2)
        self.y = lax.div(chip, SIDE)
        self.x = lax.rem(chip, SIDE)

    def chip(self, dy, dx):
        return lax.rem(self.y + dy + SIDE, SIDE) * SIDE + lax.rem(self.x + dx + SIDE, SIDE)

    def device(self, dy, dx):
        return {"exp": self.chip(dy, dx) * 2 + self.core}

    def level(self, dz):
        return {"req": lax.rem(lax.axis_index("req") + dz + SIDE, SIDE)}

    def partner(self):
        return {"exp": self.chip(0, 0) * 2 + 1 - self.core}

    def mirror(self, same_core):
        core = self.core if same_core else 1 - self.core
        return {"exp": (CHIPS - 1 - self.chip(0, 0)) * 2 + core}


OTHERS = tuple((dy, dx) for dy in range(SIDE) for dx in range(SIDE) if dy or dx)


def greet(plane):
    barrier = pltpu.get_barrier_semaphore()
    devices = [plane.device(dy, dx) for dy, dx in OTHERS]
    devices += [plane.partner(), plane.mirror(False), plane.level(1), plane.level(-1)]
    for device in devices:
        pl.semaphore_signal(
            barrier, inc=1, device_id=device, device_id_type=pl.DeviceIdType.MESH
        )
    return lambda: pl.semaphore_wait(barrier, len(devices))


def remote(src, dst, send, recv, device):
    return pltpu.make_async_remote_copy(
        src_ref=src,
        dst_ref=dst,
        send_sem=send,
        recv_sem=recv,
        device_id=device,
        device_id_type=pl.DeviceIdType.MESH,
    )


KEYS = 512
PAIR = 6
PAIR_WIDTH = PAIR * HEAD_SIZE
LOW = -1e30
SCALE = HEAD_SIZE**-0.5 * 1.4426950408889634
ACROSS = (0, -1, 1, 2)


def attention_section(
    plane, weight_copy, project_keys, project_queries, make_tables,
    queries, pairs, starts, given, out, held,
    near, store, asked, begin, packed, peak, total, bias, done,
    give, take, x_send, x_recv, y_send, y_recv, q_send, q_recv, o_send, o_recv, sems,
):
    core, odd = plane.core, lax.rem(plane.x, 2)
    here = plane.chip(0, 0)
    rows = queries.shape[0]
    friends = [plane.partner(), plane.mirror(True), plane.mirror(False)]

    mine = 2 * core + odd
    theirs = [2 * (1 - core) + odd, 2 * core + 1 - odd, 2 * (1 - core) + 1 - odd]
    slots = [core, 2 + core, 2 + core]
    from_slots = [1 - core, 2 + core, 2 + 1 - core]

    def lanes(at, size):
        return pl.ds(pl.multiple_of(at * size, size), size)

    swap = remote(
        pairs.at[:, lanes(1 - core, 512)], near, sems.at[0], sems.at[1], friends[0]
    )

    def source(h, parity):
        if h == 0:
            return pairs.at[:, lanes(2 * core + parity, 256)]
        return near.at[:, lanes(parity, 256)]

    def slot(h, dy, dx, part=None):
        low = (core if h == 0 else 1 - core) * rows
        size = rows
        if part is not None:
            size = rows // 2
            low = low + part * size
        return store.at[plane.chip(dy, dx), pl.ds(pl.multiple_of(low, size), size)]

    def keep(h):
        return pltpu.make_async_copy(source(h, odd), slot(h, 0, 0), sems.at[2 + h])

    def across(h, n, incoming=False):
        dx = (1, -1, 2)[n]
        return remote(
            source(h, odd if n == 2 else 1 - odd),
            slot(h, 0, -dx if incoming else 0),
            x_send.at[3 * h + n],
            x_recv.at[3 * h + n],
            plane.device(0, dx),
        )

    def along(h, i, n, incoming=False):
        dx = ACROSS[i]
        at, part, dy = ((0, None, 1), (0, None, -1), (-1, 0, 1), (1, 1, -1))[n]
        place = slot(h, at - dy if incoming else at, dx, part)
        src = source(h, odd) if (i == 0 and n < 2) else place
        if i == 0 and n < 2 and not incoming:
            place = slot(h, 0, 0)
        k = (h * 4 + i) * 4 + n
        return remote(src, place, y_send.at[k], y_recv.at[k], plane.device(dy, 0))

    def ask(n, incoming=False):
        at = from_slots[n] if incoming else slots[n]
        return remote(
            queries.at[:, lanes(theirs[n], PAIR_WIDTH)],
            asked.at[at],
            q_send.at[n],
            q_recv.at[n],
            friends[n],
        )

    def tell(n, incoming=False):
        at = from_slots[n] if incoming else slots[n]
        return remote(starts, begin.at[at], q_send.at[3 + n], q_recv.at[3 + n], friends[n])

    def table(n, incoming=False):
        dy, dx = OTHERS[n]
        return remote(
            given.at[plane.chip(dy, dx)],
            held.at[plane.chip(-dy, -dx) if incoming else here],
            give.at[n],
            take.at[n],
            plane.device(dy, dx),
        )

    own_asked = pltpu.make_async_copy(
        queries.at[:, lanes(mine, PAIR_WIDTH)], asked.at[core], sems.at[4]
    )
    own_begin = pltpu.make_async_copy(starts, begin.at[core], sems.at[5])
    own_table = pltpu.make_async_copy(given.at[here], held.at[here], sems.at[6])

    project_keys()
    swap.start()
    for h in (0, 1):
        if h == 1:
            make_tables()
            own_begin.start()
            own_table.start()
            swap.wait_recv()
        keep(h).start()
        for n in range(3):
            across(h, n).start()
        along(h, 0, 0).start()
        along(h, 0, 1).start()
    project_queries()
    own_asked.start()
    ask(0).start()
    tell(0).start()
    for n in (1, 2):
        ask(n).start()
        tell(n).start()
    for n in range(3):
        i = (1, 2, 3)[n]
        for h in (0, 1):
            across(h, n, True).wait_recv()
            along(h, i, 0).start()
            along(h, i, 1).start()
    for n in range(len(OTHERS)):
        table(n).start()

    own_asked.wait()
    own_begin.wait()
    for n in range(3):
        ask(n, True).wait_recv()
        tell(n, True).wait_recv()
    for h in (0, 1):
        keep(h).wait()

    lane = lax.broadcasted_iota(jnp.int32, (rows, 128), 1)
    low_half = lane < HEAD_SIZE
    for which in (0, 1):
        for side in (0, 1):
            for n in range(PAIR):
                tile = asked[2 * which + side, :, (n // 2) * 128 : (n // 2 + 1) * 128].astype(
                    jnp.float32
                )
                group = n // 3
                if n % 2 != group:
                    tile = pltpu.roll(tile, HEAD_SIZE, axis=1)
                own_half = low_half if group == 0 else jnp.logical_not(low_half)
                at = (n * 2 + side) * rows
                packed[which, at : at + rows, :] = jnp.where(own_half, tile, 0.0).astype(
                    jnp.bfloat16
                )
    peak[...] = jnp.full_like(peak, LOW)
    total[...] = jnp.zeros_like(total)
    half = PAIR * rows

    def visit(which, chip):
        stream_chip = jnp.where(which == 0, here, CHIPS - 1 - here)
        at = chip * (2 * rows)
        for side in (0, 1):
            first = jnp.broadcast_to(begin[2 * which + side, 0:1, :], (rows, rows)).T
            first = jnp.concatenate([first] * (KEYS // rows), axis=1).astype(jnp.int32)
            key_pos = at + lax.broadcasted_iota(jnp.int32, (rows, KEYS), 1)
            own_pos = (2 * stream_chip + side) * rows + lax.broadcasted_iota(
                jnp.int32, (rows, KEYS), 0
            )
            bias[side * rows : (side + 1) * rows, :] = jnp.where(
                (key_pos >= first) & (key_pos <= own_pos), 0.0, LOW
            )
        tile = store[pl.ds(chip, 2)].reshape(KEYS, 256)
        key, value = tile[:, :128], tile[:, 128:]
        key_lane = lax.broadcasted_iota(jnp.int32, (KEYS, 128), 1)
        for group in (0, 1):
            span = pl.ds(group * half, half)
            scores = lax.dot_general(
                packed[which, span, :],
                key,
                (((1,), (1,)), ((), ())),
                preferred_element_type=jnp.float32,
            )
            scores = (scores.reshape(PAIR // 2, 2 * rows, KEYS) + bias[...][None]).reshape(
                half, KEYS
            )
            before = peak[which, span, :]
            now = jnp.maximum(before, jnp.max(scores, axis=1, keepdims=True))
            peak[which, span, :] = now
            fade = jnp.exp2((before - now) * SCALE)
            wide = jnp.concatenate([now] * (KEYS // 128), axis=1)
            probs = jnp.exp2((scores - wide) * SCALE).astype(jnp.bfloat16)
            own_half = (key_lane < HEAD_SIZE) == (group == 0)
            beside = jnp.where(own_half, value, jnp.ones_like(value))
            total[which, span, :] = total[which, span, :] * fade + jnp.dot(
                probs, beside, preferred_element_type=jnp.float32
            )

    def phase(step, carry):
        @pl.when(step == 1)
        def _():
            for i in range(4):
                for n in (0, 1):
                    for h in (0, 1):
                        along(h, i, n, True).wait_recv()
                        along(h, i, n + 2).start()

        @pl.when(step == 2)
        def _():
            for n in (0, 1):
                weight_copy(n, True).wait_recv()
                weight_copy(2 + n).start()
                weight_copy(5 + n).start()

        @pl.when(step == 3)
        def _():
            for i in range(4):
                for n in (2, 3):
                    for h in (0, 1):
                        along(h, i, n, True).wait_recv()

        dy = jnp.where(step == 0, 0, jnp.where(step == 1, SIDE - 1, step - 1))
        dy = jnp.where(step == 3, 2, dy)
        row = lax.rem(plane.y + dy, SIDE) * SIDE

        def one(t, carry):
            which = lax.div(t, 2)
            chip = row + 2 * lax.rem(t, 2)
            limit = jnp.where(which == 0, here, CHIPS - 1 - here)

            @pl.when(chip <= limit)
            def _():
                visit(which, chip)

            return carry

        return lax.fori_loop(0, 4, one, carry)

    lax.fori_loop(0, 4, phase, 0)

    def answer(which, side):
        def head(n):
            at = (n * 2 + side) * rows
            sums = total[which, at : at + rows, :]
            result = sums / pltpu.roll(sums, HEAD_SIZE, axis=1)
            if n % 2 != n // 3:
                result = pltpu.roll(result, HEAD_SIZE, axis=1)
            return result

        return [
            jnp.where(low_half, head(2 * i), head(2 * i + 1)).astype(out.dtype)
            for i in range(PAIR // 2)
        ]

    for which in (1, 0):
        for side in (0, 1):
            for i, piece in enumerate(answer(which, side)):
                done[2 * which + side, :, i * 128 : (i + 1) * 128] = piece

    def reply(n, incoming=False):
        return remote(
            done.at[from_slots[n]],
            out.at[:, lanes(theirs[n] if incoming else mine, PAIR_WIDTH)],
            o_send.at[n],
            o_recv.at[n],
            friends[n],
        )

    for n in (1, 2, 0):
        reply(n).start()
    own_reply = pltpu.make_async_copy(
        done.at[core], out.at[:, lanes(mine, PAIR_WIDTH)], sems.at[7]
    )
    own_reply.start()

    swap.wait_send()
    own_table.wait()
    for h in (0, 1):
        for n in range(3):
            across(h, n).wait_send()
        for i in range(4):
            for n in range(4):
                along(h, i, n).wait_send()
    for n in range(3):
        ask(n).wait_send()
        tell(n).wait_send()
    for n in range(len(OTHERS)):
        table(n, True).wait_recv()
        table(n).wait_send()
    own_reply.wait()
    for n in range(3):
        reply(n, True).wait_recv()
        reply(n).wait_send()


BLOCKS = 4
GROUPS = (
    ((0, 0), (2, 0), (0, -1), (0, 1)),
    ((-1, 0), (1, 0), (-1, -1), (-1, 1)),
    ((-1, 2), (1, 2), (1, -1), (1, 1)),
    ((0, 2), (2, 2), (2, -1), (2, 1)),
)
TWO = (0, 2)
ENDS = (-1, 1)


def experts_section(
    plane, weight_copy, own, residual, tables, out,
    rows_in, sums, weights, picked, made, hold_q, hold_r, hold_p, hold_d,
    g_send, g_recv, q_send, q_recv, r_send, r_recv, p_send, p_recv, d_send, d_recv, sem,
):
    rows, width = own.shape
    part_rows = rows // 2
    even = lax.rem(plane.y + plane.x, 2) == 0

    def turned(o, t):
        return jnp.where(even, t, o), jnp.where(even, o, t)

    def place(at):
        return plane.chip(*turned(*at))

    def device(o, t):
        return plane.device(*turned(o, t))

    def part(n):
        return pl.ds(n * part_rows, part_rows)

    def gather(k, src, dst, to):
        return remote(src, dst, g_send.at[k], g_recv.at[k], to)

    def emit(n, incoming=False):
        d = (1, -1)[n]
        at = (0, -d) if incoming else (0, 0)
        return gather(n, own, rows_in.at[place(at)], device(d, 0))

    def pass_on(n, incoming=False):
        at = (2, 0) if incoming else (0, ENDS[n])
        ref = rows_in.at[place(at), part(n)]
        return gather(2 + n, ref, ref, device(0, -ENDS[n]))

    def spread(group, j, n, incoming=False):
        d = (1, -1)[n]
        if group == 0:
            at = (-d, TWO[j]) if incoming else (TWO[j], 0)
            to = device(0, d)
        else:
            at = (ENDS[j], -d) if incoming else (0, ENDS[j])
            to = device(d, 0)
        ref = rows_in.at[place(at)]
        src = own if at == (0, 0) else ref
        return gather(4 + group * 8 + j * 4 + n, src, ref, to)

    def relay(group, j, n, incoming=False):
        if group == 0:
            at = (TWO[j], 2) if incoming else (ENDS[n], TWO[j])
            to = device(-ENDS[n], 0)
        else:
            at = (2, ENDS[j]) if incoming else (ENDS[j], ENDS[n])
            to = device(0, -ENDS[n])
        ref = rows_in.at[place(at), part(n)]
        return gather(4 + group * 8 + j * 4 + 2 + n, ref, ref, to)

    mine = pltpu.make_async_copy(own, rows_in.at[place((0, 0))], sem)
    for n in (0, 1):
        emit(n).start()
    for n in (0, 1):
        spread(0, 0, n).start()
    mine.start()
    for n in (2, 3):
        weight_copy(n, True).wait_recv()
    weight_copy(7).start()
    for j in (0, 1):
        emit(j, True).wait_recv()
        pass_on(j).start()
        for n in (0, 1):
            spread(1, j, n).start()
    for n in (0, 1):
        pass_on(n, True).wait_recv()
    for n in (0, 1):
        spread(0, 1, n).start()
    mine.wait()
    for n in (4, 5, 6, 7):
        weight_copy(n, True).wait_recv()

    def far(group, j):
        return (TWO[j], 2) if group == 0 else (2, ENDS[j])

    def near(group, j, side):
        return (ENDS[side], TWO[j]) if group == 0 else (ENDS[j], ENDS[side])

    def line(group, along_first):
        return (lambda d: device(d, 0)) if (group == 0) == along_first else (lambda d: device(0, d))

    def give_far(group, j, n):
        k = group * 4 + j * 2 + n
        return remote(
            sums.at[place(far(group, j)), part(n)],
            hold_q.at[k],
            q_send.at[k],
            q_recv.at[k],
            line(group, False)(ENDS[n]),
        )

    def give_near(group, j, side, late):
        k = group * 4 + j * 2 + side
        span = part(side if late else 1 - side)
        return remote(
            sums.at[place(near(group, j, side)), span],
            hold_r.at[k, span],
            r_send.at[2 * k + late],
            r_recv.at[2 * k + late],
            line(group, True)(ENDS[side]),
        )

    def give_across(n):
        return remote(
            sums.at[place((2, 0)), part(n)],
            hold_p.at[n],
            p_send.at[n],
            p_recv.at[n],
            device(ENDS[n], 0),
        )

    def give_back(side, late):
        span = part(side if late else 1 - side)
        return remote(
            sums.at[place((0, ENDS[side])), span],
            hold_d.at[side, span],
            d_send.at[2 * side + late],
            d_recv.at[2 * side + late],
            device(0, ENDS[side]),
        )

    PAIRS = [(group, j) for j in (0, 1) for group in (0, 1)]
    slot = lax.broadcasted_iota(jnp.int32, (SLOTS, rows), 0).astype(jnp.float32)

    def group_step(g, carry):
        for when, j in ((1, 0), (2, 1)):

            @pl.when(g == when)
            def _():
                for n in (0, 1):
                    for group in (0, 1):
                        spread(group, j, n, True).wait_recv()
                        relay(group, j, n).start()

        @pl.when(g == 3)
        def _():
            for group, j in PAIRS:
                for n in (0, 1):
                    relay(group, j, n, True).wait_recv()
            for group, j in PAIRS:
                for side in (0, 1):
                    give_near(group, j, side, 0).start()

        ids = []
        for j in range(BLOCKS):
            at = place(GROUPS[3][j])
            for k in range(3):
                at = jnp.where(g == k, place(GROUPS[k][j]), at)
            ids.append(at)

        def hits(j, e):
            return tables[ids[j], 2 + e : 3 + e, :] == slot

        def choice(j):
            both = jnp.concatenate([hits(j, 0), hits(j, 1)], axis=0)
            return jnp.where(both, 1.0, 0.0).astype(jnp.bfloat16)

        for j in range(BLOCKS):
            picked[j] = jnp.dot(
                choice(j), rows_in[ids[j]], preferred_element_type=jnp.float32
            ).astype(jnp.bfloat16)
        for e in (0, 1):
            chosen = picked[:, e * SLOTS : (e + 1) * SLOTS, :].reshape(BLOCKS * SLOTS, width)
            gate = jnp.dot(chosen, weights[e, 0], preferred_element_type=jnp.float32)
            up = jnp.dot(chosen, weights[e, 1], preferred_element_type=jnp.float32)
            units = (gate / (1.0 + jnp.exp(-gate)) * up).astype(jnp.bfloat16)
            result = lax.dot_general(
                units, weights[e, 2], (((1,), (1,)), ((), ())), preferred_element_type=jnp.float32
            )
            for j in range(BLOCKS):
                gain = jnp.sum(
                    jnp.where(hits(j, e), tables[ids[j], e : e + 1, :], 0.0),
                    axis=1,
                    keepdims=True,
                )
                made[j, e * SLOTS : (e + 1) * SLOTS, :] = (
                    result[j * SLOTS : (j + 1) * SLOTS, :] * gain
                ).astype(jnp.bfloat16)
        for j in range(BLOCKS):
            sums[ids[j]] = lax.dot_general(
                choice(j), made[j], (((0,), (0,)), ((), ())), preferred_element_type=jnp.float32
            ).astype(jnp.bfloat16)
        return carry

    lax.fori_loop(0, len(GROUPS), group_step, 0)

    for group, j in PAIRS:
        for n in (0, 1):
            give_far(group, j, n).start()

    def add(at, held):
        sums[at] = (sums[at].astype(jnp.float32) + held.astype(jnp.float32)).astype(jnp.bfloat16)

    for group, j in PAIRS:
        for side in (0, 1):
            k = group * 4 + j * 2 + side
            give_far(group, j, side).wait_recv()
            add((place(near(group, j, side)), part(side)), hold_q[k])
            give_near(group, j, side, 1).start()

    def total(group, j):
        for side in (0, 1):
            for late in (0, 1):
                give_near(group, j, side, late).wait_recv()
        at = place((TWO[j], 0) if group == 0 else (0, ENDS[j]))
        k = group * 4 + j * 2
        return at, (
            sums[at].astype(jnp.float32)
            + hold_r[k].astype(jnp.float32)
            + hold_r[k + 1].astype(jnp.float32)
        )

    at, value = total(0, 1)
    sums[at] = value.astype(jnp.bfloat16)
    for n in (0, 1):
        give_across(n).start()
    for side in (0, 1):
        at, value = total(1, side)
        sums[at] = value.astype(jnp.bfloat16)
        give_back(side, 0).start()
    _, value = total(0, 0)
    out_sum = value + residual[...]
    for side in (0, 1):
        give_across(side).wait_recv()
        add((place((0, ENDS[side])), part(side)), hold_p[side])
        give_back(side, 1).start()
    for side in (0, 1):
        for late in (0, 1):
            give_back(side, late).wait_recv()
    out[...] = (
        out_sum + hold_d[0].astype(jnp.float32) + hold_d[1].astype(jnp.float32)
    ).astype(out.dtype)

    for n in (0, 1):
        emit(n).wait_send()
        pass_on(n).wait_send()
        give_across(n).wait_send()
        for late in (0, 1):
            give_back(n, late).wait_send()
    for n in range(8):
        weight_copy(n).wait_send()
    for group, j in PAIRS:
        for n in (0, 1):
            spread(group, j, n).wait_send()
            relay(group, j, n).wait_send()
            give_far(group, j, n).wait_send()
            for late in (0, 1):
                give_near(group, j, n, late).wait_send()


def normed(values, gain):
    mean_square = jnp.mean(values * values, axis=1, keepdims=True)
    return (values * lax.rsqrt(mean_square + epsilon) * gain).astype(jnp.bfloat16)


def layer_kernel(
    hidden, attn_gain, wq, wk, wv, wo, prompt_start, cosine, sine, ffn_gain, routes, route_weights,
    first,
    out, key_cache, value_cache,
    query_w, key_w, value_w, output_w, own_in, residual,
    queries, pairs, starts, given, attention, tables,
    near, store, asked, begin, packed, peak, total, bias, done,
    rows_in, sums, weights, picked, made, hold_q, hold_r, hold_p, hold_d,
    *sems,
):
    attention_sems, expert_sems, (w_send, w_recv, load_sems, row_sem) = (
        sems[:11],
        sems[11:21],
        sems[21:],
    )
    plane = Plane()
    core = plane.core
    rows, width = hidden.shape
    arrived = greet(plane)

    def lanes(r):
        return pl.ds(r * 128, 128)

    def weight_copy(n, incoming=False):
        half = width // 2
        e = 1 - core if incoming and n >= 4 else core
        if n < 2:
            src, dst = first, weights.at[e, :, :, lanes(1 + n)]
            to = plane.level((1, -1)[n])
        elif n < 4:
            span = pl.ds((n - 2) * half, half)
            src = weights.at[e, :, span, lanes(n - 1)]
            dst = weights.at[e, :, span, lanes(3)]
            to = plane.level((1, -1)[n - 2])
        else:
            dst = weights.at[e, :, :, lanes(n - 4)]
            src = first if n == 4 else dst
            to = plane.partner()
        return remote(src, dst, w_send.at[n], w_recv.at[n], to)

    loads = [
        pltpu.make_async_copy(src, dst, load_sems.at[n])
        for n, (src, dst) in enumerate(
            (
                (wk, key_w),
                (wv, value_w),
                (wq, query_w),
                (wo, output_w),
                (first, weights.at[core, :, :, lanes(0)]),
            )
        )
    ]
    for load in loads:
        load.start()
    own_in[...] = normed(hidden[...].astype(jnp.float32), attn_gain[...])
    arrived()
    for n in (0, 1, 4):
        weight_copy(n).start()

    lane = lax.broadcasted_iota(jnp.int32, (rows, 128), 1)
    first_half = lax.rem(lane, HEAD_SIZE) < HEAD_SIZE // 2

    def rotated(tile):
        other = jnp.where(
            first_half,
            pltpu.roll(tile, 128 - HEAD_SIZE // 2, axis=1),
            pltpu.roll(tile, HEAD_SIZE // 2, axis=1),
        )
        return (tile * cosine[...] + other * sine[...]).astype(jnp.bfloat16)

    def project_keys():
        starts[...] = jnp.broadcast_to(prompt_start[...].astype(jnp.float32), starts.shape)
        loads[0].wait()
        keys = jnp.dot(own_in[...], key_w[...], preferred_element_type=jnp.float32)
        loads[1].wait()
        values = jnp.dot(
            own_in[...], value_w[...], preferred_element_type=jnp.float32
        ).astype(jnp.bfloat16)
        value_cache[...] = values
        for p in range(KEY_VALUE_HEADS // 2):
            at = slice(p * 128, (p + 1) * 128)
            tile = rotated(keys[:, at])
            key_cache[:, at] = tile
            pairs[:, p * 256 : p * 256 + 128] = tile
            pairs[:, p * 256 + 128 : (p + 1) * 256] = values[:, at]

    def project_queries():
        loads[2].wait()
        for c in range(3):
            part = jnp.dot(
                own_in[...],
                query_w[:, c * 512 : (c + 1) * 512],
                preferred_element_type=jnp.float32,
            )
            for p in range(4):
                at = c * 512 + p * 128
                queries[:, at : at + 128] = rotated(part[:, p * 128 : (p + 1) * 128])

    def make_tables():
        expert = lax.broadcasted_iota(jnp.int32, (EXPERTS, rows), 0)
        gains = jnp.zeros((EXPERTS, rows), jnp.float32)
        named = jnp.zeros((EXPERTS, rows), jnp.float32)
        for j in range(TOP):
            hit = routes[j : j + 1, :] == expert
            gains = gains + jnp.where(hit, route_weights[j : j + 1, :], 0.0)
            named = named + jnp.where(hit, 1.0, 0.0)
        earlier = lax.broadcasted_iota(jnp.int32, (rows, rows), 0) < lax.broadcasted_iota(
            jnp.int32, (rows, rows), 1
        )
        ranks = jnp.dot(
            named.astype(jnp.bfloat16),
            jnp.where(earlier, 1.0, 0.0).astype(jnp.bfloat16),
            preferred_element_type=jnp.float32,
        )
        ranks = jnp.where(named > 0.0, ranks, -1.0)
        given[...] = jnp.zeros_like(given)
        for c in range(CHIPS):
            given[c, 0:2, :] = gains[2 * c : 2 * c + 2, :]
            given[c, 2:4, :] = ranks[2 * c : 2 * c + 2, :]

    attention_section(
        plane, weight_copy, project_keys, project_queries, make_tables,
        queries, pairs, starts, given, attention, tables,
        near, store, asked, begin, packed, peak, total, bias, done,
        *attention_sems,
    )

    loads[3].wait()
    for c in range(3):
        at = slice(c * 512, (c + 1) * 512)
        residual[:, at] = hidden[:, at].astype(jnp.float32) + jnp.dot(
            attention[...], output_w[:, at], preferred_element_type=jnp.float32
        )
    own_in[...] = normed(residual[...], ffn_gain[...])
    loads[4].wait()

    experts_section(
        plane, weight_copy, own_in, residual, tables, out,
        rows_in, sums, weights, picked, made, hold_q, hold_r, hold_p, hold_d,
        *expert_sems, row_sem,
    )


def run_layer(hidden, attn_gain, wq, wk, wv, wo, starts, trig, ffn_gain, routes, gains, first):
    rows, width = hidden.shape
    cache = wk.shape[1]
    dma = pltpu.SemaphoreType.DMA
    vmem = pl.BlockSpec(memory_space=pltpu.VMEM)
    hbm = pl.BlockSpec(memory_space=pl.ANY)

    def brief(*shape):
        return pltpu.VMEM(shape, jnp.bfloat16)

    def full(*shape):
        return pltpu.VMEM(shape, jnp.float32)

    others = len(OTHERS)
    counts = (others, 6, 32, 6, 3)
    attention_sems = [dma((n,)) for n in counts for _ in (0, 1)] + [dma((8,))]
    expert_sems = [dma((n,)) for n in (20, 8, 16, 2, 4) for _ in (0, 1)]
    both = 2 * PAIR * rows
    return pl.pallas_call(
        layer_kernel,
        out_shape=(
            jax.ShapeDtypeStruct((rows, width), jnp.bfloat16),
            jax.ShapeDtypeStruct((rows, cache), jnp.bfloat16),
            jax.ShapeDtypeStruct((rows, cache), jnp.bfloat16),
        ),
        in_specs=[vmem, vmem, hbm, hbm, hbm, hbm] + [vmem] * 6 + [hbm],
        out_specs=(vmem,) * 3,
        scratch_shapes=[
            brief(*wq.shape),
            brief(*wk.shape),
            brief(*wv.shape),
            brief(*wo.shape),
            brief(rows, width),
            full(rows, width),
            brief(rows, width),
            brief(rows, 2 * cache),
            full(8, rows),
            full(CHIPS, 8, rows),
            brief(rows, width),
            full(CHIPS, 8, rows),
            brief(rows, 512),
            brief(CHIPS, 2 * rows, 256),
            brief(4, rows, PAIR_WIDTH),
            full(4, 8, rows),
            brief(2, both, 128),
            full(2, both, 128),
            full(2, both, 128),
            full(2 * rows, KEYS),
            brief(4, rows, PAIR_WIDTH),
            brief(CHIPS, rows, width),
            brief(CHIPS, rows, width),
            brief(2, 3, width, FF),
            brief(BLOCKS, 2 * SLOTS, width),
            brief(BLOCKS, 2 * SLOTS, width),
            brief(8, rows // 2, width),
            brief(8, rows, width),
            brief(2, rows // 2, width),
            brief(2, rows, width),
            *attention_sems,
            *expert_sems,
            dma((8,)),
            dma((8,)),
            dma((5,)),
            dma,
        ],
        compiler_params=pltpu.CompilerParams(
            collective_id=0, has_side_effects=True, vmem_limit_bytes=63 << 20
        ),
        name="layer",
    )(
        hidden, attn_gain, wq, wk, wv, wo, starts, *trig, ffn_gain, routes, gains, first
    )


def rotation_tables(offsets):
    half = HEAD_SIZE // 2
    freqs = 10000.0 ** (-jnp.arange(half, dtype=jnp.float32) / half)
    freqs = jnp.tile(freqs, 128 // half)
    sign = jnp.where(jnp.arange(128) % HEAD_SIZE < half, -1.0, 1.0)
    angle = offsets.astype(jnp.float32)[:, None] * freqs[None, :]
    return jnp.cos(angle), jnp.sin(angle) * sign[None, :]


def shards(
    hidden,
    attn_gain,
    query_weight,
    key_matrix,
    value_matrix,
    output_weight,
    prompt_start,
    ffn_gain,
    routes,
    route_weights,
    expert_weights,
):
    rows = hidden.shape[0]
    positions = lax.axis_index("exp") * rows + jnp.arange(rows, dtype=jnp.int32)
    return run_layer(
        hidden,
        attn_gain[None],
        query_weight,
        key_matrix,
        value_matrix,
        output_weight,
        prompt_start[None],
        rotation_tables(positions - prompt_start),
        ffn_gain[None],
        routes.T,
        route_weights.T,
        expert_weights[0],
    )


def solution(mesh):
    in_specs = (
        P(("req", "exp"), None),
        P(),
        P(),
        P(),
        P(),
        P(),
        P(("req", "exp")),
        P(),
        P(("req", "exp"), None),
        P(("req", "exp"), None),
        P("exp", None, None, "req"),
    )
    out_specs = (P(("req", "exp"), None), P(("req", "exp"), None), P(("req", "exp"), None))
    return jax.shard_map(shards, mesh=mesh, in_specs=in_specs, out_specs=out_specs, check_vma=False)
```

```python
import jax
import jax.numpy as jnp
from jax import lax
from jax.experimental import pallas as pl
from jax.experimental.pallas import tpu as pltpu
from jax.sharding import PartitionSpec as P

QUERY_HEADS = 24
KEY_VALUE_HEADS = 8
HEAD_SIZE = 64
TOP = 8
SIDE = 4
CHIPS = SIDE * SIDE
EXPERTS = 32
SLOTS = 64
FF = 512


epsilon = 1e-05


class Plane:
    def __init__(self):
        me = lax.axis_index("exp")
        self.core = lax.rem(me, 2)
        chip = lax.div(me, 2)
        self.y = lax.div(chip, SIDE)
        self.x = lax.rem(chip, SIDE)

    def chip(self, dy, dx):
        return lax.rem(self.y + dy + SIDE, SIDE) * SIDE + lax.rem(self.x + dx + SIDE, SIDE)

    def device(self, dy, dx):
        return {"exp": self.chip(dy, dx) * 2 + self.core}

    def level(self, dz):
        return {"req": lax.rem(lax.axis_index("req") + dz + SIDE, SIDE)}

    def partner(self):
        return {"exp": self.chip(0, 0) * 2 + 1 - self.core}

    def friend(self, dx, dc):
        x = lax.rem(self.x + dx + SIDE, SIDE)
        y = self.y if dx % 2 == 0 else SIDE - 1 - self.y
        core = 1 - self.core if dc else self.core
        return y * SIDE + x, core, 2 * x + core

    def friend_device(self, dx, dc):
        chip, core, _ = self.friend(dx, dc)
        return {"exp": chip * 2 + core}


FRIENDS = tuple((dx, dc) for dx in range(SIDE) for dc in (0, 1) if dx or dc)
OTHERS = tuple((dy, dx) for dy in range(SIDE) for dx in range(SIDE) if dy or dx)


def greet(plane):
    barrier = pltpu.get_barrier_semaphore()
    devices = [plane.device(dy, dx) for dy, dx in OTHERS]
    devices += [plane.friend_device(dx, 1) for dx in range(SIDE)]
    devices += [plane.level(1), plane.level(-1)]
    for device in devices:
        pl.semaphore_signal(
            barrier, inc=1, device_id=device, device_id_type=pl.DeviceIdType.MESH
        )
    return lambda: pl.semaphore_wait(barrier, len(devices))


def remote(src, dst, send, recv, device):
    return pltpu.make_async_remote_copy(
        src_ref=src,
        dst_ref=dst,
        send_sem=send,
        recv_sem=recv,
        device_id=device,
        device_id_type=pl.DeviceIdType.MESH,
    )


KEYS = 512
HEADS = QUERY_HEADS // KEY_VALUE_HEADS
ASK = 256
LOW = -1e30
SCALE = HEAD_SIZE**-0.5 * 1.4426950408889634
ACROSS = (0, -1, 1, 2)


def attention_section(
    plane, weight_copy, project_keys, project_queries, make_tables,
    queries, pairs, starts, given, out, held,
    near, store, asked, begin, packed, peak, total, bias, done, replies,
    give, take, x_send, x_recv, y_send, y_recv, q_send, q_recv, o_send, o_recv, sems,
):
    core = plane.core
    here = plane.chip(0, 0)
    rows = queries.shape[0]
    mine = 2 * plane.x + core

    def lanes(at, size):
        return pl.ds(pl.multiple_of(at * size, size), size)

    swap = remote(
        pairs.at[:, lanes(1 - core, 512)], near, sems.at[0], sems.at[1], plane.partner()
    )

    def source(h, dx):
        x = lax.rem(plane.x + dx + SIDE, SIDE)
        if h == 0:
            return pairs.at[:, lanes(SIDE * core + x, 128)]
        return near.at[:, lanes(x, 128)]

    def slot(h, dy, dx, part=None):
        low = (core if h == 0 else 1 - core) * rows
        size = rows
        if part is not None:
            size = rows // 2
            low = low + part * size
        return store.at[plane.chip(dy, dx), pl.ds(pl.multiple_of(low, size), size)]

    def keep(h):
        return pltpu.make_async_copy(source(h, 0), slot(h, 0, 0), sems.at[2 + h])

    def across(h, n, incoming=False):
        dx = (1, -1, 2)[n]
        return remote(
            source(h, dx),
            slot(h, 0, -dx if incoming else 0),
            x_send.at[3 * h + n],
            x_recv.at[3 * h + n],
            plane.device(0, dx),
        )

    def along(h, i, n, incoming=False):
        dx = ACROSS[i]
        at, part, dy = ((0, None, 1), (0, None, -1), (-1, 0, 1), (1, 1, -1))[n]
        place = slot(h, at - dy if incoming else at, dx, part)
        src = source(h, 0) if (i == 0 and n < 2) else place
        if i == 0 and n < 2 and not incoming:
            place = slot(h, 0, 0)
        k = (h * 4 + i) * 4 + n
        return remote(src, place, y_send.at[k], y_recv.at[k], plane.device(dy, 0))

    def other(n, incoming):
        dx, dc = FRIENDS[n]
        return plane.friend(-dx if incoming else dx, dc)[2]

    def asking(head):
        return pl.ds(pl.multiple_of(lax.div(3 * head, 2) * 128, 128), ASK)

    def ask(n, incoming=False):
        return remote(
            queries.at[:, asking(other(n, False))],
            asked.at[other(n, True) if incoming else mine],
            q_send.at[n],
            q_recv.at[n],
            plane.friend_device(*FRIENDS[n]),
        )

    def tell(n, incoming=False):
        return remote(
            starts,
            begin.at[other(n, True) if incoming else mine],
            q_send.at[len(FRIENDS) + n],
            q_recv.at[len(FRIENDS) + n],
            plane.friend_device(*FRIENDS[n]),
        )

    def table(n, incoming=False):
        dy, dx = OTHERS[n]
        return remote(
            given.at[plane.chip(dy, dx)],
            held.at[plane.chip(-dy, -dx) if incoming else here],
            give.at[n],
            take.at[n],
            plane.device(dy, dx),
        )

    own_asked = pltpu.make_async_copy(
        queries.at[:, asking(mine)], asked.at[mine], sems.at[4]
    )
    own_begin = pltpu.make_async_copy(starts, begin.at[mine], sems.at[5])
    own_table = pltpu.make_async_copy(given.at[here], held.at[here], sems.at[6])

    project_keys()
    swap.start()
    for h in (0, 1):
        if h == 1:
            make_tables()
            own_begin.start()
            own_table.start()
            swap.wait_recv()
        keep(h).start()
        for n in range(3):
            across(h, n).start()
        along(h, 0, 0).start()
        along(h, 0, 1).start()
    project_queries()
    own_asked.start()
    for n in range(len(FRIENDS)):
        ask(n).start()
        tell(n).start()
    for n in range(3):
        i = (1, 2, 3)[n]
        for h in (0, 1):
            across(h, n, True).wait_recv()
            along(h, i, 0).start()
            along(h, i, 1).start()
    for n in range(len(OTHERS)):
        table(n).start()

    own_asked.wait()
    own_begin.wait()
    for n in range(len(FRIENDS)):
        ask(n, True).wait_recv()
        tell(n, True).wait_recv()
    for h in (0, 1):
        keep(h).wait()

    lane = lax.broadcasted_iota(jnp.int32, (rows, 128), 1)
    low = lane < HEAD_SIZE
    upper = core == 1
    for which in range(SIDE):
        for side in (0, 1):
            tiles = [
                asked[2 * which + side, :, i * 128 : (i + 1) * 128].astype(jnp.float32)
                for i in (0, 1)
            ]
            turned = [pltpu.roll(tile, HEAD_SIZE, axis=1) for tile in tiles]
            heads = (
                jnp.where(upper, turned[0], tiles[0]),
                jnp.where(upper, tiles[1], turned[0]),
                jnp.where(upper, turned[1], tiles[1]),
            )
            for n in range(HEADS):
                at = (n * 2 + side) * rows
                packed[which, at : at + rows, :] = jnp.where(low, heads[n], 0.0).astype(
                    jnp.bfloat16
                )
    peak[...] = jnp.full_like(peak, LOW)
    total[...] = jnp.zeros_like(total)
    both = 2 * HEADS * rows

    def member(which):
        flip = lax.rem(plane.x + which, 2)
        return jnp.where(flip == 0, plane.y, SIDE - 1 - plane.y) * SIDE + which

    def visit(which, chip):
        stream_chip = member(which)
        at = chip * (2 * rows)
        for side in (0, 1):
            first = jnp.broadcast_to(begin[2 * which + side, 0:1, :], (rows, rows)).T
            first = jnp.concatenate([first] * (KEYS // rows), axis=1).astype(jnp.int32)
            key_pos = at + lax.broadcasted_iota(jnp.int32, (rows, KEYS), 1)
            own_pos = (2 * stream_chip + side) * rows + lax.broadcasted_iota(
                jnp.int32, (rows, KEYS), 0
            )
            bias[side * rows : (side + 1) * rows, :] = jnp.where(
                (key_pos >= first) & (key_pos <= own_pos), 0.0, LOW
            )
        tile = store[pl.ds(chip, 2)].reshape(KEYS, 128)
        scores = lax.dot_general(
            packed[which], tile, (((1,), (1,)), ((), ())), preferred_element_type=jnp.float32
        )
        scores = (scores.reshape(HEADS, 2 * rows, KEYS) + bias[...][None]).reshape(both, KEYS)
        before = peak[which]
        now = jnp.maximum(before, jnp.max(scores, axis=1, keepdims=True))
        peak[which] = now
        fade = jnp.exp2((before - now) * SCALE)
        wide = jnp.concatenate([now] * (KEYS // 128), axis=1)
        probs = jnp.exp2((scores - wide) * SCALE).astype(jnp.bfloat16)
        value_lane = lax.broadcasted_iota(jnp.int32, (KEYS, 128), 1) >= HEAD_SIZE
        beside = jnp.where(value_lane, tile, jnp.ones_like(tile))
        total[which] = total[which] * fade + jnp.dot(
            probs, beside, preferred_element_type=jnp.float32
        )

    def phase(step, carry):
        @pl.when(step == 1)
        def _():
            for i in range(4):
                for n in (0, 1):
                    for h in (0, 1):
                        along(h, i, n, True).wait_recv()
                        along(h, i, n + 2).start()

        @pl.when(step == 3)
        def _():
            for i in range(4):
                for n in (2, 3):
                    for h in (0, 1):
                        along(h, i, n, True).wait_recv()

        dy = jnp.where(step == 0, 0, jnp.where(step == 1, SIDE - 1, step - 1))
        dy = jnp.where(step == 3, 2, dy)
        row = lax.rem(plane.y + dy, SIDE) * SIDE

        def one(t, carry):
            which = lax.div(t, 2)
            chip = row + 2 * lax.rem(t, 2)
            @pl.when(chip <= member(which))
            def _():
                visit(which, chip)

            return carry

        return lax.fori_loop(0, 2 * SIDE, one, carry)

    lax.fori_loop(0, 4, phase, 0)

    for which in range(SIDE):
        for side in (0, 1):
            high, turned = [], []
            for n in range(HEADS):
                at = (n * 2 + side) * rows
                sums_here = total[which, at : at + rows, :]
                high.append(sums_here / pltpu.roll(sums_here, HEAD_SIZE, axis=1))
                turned.append(pltpu.roll(high[n], HEAD_SIZE, axis=1))
            answer = (
                jnp.where(upper, high[0], jnp.where(low, turned[0], high[1])),
                jnp.where(upper, jnp.where(low, turned[1], high[2]), turned[2]),
            )
            for i in (0, 1):
                done[2 * which + side, :, i * 128 : (i + 1) * 128] = answer[i].astype(jnp.bfloat16)

    def reply(n, incoming=False):
        return remote(
            done.at[other(n, False)],
            replies.at[other(n, True) if incoming else mine],
            o_send.at[n],
            o_recv.at[n],
            plane.friend_device(*FRIENDS[n]),
        )

    for n in range(len(FRIENDS)):
        reply(n).start()
    own_reply = pltpu.make_async_copy(done.at[mine], replies.at[mine], sems.at[7])
    own_reply.start()
    for n in (0, 1):
        weight_copy(n, True).wait_recv()
        weight_copy(2 + n).start()
        weight_copy(5 + n).start()

    swap.wait_send()
    own_table.wait()
    for h in (0, 1):
        for n in range(3):
            across(h, n).wait_send()
        for i in range(4):
            for n in range(4):
                along(h, i, n).wait_send()
    for n in range(len(FRIENDS)):
        ask(n).wait_send()
        tell(n).wait_send()
    for n in range(len(OTHERS)):
        table(n, True).wait_recv()
        table(n).wait_send()
    own_reply.wait()
    for n in range(len(FRIENDS)):
        reply(n, True).wait_recv()
        reply(n).wait_send()
    for p in range(KEY_VALUE_HEADS // 2):
        even, odd = replies[2 * p], replies[2 * p + 1]
        out[:, p * 384 : p * 384 + 128] = even[:, :128]
        out[:, p * 384 + 128 : p * 384 + 256] = jnp.where(
            low, even[:, 128:].astype(jnp.float32), odd[:, :128].astype(jnp.float32)
        ).astype(jnp.bfloat16)
        out[:, p * 384 + 256 : p * 384 + 384] = odd[:, 128:]


BLOCKS = 4
GROUPS = (
    ((0, 0), (2, 0), (0, -1), (0, 1)),
    ((-1, 0), (1, 0), (-1, -1), (-1, 1)),
    ((-1, 2), (1, 2), (1, -1), (1, 1)),
    ((0, 2), (2, 2), (2, -1), (2, 1)),
)
TWO = (0, 2)
ENDS = (-1, 1)


def experts_section(
    plane, weight_copy, own, residual, tables, out,
    rows_in, sums, weights, picked, made, hold_q, hold_r, hold_p, hold_d,
    g_send, g_recv, q_send, q_recv, r_send, r_recv, p_send, p_recv, d_send, d_recv, sem,
):
    rows, width = own.shape
    part_rows = rows // 2
    even = lax.rem(plane.y + plane.x, 2) == 0

    def turned(o, t):
        return jnp.where(even, t, o), jnp.where(even, o, t)

    def place(at):
        return plane.chip(*turned(*at))

    def device(o, t):
        return plane.device(*turned(o, t))

    def part(n):
        return pl.ds(n * part_rows, part_rows)

    def gather(k, src, dst, to):
        return remote(src, dst, g_send.at[k], g_recv.at[k], to)

    def emit(n, incoming=False):
        d = (1, -1)[n]
        at = (0, -d) if incoming else (0, 0)
        return gather(n, own, rows_in.at[place(at)], device(d, 0))

    def pass_on(n, incoming=False):
        at = (2, 0) if incoming else (0, ENDS[n])
        ref = rows_in.at[place(at), part(n)]
        return gather(2 + n, ref, ref, device(0, -ENDS[n]))

    def spread(group, j, n, incoming=False):
        d = (1, -1)[n]
        if group == 0:
            at = (-d, TWO[j]) if incoming else (TWO[j], 0)
            to = device(0, d)
        else:
            at = (ENDS[j], -d) if incoming else (0, ENDS[j])
            to = device(d, 0)
        ref = rows_in.at[place(at)]
        src = own if at == (0, 0) else ref
        return gather(4 + group * 8 + j * 4 + n, src, ref, to)

    def relay(group, j, n, incoming=False):
        if group == 0:
            at = (TWO[j], 2) if incoming else (ENDS[n], TWO[j])
            to = device(-ENDS[n], 0)
        else:
            at = (2, ENDS[j]) if incoming else (ENDS[j], ENDS[n])
            to = device(0, -ENDS[n])
        ref = rows_in.at[place(at), part(n)]
        return gather(4 + group * 8 + j * 4 + 2 + n, ref, ref, to)

    mine = pltpu.make_async_copy(own, rows_in.at[place((0, 0))], sem)
    for n in (0, 1):
        emit(n).start()
    for n in (0, 1):
        spread(0, 0, n).start()
    mine.start()
    for j in (0, 1):
        emit(j, True).wait_recv()
        pass_on(j).start()
        for n in (0, 1):
            spread(1, j, n).start()
    for n in (0, 1):
        pass_on(n, True).wait_recv()
    for n in (0, 1):
        spread(0, 1, n).start()
    for n in (2, 3):
        weight_copy(n, True).wait_recv()
    weight_copy(7).start()
    mine.wait()
    for n in (4, 5, 6, 7):
        weight_copy(n, True).wait_recv()

    def far(group, j):
        return (TWO[j], 2) if group == 0 else (2, ENDS[j])

    def near(group, j, side):
        return (ENDS[side], TWO[j]) if group == 0 else (ENDS[j], ENDS[side])

    def line(group, along_first):
        return (lambda d: device(d, 0)) if (group == 0) == along_first else (lambda d: device(0, d))

    def give_far(group, j, n):
        k = group * 4 + j * 2 + n
        return remote(
            sums.at[place(far(group, j)), part(n)],
            hold_q.at[k],
            q_send.at[k],
            q_recv.at[k],
            line(group, False)(ENDS[n]),
        )

    def give_near(group, j, side, late):
        k = group * 4 + j * 2 + side
        span = part(side if late else 1 - side)
        return remote(
            sums.at[place(near(group, j, side)), span],
            hold_r.at[k, span],
            r_send.at[2 * k + late],
            r_recv.at[2 * k + late],
            line(group, True)(ENDS[side]),
        )

    def give_across(n):
        return remote(
            sums.at[place((2, 0)), part(n)],
            hold_p.at[n],
            p_send.at[n],
            p_recv.at[n],
            device(ENDS[n], 0),
        )

    def give_back(side, late):
        span = part(side if late else 1 - side)
        return remote(
            sums.at[place((0, ENDS[side])), span],
            hold_d.at[side, span],
            d_send.at[2 * side + late],
            d_recv.at[2 * side + late],
            device(0, ENDS[side]),
        )

    PAIRS = [(group, j) for j in (0, 1) for group in (0, 1)]
    slot = lax.broadcasted_iota(jnp.int32, (SLOTS, rows), 0).astype(jnp.float32)

    def group_step(g, carry):
        for when, j in ((1, 0), (2, 1)):

            @pl.when(g == when)
            def _():
                for n in (0, 1):
                    for group in (0, 1):
                        spread(group, j, n, True).wait_recv()
                        relay(group, j, n).start()

        @pl.when(g == 3)
        def _():
            for group, j in PAIRS:
                for n in (0, 1):
                    relay(group, j, n, True).wait_recv()
            for group, j in PAIRS:
                for side in (0, 1):
                    give_near(group, j, side, 0).start()

        ids = []
        for j in range(BLOCKS):
            at = place(GROUPS[3][j])
            for k in range(3):
                at = jnp.where(g == k, place(GROUPS[k][j]), at)
            ids.append(at)

        def hits(j, e):
            return tables[ids[j], 2 + e : 3 + e, :] == slot

        def choice(j):
            both = jnp.concatenate([hits(j, 0), hits(j, 1)], axis=0)
            return jnp.where(both, 1.0, 0.0).astype(jnp.bfloat16)

        for j in range(BLOCKS):
            picked[j] = jnp.dot(
                choice(j), rows_in[ids[j]], preferred_element_type=jnp.float32
            ).astype(jnp.bfloat16)
        for e in (0, 1):
            chosen = picked[:, e * SLOTS : (e + 1) * SLOTS, :].reshape(BLOCKS * SLOTS, width)
            gate = jnp.dot(chosen, weights[e, 0], preferred_element_type=jnp.float32)
            up = jnp.dot(chosen, weights[e, 1], preferred_element_type=jnp.float32)
            units = (gate / (1.0 + jnp.exp(-gate)) * up).astype(jnp.bfloat16)
            result = lax.dot_general(
                units, weights[e, 2], (((1,), (1,)), ((), ())), preferred_element_type=jnp.float32
            )
            for j in range(BLOCKS):
                gain = jnp.sum(
                    jnp.where(hits(j, e), tables[ids[j], e : e + 1, :], 0.0),
                    axis=1,
                    keepdims=True,
                )
                made[j, e * SLOTS : (e + 1) * SLOTS, :] = (
                    result[j * SLOTS : (j + 1) * SLOTS, :] * gain
                ).astype(jnp.bfloat16)
        for j in range(BLOCKS):
            sums[ids[j]] = lax.dot_general(
                choice(j), made[j], (((0,), (0,)), ((), ())), preferred_element_type=jnp.float32
            ).astype(jnp.bfloat16)
        return carry

    lax.fori_loop(0, len(GROUPS), group_step, 0)

    for group, j in PAIRS:
        for n in (0, 1):
            give_far(group, j, n).start()

    def add(at, held):
        sums[at] = (sums[at].astype(jnp.float32) + held.astype(jnp.float32)).astype(jnp.bfloat16)

    for group, j in PAIRS:
        for side in (0, 1):
            k = group * 4 + j * 2 + side
            give_far(group, j, side).wait_recv()
            add((place(near(group, j, side)), part(side)), hold_q[k])
            give_near(group, j, side, 1).start()

    def total(group, j):
        for side in (0, 1):
            for late in (0, 1):
                give_near(group, j, side, late).wait_recv()
        at = place((TWO[j], 0) if group == 0 else (0, ENDS[j]))
        k = group * 4 + j * 2
        return at, (
            sums[at].astype(jnp.float32)
            + hold_r[k].astype(jnp.float32)
            + hold_r[k + 1].astype(jnp.float32)
        )

    at, value = total(0, 1)
    sums[at] = value.astype(jnp.bfloat16)
    for n in (0, 1):
        give_across(n).start()
    for side in (0, 1):
        at, value = total(1, side)
        sums[at] = value.astype(jnp.bfloat16)
        give_back(side, 0).start()
    _, value = total(0, 0)
    out_sum = value + residual[...]
    for side in (0, 1):
        give_across(side).wait_recv()
        add((place((0, ENDS[side])), part(side)), hold_p[side])
        give_back(side, 1).start()
    for side in (0, 1):
        for late in (0, 1):
            give_back(side, late).wait_recv()
    out[...] = (
        out_sum + hold_d[0].astype(jnp.float32) + hold_d[1].astype(jnp.float32)
    ).astype(out.dtype)

    for n in (0, 1):
        emit(n).wait_send()
        pass_on(n).wait_send()
        give_across(n).wait_send()
        for late in (0, 1):
            give_back(n, late).wait_send()
    for n in range(8):
        weight_copy(n).wait_send()
    for group, j in PAIRS:
        for n in (0, 1):
            spread(group, j, n).wait_send()
            relay(group, j, n).wait_send()
            give_far(group, j, n).wait_send()
            for late in (0, 1):
                give_near(group, j, n, late).wait_send()


def normed(values, gain):
    mean_square = jnp.mean(values * values, axis=1, keepdims=True)
    return (values * lax.rsqrt(mean_square + epsilon) * gain[None]).astype(jnp.bfloat16)


def layer_kernel(
    hidden, attn_gain, wq, wk, wv, wo, prompt_start, cosine, sine, ffn_gain, routes, route_weights,
    first,
    out, key_cache, value_cache,
    query_w, key_w, value_w, output_w, own_in, residual,
    queries, pairs, starts, given, attention, tables,
    near, store, asked, begin, packed, peak, total, bias, done, replies,
    rows_in, sums, weights, picked, made, hold_q, hold_r, hold_p, hold_d,
    *sems,
):
    attention_sems, expert_sems, (w_send, w_recv, load_sems, row_sem) = (
        sems[:11],
        sems[11:21],
        sems[21:],
    )
    plane = Plane()
    core = plane.core
    rows, width = hidden.shape
    arrived = greet(plane)

    def lanes(r):
        return pl.ds(r * 128, 128)

    def weight_copy(n, incoming=False):
        half = width // 2
        e = 1 - core if incoming and n >= 4 else core
        if n < 2:
            src, dst = first, weights.at[e, :, :, lanes(1 + n)]
            to = plane.level((1, -1)[n])
        elif n < 4:
            span = pl.ds((n - 2) * half, half)
            src = weights.at[e, :, span, lanes(n - 1)]
            dst = weights.at[e, :, span, lanes(3)]
            to = plane.level((1, -1)[n - 2])
        else:
            dst = weights.at[e, :, :, lanes(n - 4)]
            src = first if n == 4 else dst
            to = plane.partner()
        return remote(src, dst, w_send.at[n], w_recv.at[n], to)

    loads = [
        pltpu.make_async_copy(src, dst, load_sems.at[n])
        for n, (src, dst) in enumerate(
            (
                (wk, key_w),
                (wv, value_w),
                (wq, query_w),
                (wo, output_w),
                (first, weights.at[core, :, :, lanes(0)]),
            )
        )
    ]
    for load in loads:
        load.start()
    own_in[...] = normed(hidden[...].astype(jnp.float32), attn_gain[...])
    arrived()
    for n in (0, 1, 4):
        weight_copy(n).start()

    lane = lax.broadcasted_iota(jnp.int32, (rows, 128), 1)
    first_half = lax.rem(lane, HEAD_SIZE) < HEAD_SIZE // 2

    def rotated(tile):
        other = jnp.where(
            first_half,
            pltpu.roll(tile, 128 - HEAD_SIZE // 2, axis=1),
            pltpu.roll(tile, HEAD_SIZE // 2, axis=1),
        )
        return tile * cosine[...] + other * sine[...]

    def project_keys():
        starts[...] = jnp.broadcast_to(prompt_start[...].astype(jnp.float32), starts.shape)
        loads[0].wait()
        keys = jnp.dot(own_in[...], key_w[...], preferred_element_type=jnp.float32)
        loads[1].wait()
        values = jnp.dot(own_in[...], value_w[...], preferred_element_type=jnp.float32)
        value_cache[...] = values.astype(jnp.bfloat16)
        low = lane < HEAD_SIZE
        for p in range(KEY_VALUE_HEADS // 2):
            at = slice(p * 128, (p + 1) * 128)
            key, value = rotated(keys[:, at]), values[:, at]
            key_cache[:, at] = key.astype(jnp.bfloat16)
            sides = (
                jnp.where(low, key, pltpu.roll(value, HEAD_SIZE, axis=1)),
                jnp.where(low, pltpu.roll(key, HEAD_SIZE, axis=1), value),
            )
            for c in (0, 1):
                to = (c * SIDE + p) * 128
                pairs[:, to : to + 128] = sides[c].astype(jnp.bfloat16)

    def project_queries():
        loads[2].wait()
        for c in range(3):
            part = jnp.dot(
                own_in[...],
                query_w[:, c * 512 : (c + 1) * 512],
                preferred_element_type=jnp.float32,
            )
            for p in range(4):
                at = c * 512 + p * 128
                queries[:, at : at + 128] = rotated(part[:, p * 128 : (p + 1) * 128]).astype(
                    jnp.bfloat16
                )

    def make_tables():
        expert = lax.broadcasted_iota(jnp.int32, (EXPERTS, rows), 0)
        gains = jnp.zeros((EXPERTS, rows), jnp.float32)
        named = jnp.zeros((EXPERTS, rows), jnp.float32)
        for j in range(TOP):
            hit = routes[j : j + 1, :] == expert
            gains = gains + jnp.where(hit, route_weights[j : j + 1, :], 0.0)
            named = named + jnp.where(hit, 1.0, 0.0)
        earlier = lax.broadcasted_iota(jnp.int32, (rows, rows), 0) < lax.broadcasted_iota(
            jnp.int32, (rows, rows), 1
        )
        ranks = jnp.dot(
            named.astype(jnp.bfloat16),
            jnp.where(earlier, 1.0, 0.0).astype(jnp.bfloat16),
            preferred_element_type=jnp.float32,
        )
        ranks = jnp.where(named > 0.0, ranks, -1.0)
        given[...] = jnp.zeros_like(given)
        for c in range(CHIPS):
            given[c, 0:2, :] = gains[2 * c : 2 * c + 2, :]
            given[c, 2:4, :] = ranks[2 * c : 2 * c + 2, :]

    attention_section(
        plane, weight_copy, project_keys, project_queries, make_tables,
        queries, pairs, starts, given, attention, tables,
        near, store, asked, begin, packed, peak, total, bias, done, replies,
        *attention_sems,
    )

    loads[3].wait()
    for c in range(3):
        at = slice(c * 512, (c + 1) * 512)
        residual[:, at] = hidden[:, at].astype(jnp.float32) + jnp.dot(
            attention[...], output_w[:, at], preferred_element_type=jnp.float32
        )
    own_in[...] = normed(residual[...], ffn_gain[...])
    loads[4].wait()

    experts_section(
        plane, weight_copy, own_in, residual, tables, out,
        rows_in, sums, weights, picked, made, hold_q, hold_r, hold_p, hold_d,
        *expert_sems, row_sem,
    )


def run_layer(hidden, attn_gain, wq, wk, wv, wo, starts, trig, ffn_gain, routes, gains, first):
    rows, width = hidden.shape
    cache = wk.shape[1]
    dma = pltpu.SemaphoreType.DMA
    vmem = pl.BlockSpec(memory_space=pltpu.VMEM)
    hbm = pl.BlockSpec(memory_space=pl.ANY)

    def brief(*shape):
        return pltpu.VMEM(shape, jnp.bfloat16)

    def full(*shape):
        return pltpu.VMEM(shape, jnp.float32)

    others = len(OTHERS)
    friends = len(FRIENDS)
    counts = (others, 6, 32, 2 * friends, friends)
    attention_sems = [dma((n,)) for n in counts for _ in (0, 1)] + [dma((8,))]
    expert_sems = [dma((n,)) for n in (20, 8, 16, 2, 4) for _ in (0, 1)]
    both = 2 * HEADS * rows
    return pl.pallas_call(
        layer_kernel,
        out_shape=(
            jax.ShapeDtypeStruct((rows, width), jnp.bfloat16),
            jax.ShapeDtypeStruct((rows, cache), jnp.bfloat16),
            jax.ShapeDtypeStruct((rows, cache), jnp.bfloat16),
        ),
        in_specs=[vmem, vmem, hbm, hbm, hbm, hbm] + [vmem] * 6 + [hbm],
        out_specs=(vmem,) * 3,
        scratch_shapes=[
            brief(*wq.shape),
            brief(*wk.shape),
            brief(*wv.shape),
            brief(*wo.shape),
            brief(rows, width),
            full(rows, width),
            brief(rows, width),
            brief(rows, 2 * cache),
            full(8, rows),
            full(CHIPS, 8, rows),
            brief(rows, width),
            full(CHIPS, 8, rows),
            brief(rows, 512),
            brief(CHIPS, 2 * rows, 128),
            brief(KEY_VALUE_HEADS, rows, ASK),
            full(KEY_VALUE_HEADS, 8, rows),
            brief(SIDE, both, 128),
            full(SIDE, both, 128),
            full(SIDE, both, 128),
            full(2 * rows, KEYS),
            brief(KEY_VALUE_HEADS, rows, ASK),
            brief(KEY_VALUE_HEADS, rows, ASK),
            brief(CHIPS, rows, width),
            brief(CHIPS, rows, width),
            brief(2, 3, width, FF),
            brief(BLOCKS, 2 * SLOTS, width),
            brief(BLOCKS, 2 * SLOTS, width),
            brief(8, rows // 2, width),
            brief(8, rows, width),
            brief(2, rows // 2, width),
            brief(2, rows, width),
            *attention_sems,
            *expert_sems,
            dma((8,)),
            dma((8,)),
            dma((5,)),
            dma,
        ],
        compiler_params=pltpu.CompilerParams(
            collective_id=0, has_side_effects=True, vmem_limit_bytes=63 << 20
        ),
        name="layer",
    )(
        hidden, attn_gain, wq, wk, wv, wo, starts, *trig, ffn_gain, routes, gains, first
    )


def publish(*results):
    def kernel(*refs):
        for src, dst in zip(refs[: len(results)], refs[len(results) :]):
            dst[...] = src[...]

    vmem = pl.BlockSpec(memory_space=pltpu.VMEM)
    return pl.pallas_call(
        kernel,
        out_shape=tuple(jax.ShapeDtypeStruct(r.shape, r.dtype) for r in results),
        in_specs=[vmem] * len(results),
        out_specs=(vmem,) * len(results),
        name="publish",
    )(*results)


def rotation_tables(offsets):
    half = HEAD_SIZE // 2
    freqs = 10000.0 ** (-jnp.arange(half, dtype=jnp.float32) / half)
    freqs = jnp.tile(freqs, 128 // half)
    sign = jnp.where(jnp.arange(128) % HEAD_SIZE < half, -1.0, 1.0)
    angle = offsets.astype(jnp.float32)[:, None] * freqs[None, :]
    return jnp.cos(angle), jnp.sin(angle) * sign[None, :]


def shards(
    hidden,
    attn_gain,
    query_weight,
    key_matrix,
    value_matrix,
    output_weight,
    prompt_start,
    ffn_gain,
    routes,
    route_weights,
    expert_weights,
):
    rows = hidden.shape[0]
    positions = lax.axis_index("exp") * rows + jnp.arange(rows, dtype=jnp.int32)
    results = run_layer(
        hidden,
        attn_gain,
        query_weight,
        key_matrix,
        value_matrix,
        output_weight,
        prompt_start[None],
        rotation_tables(positions - prompt_start),
        ffn_gain,
        routes.T,
        route_weights.T,
        expert_weights[0],
    )
    return publish(*results)


def solution(mesh):
    in_specs = (
        P(("req", "exp"), None),
        P(),
        P(),
        P(),
        P(),
        P(),
        P(("req", "exp")),
        P(),
        P(("req", "exp"), None),
        P(("req", "exp"), None),
        P("exp", None, None, "req"),
    )
    out_specs = (P(("req", "exp"), None), P(("req", "exp"), None), P(("req", "exp"), None))
    return jax.shard_map(shards, mesh=mesh, in_specs=in_specs, out_specs=out_specs, check_vma=False)
```

```python
import math

import jax
import jax.numpy as jnp
from jax import lax
from jax.experimental import pallas as pl
from jax.experimental.pallas import tpu as pltpu
from jax.sharding import PartitionSpec as P

QUERY_HEADS = 24
KEY_VALUE_HEADS = 8
HEAD_SIZE = 64
TOP = 8
SIDE = 4
CHIPS = SIDE * SIDE
EXPERTS = 32
SLOTS = 64
FF = 512


epsilon = 1e-05


class Plane:
    def __init__(self):
        me = lax.axis_index("exp")
        self.core = lax.rem(me, 2)
        chip = lax.div(me, 2)
        self.y = lax.div(chip, SIDE)
        self.x = lax.rem(chip, SIDE)

    def chip(self, dy, dx):
        return lax.rem(self.y + dy + SIDE, SIDE) * SIDE + lax.rem(self.x + dx + SIDE, SIDE)

    def device(self, dy, dx):
        return {"exp": self.chip(dy, dx) * 2 + self.core}

    def level(self, dz):
        return {"req": lax.rem(lax.axis_index("req") + dz + SIDE, SIDE)}

    def partner(self):
        return {"exp": self.chip(0, 0) * 2 + 1 - self.core}

    def friend(self, dx, dc):
        x = lax.rem(self.x + dx + SIDE, SIDE)
        y = self.y if dx % 2 == 0 else SIDE - 1 - self.y
        core = 1 - self.core if dc else self.core
        return y * SIDE + x, core, 2 * x + core

    def friend_device(self, dx, dc):
        chip, core, _ = self.friend(dx, dc)
        return {"exp": chip * 2 + core}


FRIENDS = tuple((dx, dc) for dx in range(SIDE) for dc in (0, 1) if dx or dc)
OTHERS = tuple((dy, dx) for dy in range(SIDE) for dx in range(SIDE) if dy or dx)


def greet(plane):
    barrier = pltpu.get_barrier_semaphore()
    devices = [plane.device(dy, dx) for dy, dx in OTHERS]
    devices += [plane.friend_device(dx, 1) for dx in range(SIDE)]
    devices += [plane.level(1), plane.level(-1)]
    for device in devices:
        pl.semaphore_signal(
            barrier, inc=1, device_id=device, device_id_type=pl.DeviceIdType.MESH
        )
    return lambda: pl.semaphore_wait(barrier, len(devices))


def remote(src, dst, send, recv, device):
    return pltpu.make_async_remote_copy(
        src_ref=src,
        dst_ref=dst,
        send_sem=send,
        recv_sem=recv,
        device_id=device,
        device_id_type=pl.DeviceIdType.MESH,
    )


KEYS = 512
HEADS = QUERY_HEADS // KEY_VALUE_HEADS
ASK = 256
LOW = -1e30
SCALE = HEAD_SIZE**-0.5 * 1.4426950408889634
ACROSS = (0, -1, 1, 2)


def attention_section(
    plane, weight_copy, project_keys, project_queries, make_tables,
    queries, pairs, starts, given, out, held,
    near, store, asked, begin, begins, packed, peak, total, bias, done, replies,
    give, take, x_send, x_recv, y_send, y_recv, q_send, q_recv, o_send, o_recv, sems,
):
    core = plane.core
    here = plane.chip(0, 0)
    rows = queries.shape[0]
    mine = 2 * plane.x + core

    def lanes(at, size):
        return pl.ds(pl.multiple_of(at * size, size), size)

    swap = remote(
        pairs.at[:, lanes(1 - core, 512)], near, sems.at[0], sems.at[1], plane.partner()
    )

    def source(h, dx):
        x = lax.rem(plane.x + dx + SIDE, SIDE)
        if h == 0:
            return pairs.at[:, lanes(SIDE * core + x, 128)]
        return near.at[:, lanes(x, 128)]

    def slot(h, dy, dx, part=None):
        low = (core if h == 0 else 1 - core) * rows
        size = rows
        if part is not None:
            size = rows // 2
            low = low + part * size
        return store.at[plane.chip(dy, dx), pl.ds(pl.multiple_of(low, size), size)]

    def keep(h):
        return pltpu.make_async_copy(source(h, 0), slot(h, 0, 0), sems.at[2 + h])

    def across(h, n, incoming=False):
        dx = (1, -1, 2)[n]
        return remote(
            source(h, dx),
            slot(h, 0, -dx if incoming else 0),
            x_send.at[3 * h + n],
            x_recv.at[3 * h + n],
            plane.device(0, dx),
        )

    def along(h, i, n, incoming=False):
        dx = ACROSS[i]
        at, part, dy = ((0, None, 1), (0, None, -1), (-1, 0, 1), (1, 1, -1))[n]
        place = slot(h, at - dy if incoming else at, dx, part)
        src = source(h, 0) if (i == 0 and n < 2) else place
        if i == 0 and n < 2 and not incoming:
            place = slot(h, 0, 0)
        k = (h * 4 + i) * 4 + n
        return remote(src, place, y_send.at[k], y_recv.at[k], plane.device(dy, 0))

    def other(n, incoming):
        dx, dc = FRIENDS[n]
        return plane.friend(-dx if incoming else dx, dc)[2]

    def asking(head):
        return pl.ds(pl.multiple_of(lax.div(3 * head, 2) * 128, 128), ASK)

    def ask(n, incoming=False):
        return remote(
            queries.at[:, asking(other(n, False))],
            asked.at[other(n, True) if incoming else mine],
            q_send.at[n],
            q_recv.at[n],
            plane.friend_device(*FRIENDS[n]),
        )

    def tell(n, incoming=False):
        return remote(
            starts,
            begin.at[other(n, True) if incoming else mine],
            q_send.at[len(FRIENDS) + n],
            q_recv.at[len(FRIENDS) + n],
            plane.friend_device(*FRIENDS[n]),
        )

    def table(n, incoming=False):
        dy, dx = OTHERS[n]
        return remote(
            given.at[plane.chip(dy, dx)],
            held.at[plane.chip(-dy, -dx) if incoming else here],
            give.at[n],
            take.at[n],
            plane.device(dy, dx),
        )

    own_asked = pltpu.make_async_copy(
        queries.at[:, asking(mine)], asked.at[mine], sems.at[4]
    )
    own_begin = pltpu.make_async_copy(starts, begin.at[mine], sems.at[5])
    own_table = pltpu.make_async_copy(given.at[here], held.at[here], sems.at[6])

    project_keys()
    swap.start()
    for h in (0, 1):
        if h == 1:
            make_tables()
            own_begin.start()
            own_table.start()
            swap.wait_recv()
        keep(h).start()
        for n in range(3):
            across(h, n).start()
        along(h, 0, 0).start()
        along(h, 0, 1).start()
    project_queries()
    own_asked.start()
    for n in range(len(FRIENDS)):
        ask(n).start()
        tell(n).start()
    for n in range(3):
        i = (1, 2, 3)[n]
        for h in (0, 1):
            across(h, n, True).wait_recv()
            along(h, i, 0).start()
            along(h, i, 1).start()
    for n in range(len(OTHERS)):
        table(n).start()

    own_asked.wait()
    own_begin.wait()
    for n in range(len(FRIENDS)):
        ask(n, True).wait_recv()
        tell(n, True).wait_recv()
    for h in (0, 1):
        keep(h).wait()

    lane = lax.broadcasted_iota(jnp.int32, (rows, 128), 1)
    low = lane < HEAD_SIZE
    upper = core == 1
    for which in range(SIDE):
        for side in (0, 1):
            begins[2 * which + side] = jnp.broadcast_to(
                begin[2 * which + side, 0:1, :], (rows, rows)
            ).T
            tiles = [
                asked[2 * which + side, :, i * 128 : (i + 1) * 128].astype(jnp.float32)
                for i in (0, 1)
            ]
            turned = [pltpu.roll(tile, HEAD_SIZE, axis=1) for tile in tiles]
            heads = (
                jnp.where(upper, turned[0], tiles[0]),
                jnp.where(upper, tiles[1], turned[0]),
                jnp.where(upper, turned[1], tiles[1]),
            )
            for n in range(HEADS):
                at = (n * 2 + side) * rows
                packed[which, at : at + rows, :] = jnp.where(low, heads[n], 0.0).astype(
                    jnp.bfloat16
                )
    peak[...] = jnp.full_like(peak, LOW)
    total[...] = jnp.zeros_like(total)
    both = 2 * HEADS * rows
    lane_number = lax.broadcasted_iota(jnp.int32, (1, 128), 1).astype(jnp.float32)
    row_number = lax.broadcasted_iota(jnp.int32, (rows, 128), 0).astype(jnp.float32)

    def member(which):
        flip = lax.rem(plane.x + which, 2)
        return jnp.where(flip == 0, plane.y, SIDE - 1 - plane.y) * SIDE + which

    def visit(which, chip):
        stream_chip = member(which)
        at = chip * (2 * rows)
        shift = (stream_chip * (2 * rows) - at).astype(jnp.float32)
        base = at.astype(jnp.float32)
        for side in (0, 1):
            first = begins[2 * which + side] - base
            last = row_number + (shift + side * rows)
            for j in range(KEYS // 128):
                key_number = lane_number + j * 128
                bias[side * rows : (side + 1) * rows, j * 128 : (j + 1) * 128] = jnp.where(
                    (key_number >= first) & (key_number <= last), 0.0, LOW
                )
        tile = store[pl.ds(chip, 2)].reshape(KEYS, 128)
        scores = lax.dot_general(
            packed[which], tile, (((1,), (1,)), ((), ())), preferred_element_type=jnp.float32
        )
        scores = (scores.reshape(HEADS, 2 * rows, KEYS) + bias[...][None]).reshape(both, KEYS)
        before = peak[which]
        now = jnp.maximum(before, jnp.max(scores, axis=1, keepdims=True))
        peak[which] = now
        fade = jnp.exp2((before - now) * SCALE)
        wide = jnp.concatenate([now] * (KEYS // 128), axis=1)
        probs = jnp.exp2((scores - wide) * SCALE).astype(jnp.bfloat16)
        value_lane = lax.broadcasted_iota(jnp.int32, (KEYS, 128), 1) >= HEAD_SIZE
        beside = jnp.where(value_lane, tile, jnp.ones_like(tile))
        total[which] = total[which] * fade + jnp.dot(
            probs, beside, preferred_element_type=jnp.float32
        )

    def answer(which):
        for side in (0, 1):
            high, turned = [], []
            for n in range(HEADS):
                at = (n * 2 + side) * rows
                sums_here = total[which, at : at + rows, :]
                high.append(sums_here / pltpu.roll(sums_here, HEAD_SIZE, axis=1))
                turned.append(pltpu.roll(high[n], HEAD_SIZE, axis=1))
            tiles = (
                jnp.where(upper, high[0], jnp.where(low, turned[0], high[1])),
                jnp.where(upper, jnp.where(low, turned[1], high[2]), turned[2]),
            )
            for i in (0, 1):
                done[2 * which + side, :, i * 128 : (i + 1) * 128] = tiles[i].astype(jnp.bfloat16)

    def reply(n, incoming=False):
        return remote(
            done.at[other(n, False)],
            replies.at[other(n, True) if incoming else mine],
            o_send.at[n],
            o_recv.at[n],
            plane.friend_device(*FRIENDS[n]),
        )

    own_reply = pltpu.make_async_copy(done.at[mine], replies.at[mine], sems.at[7])

    def phase(step, carry):
        @pl.when(step == 1)
        def _():
            for i in range(4):
                for n in (0, 1):
                    for h in (0, 1):
                        along(h, i, n, True).wait_recv()
                        along(h, i, n + 2).start()

        @pl.when(step == 3)
        def _():
            for i in range(4):
                for n in (2, 3):
                    for h in (0, 1):
                        along(h, i, n, True).wait_recv()

        dy = jnp.where(step == 0, 0, jnp.where(step == 1, SIDE - 1, step - 1))
        dy = jnp.where(step == 3, 2, dy)
        row = lax.rem(plane.y + dy, SIDE) * SIDE

        def one(t, carry):
            turn, part = lax.div(t, 2), lax.rem(t, 2)
            dx = jnp.where(turn == 0, 2, jnp.where(turn == 1, 1, jnp.where(turn == 2, 3, 0)))
            which = lax.rem(plane.x + dx, SIDE)
            chip = row + 2 * part

            @pl.when(chip <= member(which))
            def _():
                visit(which, chip)

            @pl.when((step == 3) & (part == 1))
            def _():
                answer(which)

            for column in range(SIDE):

                @pl.when((step == 3) & (part == 1) & (dx == column))
                def _():
                    for n, friend in enumerate(FRIENDS):
                        if friend[0] == column:
                            reply(n).start()
                    if column == 0:
                        own_reply.start()

            return carry

        return lax.fori_loop(0, 2 * SIDE, one, carry)

    lax.fori_loop(0, 4, phase, 0)

    for n in (0, 1):
        weight_copy(n, True).wait_recv()
        weight_copy(2 + n).start()
        weight_copy(5 + n).start()

    swap.wait_send()
    own_table.wait()
    for h in (0, 1):
        for n in range(3):
            across(h, n).wait_send()
        for i in range(4):
            for n in range(4):
                along(h, i, n).wait_send()
    for n in range(len(FRIENDS)):
        ask(n).wait_send()
        tell(n).wait_send()
    for n in range(len(OTHERS)):
        table(n, True).wait_recv()
        table(n).wait_send()
    own_reply.wait()
    for n in range(len(FRIENDS)):
        reply(n, True).wait_recv()
        reply(n).wait_send()
    for p in range(KEY_VALUE_HEADS // 2):
        even, odd = replies[2 * p], replies[2 * p + 1]
        out[:, p * 384 : p * 384 + 128] = even[:, :128]
        out[:, p * 384 + 128 : p * 384 + 256] = jnp.where(
            low, even[:, 128:].astype(jnp.float32), odd[:, :128].astype(jnp.float32)
        ).astype(jnp.bfloat16)
        out[:, p * 384 + 256 : p * 384 + 384] = odd[:, 128:]


BLOCKS = 4
GROUPS = (
    ((0, 0), (2, 0), (0, -1), (0, 1)),
    ((-1, 0), (1, 0), (-1, -1), (-1, 1)),
    ((-1, 2), (1, 2), (1, -1), (1, 1)),
    ((0, 2), (2, 2), (2, -1), (2, 1)),
)
TWO = (0, 2)
ENDS = (-1, 1)


def experts_section(
    plane, weight_copy, own, residual, tables, out,
    rows_in, sums, weights, picked, made, hold_q, hold_r, hold_p, hold_d,
    g_send, g_recv, q_send, q_recv, r_send, r_recv, p_send, p_recv, d_send, d_recv, sem,
):
    rows, width = own.shape
    part_rows = rows // 2
    even = lax.rem(plane.y + plane.x, 2) == 0

    def turned(o, t):
        return jnp.where(even, t, o), jnp.where(even, o, t)

    def place(at):
        return plane.chip(*turned(*at))

    def device(o, t):
        return plane.device(*turned(o, t))

    def part(n):
        return pl.ds(n * part_rows, part_rows)

    def gather(k, src, dst, to):
        return remote(src, dst, g_send.at[k], g_recv.at[k], to)

    def emit(n, incoming=False):
        d = (1, -1)[n]
        at = (0, -d) if incoming else (0, 0)
        return gather(n, own, rows_in.at[place(at)], device(d, 0))

    def pass_on(n, incoming=False):
        at = (2, 0) if incoming else (0, ENDS[n])
        ref = rows_in.at[place(at), part(n)]
        return gather(2 + n, ref, ref, device(0, -ENDS[n]))

    def spread(group, j, n, incoming=False):
        d = (1, -1)[n]
        if group == 0:
            at = (-d, TWO[j]) if incoming else (TWO[j], 0)
            to = device(0, d)
        else:
            at = (ENDS[j], -d) if incoming else (0, ENDS[j])
            to = device(d, 0)
        ref = rows_in.at[place(at)]
        src = own if at == (0, 0) else ref
        return gather(4 + group * 8 + j * 4 + n, src, ref, to)

    def relay(group, j, n, incoming=False):
        if group == 0:
            at = (TWO[j], 2) if incoming else (ENDS[n], TWO[j])
            to = device(-ENDS[n], 0)
        else:
            at = (2, ENDS[j]) if incoming else (ENDS[j], ENDS[n])
            to = device(0, -ENDS[n])
        ref = rows_in.at[place(at), part(n)]
        return gather(4 + group * 8 + j * 4 + 2 + n, ref, ref, to)

    mine = pltpu.make_async_copy(own, rows_in.at[place((0, 0))], sem)
    for n in (0, 1):
        emit(n).start()
    for n in (0, 1):
        spread(0, 0, n).start()
    mine.start()
    for j in (0, 1):
        emit(j, True).wait_recv()
        pass_on(j).start()
        for n in (0, 1):
            spread(1, j, n).start()
    for n in (0, 1):
        pass_on(n, True).wait_recv()
    for n in (0, 1):
        spread(0, 1, n).start()
    for n in (2, 3):
        weight_copy(n, True).wait_recv()
    weight_copy(7).start()
    mine.wait()
    for n in (4, 5, 6, 7):
        weight_copy(n, True).wait_recv()

    def far(group, j):
        return (TWO[j], 2) if group == 0 else (2, ENDS[j])

    def near(group, j, side):
        return (ENDS[side], TWO[j]) if group == 0 else (ENDS[j], ENDS[side])

    def line(group, along_first):
        return (lambda d: device(d, 0)) if (group == 0) == along_first else (lambda d: device(0, d))

    def give_far(group, j, n):
        k = group * 4 + j * 2 + n
        return remote(
            sums.at[place(far(group, j)), part(n)],
            hold_q.at[k],
            q_send.at[k],
            q_recv.at[k],
            line(group, False)(ENDS[n]),
        )

    def give_near(group, j, side, late):
        k = group * 4 + j * 2 + side
        span = part(side if late else 1 - side)
        return remote(
            sums.at[place(near(group, j, side)), span],
            hold_r.at[k, span],
            r_send.at[2 * k + late],
            r_recv.at[2 * k + late],
            line(group, True)(ENDS[side]),
        )

    def give_across(n):
        return remote(
            sums.at[place((2, 0)), part(n)],
            hold_p.at[n],
            p_send.at[n],
            p_recv.at[n],
            device(ENDS[n], 0),
        )

    def give_back(side, late):
        span = part(side if late else 1 - side)
        return remote(
            sums.at[place((0, ENDS[side])), span],
            hold_d.at[side, span],
            d_send.at[2 * side + late],
            d_recv.at[2 * side + late],
            device(0, ENDS[side]),
        )

    PAIRS = [(group, j) for j in (0, 1) for group in (0, 1)]
    slot = lax.broadcasted_iota(jnp.int32, (SLOTS, rows), 0).astype(jnp.float32)

    def group_step(g, carry):
        for when, j in ((1, 0), (2, 1)):

            @pl.when(g == when)
            def _():
                for n in (0, 1):
                    for group in (0, 1):
                        spread(group, j, n, True).wait_recv()
                        relay(group, j, n).start()

        @pl.when(g == 3)
        def _():
            for group, j in PAIRS:
                for n in (0, 1):
                    relay(group, j, n, True).wait_recv()
            for group, j in PAIRS:
                for side in (0, 1):
                    give_near(group, j, side, 0).start()

        ids = []
        for j in range(BLOCKS):
            at = place(GROUPS[3][j])
            for k in range(3):
                at = jnp.where(g == k, place(GROUPS[k][j]), at)
            ids.append(at)

        def hits(j, e):
            return tables[ids[j], 2 + e : 3 + e, :] == slot

        def choice(j):
            both = jnp.concatenate([hits(j, 0), hits(j, 1)], axis=0)
            return jnp.where(both, 1.0, 0.0).astype(jnp.bfloat16)

        for j in range(BLOCKS):
            picked[j] = jnp.dot(
                choice(j), rows_in[ids[j]], preferred_element_type=jnp.float32
            ).astype(jnp.bfloat16)
        for e in (0, 1):
            chosen = picked[:, e * SLOTS : (e + 1) * SLOTS, :].reshape(BLOCKS * SLOTS, width)
            gate = jnp.dot(chosen, weights[e, 0], preferred_element_type=jnp.float32)
            up = jnp.dot(chosen, weights[e, 1], preferred_element_type=jnp.float32)
            units = (gate / (1.0 + jnp.exp(-gate)) * up).astype(jnp.bfloat16)
            result = lax.dot_general(
                units, weights[e, 2], (((1,), (1,)), ((), ())), preferred_element_type=jnp.float32
            )
            for j in range(BLOCKS):
                gain = jnp.sum(
                    jnp.where(hits(j, e), tables[ids[j], e : e + 1, :], 0.0),
                    axis=1,
                    keepdims=True,
                )
                made[j, e * SLOTS : (e + 1) * SLOTS, :] = (
                    result[j * SLOTS : (j + 1) * SLOTS, :] * gain
                ).astype(jnp.bfloat16)
        for j in range(BLOCKS):
            sums[ids[j]] = lax.dot_general(
                choice(j), made[j], (((0,), (0,)), ((), ())), preferred_element_type=jnp.float32
            ).astype(jnp.bfloat16)
        return carry

    lax.fori_loop(0, len(GROUPS), group_step, 0)

    for group, j in PAIRS:
        for n in (0, 1):
            give_far(group, j, n).start()

    def add(at, held):
        sums[at] = (sums[at].astype(jnp.float32) + held.astype(jnp.float32)).astype(jnp.bfloat16)

    for group, j in PAIRS:
        for side in (0, 1):
            k = group * 4 + j * 2 + side
            give_far(group, j, side).wait_recv()
            add((place(near(group, j, side)), part(side)), hold_q[k])
            give_near(group, j, side, 1).start()

    def total(group, j):
        for side in (0, 1):
            for late in (0, 1):
                give_near(group, j, side, late).wait_recv()
        at = place((TWO[j], 0) if group == 0 else (0, ENDS[j]))
        k = group * 4 + j * 2
        return at, (
            sums[at].astype(jnp.float32)
            + hold_r[k].astype(jnp.float32)
            + hold_r[k + 1].astype(jnp.float32)
        )

    at, value = total(0, 1)
    sums[at] = value.astype(jnp.bfloat16)
    for n in (0, 1):
        give_across(n).start()
    for side in (0, 1):
        at, value = total(1, side)
        sums[at] = value.astype(jnp.bfloat16)
        give_back(side, 0).start()
    _, value = total(0, 0)
    out_sum = value + residual[...]
    for side in (0, 1):
        give_across(side).wait_recv()
        add((place((0, ENDS[side])), part(side)), hold_p[side])
        give_back(side, 1).start()
    for side in (0, 1):
        for late in (0, 1):
            give_back(side, late).wait_recv()
    out[...] = (
        out_sum + hold_d[0].astype(jnp.float32) + hold_d[1].astype(jnp.float32)
    ).astype(out.dtype)

    for n in (0, 1):
        emit(n).wait_send()
        pass_on(n).wait_send()
        give_across(n).wait_send()
        for late in (0, 1):
            give_back(n, late).wait_send()
    for n in range(8):
        weight_copy(n).wait_send()
    for group, j in PAIRS:
        for n in (0, 1):
            spread(group, j, n).wait_send()
            relay(group, j, n).wait_send()
            give_far(group, j, n).wait_send()
            for late in (0, 1):
                give_near(group, j, n, late).wait_send()


def normed(values, gain):
    mean_square = jnp.mean(values * values, axis=1, keepdims=True)
    return (values * lax.rsqrt(mean_square + epsilon) * gain[None]).astype(jnp.bfloat16)


def rotation_tables(plane, prompt_start, cosine, sine):
    rows = prompt_start.shape[1]
    half = HEAD_SIZE // 2
    lane = lax.broadcasted_iota(jnp.int32, (rows, 128), 1)
    begin = jnp.broadcast_to(prompt_start[...].astype(jnp.float32), (rows, rows)).T
    first = (plane.chip(0, 0) * 2 + plane.core) * rows
    position = first + lax.broadcasted_iota(jnp.int32, (rows, 128), 0)
    power = lax.rem(lane, half).astype(jnp.float32) / half
    angle = (position.astype(jnp.float32) - begin) * jnp.exp(power * -math.log(10000.0))
    cosine[...] = jnp.cos(angle)
    sine[...] = jnp.where(lax.rem(lane, HEAD_SIZE) < half, -jnp.sin(angle), jnp.sin(angle))


def layer_kernel(
    hidden, attn_gain, wq, wk, wv, wo, prompt_start, ffn_gain, routes, route_weights,
    first,
    out, key_cache, value_cache,
    query_w, key_w, value_w, output_w, own_in, residual, cosine, sine,
    queries, pairs, starts, given, attention, tables,
    near, store, asked, begin, begins, packed, peak, total, bias, done, replies,
    rows_in, sums, weights, picked, made, hold_q, hold_r, hold_p, hold_d,
    *sems,
):
    attention_sems, expert_sems, (w_send, w_recv, load_sems, row_sem) = (
        sems[:11],
        sems[11:21],
        sems[21:],
    )
    plane = Plane()
    core = plane.core
    rows, width = hidden.shape
    arrived = greet(plane)

    def lanes(r):
        return pl.ds(r * 128, 128)

    def weight_copy(n, incoming=False):
        half = width // 2
        e = 1 - core if incoming and n >= 4 else core
        if n < 2:
            src, dst = first, weights.at[e, :, :, lanes(1 + n)]
            to = plane.level((1, -1)[n])
        elif n < 4:
            span = pl.ds((n - 2) * half, half)
            src = weights.at[e, :, span, lanes(n - 1)]
            dst = weights.at[e, :, span, lanes(3)]
            to = plane.level((1, -1)[n - 2])
        else:
            dst = weights.at[e, :, :, lanes(n - 4)]
            src = first if n == 4 else dst
            to = plane.partner()
        return remote(src, dst, w_send.at[n], w_recv.at[n], to)

    loads = [
        pltpu.make_async_copy(src, dst, load_sems.at[n])
        for n, (src, dst) in enumerate(
            (
                (wk, key_w),
                (wv, value_w),
                (wq, query_w),
                (wo, output_w),
                (first, weights.at[core, :, :, lanes(0)]),
            )
        )
    ]
    for load in loads[:2]:
        load.start()
    own_in[...] = normed(hidden[...].astype(jnp.float32), attn_gain[...])
    rotation_tables(plane, prompt_start, cosine, sine)
    arrived()
    for n in (0, 1, 4):
        weight_copy(n).start()

    lane = lax.broadcasted_iota(jnp.int32, (rows, 128), 1)
    first_half = lax.rem(lane, HEAD_SIZE) < HEAD_SIZE // 2

    def rotated(tile):
        other = jnp.where(
            first_half,
            pltpu.roll(tile, 128 - HEAD_SIZE // 2, axis=1),
            pltpu.roll(tile, HEAD_SIZE // 2, axis=1),
        )
        return tile * cosine[...] + other * sine[...]

    def project_keys():
        for load in loads[2:]:
            load.start()
        starts[...] = jnp.broadcast_to(prompt_start[...].astype(jnp.float32), starts.shape)
        loads[0].wait()
        keys = jnp.dot(own_in[...], key_w[...], preferred_element_type=jnp.float32)
        loads[1].wait()
        values = jnp.dot(own_in[...], value_w[...], preferred_element_type=jnp.float32)
        value_cache[...] = values.astype(jnp.bfloat16)
        low = lane < HEAD_SIZE
        for p in range(KEY_VALUE_HEADS // 2):
            at = slice(p * 128, (p + 1) * 128)
            key, value = rotated(keys[:, at]), values[:, at]
            key_cache[:, at] = key.astype(jnp.bfloat16)
            sides = (
                jnp.where(low, key, pltpu.roll(value, HEAD_SIZE, axis=1)),
                jnp.where(low, pltpu.roll(key, HEAD_SIZE, axis=1), value),
            )
            for c in (0, 1):
                to = (c * SIDE + p) * 128
                pairs[:, to : to + 128] = sides[c].astype(jnp.bfloat16)

    def project_queries():
        loads[2].wait()
        for c in range(3):
            part = jnp.dot(
                own_in[...],
                query_w[:, c * 512 : (c + 1) * 512],
                preferred_element_type=jnp.float32,
            )
            for p in range(4):
                at = c * 512 + p * 128
                queries[:, at : at + 128] = rotated(part[:, p * 128 : (p + 1) * 128]).astype(
                    jnp.bfloat16
                )

    def make_tables():
        expert = lax.broadcasted_iota(jnp.int32, (EXPERTS, rows), 0)
        gains = jnp.zeros((EXPERTS, rows), jnp.float32)
        named = jnp.zeros((EXPERTS, rows), jnp.float32)
        for j in range(TOP):
            hit = routes[j : j + 1, :] == expert
            gains = gains + jnp.where(hit, route_weights[j : j + 1, :], 0.0)
            named = named + jnp.where(hit, 1.0, 0.0)
        earlier = lax.broadcasted_iota(jnp.int32, (rows, rows), 0) < lax.broadcasted_iota(
            jnp.int32, (rows, rows), 1
        )
        ranks = jnp.dot(
            named.astype(jnp.bfloat16),
            jnp.where(earlier, 1.0, 0.0).astype(jnp.bfloat16),
            preferred_element_type=jnp.float32,
        )
        ranks = jnp.where(named > 0.0, ranks, -1.0)
        given[...] = jnp.zeros_like(given)
        for c in range(CHIPS):
            given[c, 0:2, :] = gains[2 * c : 2 * c + 2, :]
            given[c, 2:4, :] = ranks[2 * c : 2 * c + 2, :]

    attention_section(
        plane, weight_copy, project_keys, project_queries, make_tables,
        queries, pairs, starts, given, attention, tables,
        near, store, asked, begin, begins, packed, peak, total, bias, done, replies,
        *attention_sems,
    )

    loads[3].wait()
    for c in range(3):
        at = slice(c * 512, (c + 1) * 512)
        residual[:, at] = hidden[:, at].astype(jnp.float32) + jnp.dot(
            attention[...], output_w[:, at], preferred_element_type=jnp.float32
        )
    own_in[...] = normed(residual[...], ffn_gain[...])
    loads[4].wait()

    experts_section(
        plane, weight_copy, own_in, residual, tables, out,
        rows_in, sums, weights, picked, made, hold_q, hold_r, hold_p, hold_d,
        *expert_sems, row_sem,
    )


def run_layer(hidden, attn_gain, wq, wk, wv, wo, starts, ffn_gain, routes, gains, first):
    rows, width = hidden.shape
    cache = wk.shape[1]
    dma = pltpu.SemaphoreType.DMA
    vmem = pl.BlockSpec(memory_space=pltpu.VMEM)
    hbm = pl.BlockSpec(memory_space=pl.ANY)

    def brief(*shape):
        return pltpu.VMEM(shape, jnp.bfloat16)

    def full(*shape):
        return pltpu.VMEM(shape, jnp.float32)

    others = len(OTHERS)
    friends = len(FRIENDS)
    counts = (others, 6, 32, 2 * friends, friends)
    attention_sems = [dma((n,)) for n in counts for _ in (0, 1)] + [dma((8,))]
    expert_sems = [dma((n,)) for n in (20, 8, 16, 2, 4) for _ in (0, 1)]
    both = 2 * HEADS * rows
    return pl.pallas_call(
        layer_kernel,
        out_shape=(
            jax.ShapeDtypeStruct((rows, width), jnp.bfloat16),
            jax.ShapeDtypeStruct((rows, cache), jnp.bfloat16),
            jax.ShapeDtypeStruct((rows, cache), jnp.bfloat16),
        ),
        in_specs=[vmem, vmem, hbm, hbm, hbm, hbm] + [vmem] * 4 + [hbm],
        out_specs=(vmem,) * 3,
        scratch_shapes=[
            brief(*wq.shape),
            brief(*wk.shape),
            brief(*wv.shape),
            brief(*wo.shape),
            brief(rows, width),
            full(rows, width),
            full(rows, 128),
            full(rows, 128),
            brief(rows, width),
            brief(rows, 2 * cache),
            full(8, rows),
            full(CHIPS, 8, rows),
            brief(rows, width),
            full(CHIPS, 8, rows),
            brief(rows, 512),
            brief(CHIPS, 2 * rows, 128),
            brief(KEY_VALUE_HEADS, rows, ASK),
            full(KEY_VALUE_HEADS, 8, rows),
            full(KEY_VALUE_HEADS, rows, rows),
            brief(SIDE, both, 128),
            full(SIDE, both, 128),
            full(SIDE, both, 128),
            full(2 * rows, KEYS),
            brief(KEY_VALUE_HEADS, rows, ASK),
            brief(KEY_VALUE_HEADS, rows, ASK),
            brief(CHIPS, rows, width),
            brief(CHIPS, rows, width),
            brief(2, 3, width, FF),
            brief(BLOCKS, 2 * SLOTS, width),
            brief(BLOCKS, 2 * SLOTS, width),
            brief(8, rows // 2, width),
            brief(8, rows, width),
            brief(2, rows // 2, width),
            brief(2, rows, width),
            *attention_sems,
            *expert_sems,
            dma((8,)),
            dma((8,)),
            dma((5,)),
            dma,
        ],
        compiler_params=pltpu.CompilerParams(
            collective_id=0, has_side_effects=True, vmem_limit_bytes=63 << 20
        ),
        name="layer",
    )(
        hidden, attn_gain, wq, wk, wv, wo, starts, ffn_gain, routes, gains, first
    )


def publish(*results):
    def kernel(*refs):
        for src, dst in zip(refs[: len(results)], refs[len(results) :]):
            dst[...] = src[...]

    vmem = pl.BlockSpec(memory_space=pltpu.VMEM)
    return pl.pallas_call(
        kernel,
        out_shape=tuple(jax.ShapeDtypeStruct(r.shape, r.dtype) for r in results),
        in_specs=[vmem] * len(results),
        out_specs=(vmem,) * len(results),
        name="publish",
    )(*results)


def shards(
    hidden,
    attn_gain,
    query_weight,
    key_matrix,
    value_matrix,
    output_weight,
    prompt_start,
    ffn_gain,
    routes,
    route_weights,
    expert_weights,
):
    results = run_layer(
        hidden,
        attn_gain,
        query_weight,
        key_matrix,
        value_matrix,
        output_weight,
        prompt_start[None],
        ffn_gain,
        routes.T,
        route_weights.T,
        expert_weights[0],
    )
    return publish(*results)


def solution(mesh):
    in_specs = (
        P(("req", "exp"), None),
        P(),
        P(),
        P(),
        P(),
        P(),
        P(("req", "exp")),
        P(),
        P(("req", "exp"), None),
        P(("req", "exp"), None),
        P("exp", None, None, "req"),
    )
    out_specs = (P(("req", "exp"), None), P(("req", "exp"), None), P(("req", "exp"), None))
    return jax.shard_map(shards, mesh=mesh, in_specs=in_specs, out_specs=out_specs, check_vma=False)
```

```python
import math

import jax
import jax.numpy as jnp
from jax import lax
from jax.experimental import pallas as pl
from jax.experimental.pallas import tpu as pltpu
from jax.sharding import PartitionSpec as P

QUERY_HEADS = 24
KEY_VALUE_HEADS = 8
HEAD_SIZE = 64
TOP = 8
SIDE = 4
CHIPS = SIDE * SIDE
EXPERTS = 32
SLOTS = 64
FF = 512


epsilon = 1e-05


class Plane:
    def __init__(self):
        me = lax.axis_index("exp")
        self.core = lax.rem(me, 2)
        chip = lax.div(me, 2)
        self.y = lax.div(chip, SIDE)
        self.x = lax.rem(chip, SIDE)

    def chip(self, dy, dx):
        return lax.rem(self.y + dy + SIDE, SIDE) * SIDE + lax.rem(self.x + dx + SIDE, SIDE)

    def device(self, dy, dx):
        return {"exp": self.chip(dy, dx) * 2 + self.core}

    def level(self, dz):
        return {"req": lax.rem(lax.axis_index("req") + dz + SIDE, SIDE)}

    def partner(self):
        return {"exp": self.chip(0, 0) * 2 + 1 - self.core}

    def friend(self, dx, dc):
        x = lax.rem(self.x + dx + SIDE, SIDE)
        y = self.y if dx % 2 == 0 else SIDE - 1 - self.y
        core = 1 - self.core if dc else self.core
        return y * SIDE + x, core, 2 * x + core

    def friend_device(self, dx, dc):
        chip, core, _ = self.friend(dx, dc)
        return {"exp": chip * 2 + core}


FRIENDS = tuple((dx, dc) for dx in range(SIDE) for dc in (0, 1) if dx or dc)
OTHERS = tuple((dy, dx) for dy in range(SIDE) for dx in range(SIDE) if dy or dx)


def greet(plane):
    barrier = pltpu.get_barrier_semaphore()
    devices = [plane.device(dy, dx) for dy, dx in OTHERS]
    devices += [plane.friend_device(dx, 1) for dx in range(SIDE)]
    devices += [plane.level(1), plane.level(-1)]
    for device in devices:
        pl.semaphore_signal(
            barrier, inc=1, device_id=device, device_id_type=pl.DeviceIdType.MESH
        )
    return lambda: pl.semaphore_wait(barrier, len(devices))


def remote(src, dst, send, recv, device):
    return pltpu.make_async_remote_copy(
        src_ref=src,
        dst_ref=dst,
        send_sem=send,
        recv_sem=recv,
        device_id=device,
        device_id_type=pl.DeviceIdType.MESH,
    )


KEYS = 512
HEADS = QUERY_HEADS // KEY_VALUE_HEADS
ASK = 256
LOW = -1e30
SCALE = HEAD_SIZE**-0.5 * 1.4426950408889634
ACROSS = (0, -1, 1, 2)


def attention_section(
    plane, weight_copy, project_keys, project_queries, make_tables,
    queries, pairs, starts, given, out, held,
    near, store, asked, begin, begins, packed, peak, total, bias, done, replies,
    give, take, x_send, x_recv, y_send, y_recv, q_send, q_recv, o_send, o_recv, sems,
):
    core = plane.core
    here = plane.chip(0, 0)
    rows = queries.shape[0]
    mine = 2 * plane.x + core

    def lanes(at, size):
        return pl.ds(pl.multiple_of(at * size, size), size)

    swap = remote(
        pairs.at[:, lanes(1 - core, 512)], near, sems.at[0], sems.at[1], plane.partner()
    )

    def source(h, dx):
        x = lax.rem(plane.x + dx + SIDE, SIDE)
        if h == 0:
            return pairs.at[:, lanes(SIDE * core + x, 128)]
        return near.at[:, lanes(x, 128)]

    def slot(h, dy, dx, part=None):
        low = (core if h == 0 else 1 - core) * rows
        size = rows
        if part is not None:
            size = rows // 2
            low = low + part * size
        return store.at[plane.chip(dy, dx), pl.ds(pl.multiple_of(low, size), size)]

    def keep(h):
        return pltpu.make_async_copy(source(h, 0), slot(h, 0, 0), sems.at[2 + h])

    def across(h, n, incoming=False):
        dx = (1, -1, 2)[n]
        return remote(
            source(h, dx),
            slot(h, 0, -dx if incoming else 0),
            x_send.at[3 * h + n],
            x_recv.at[3 * h + n],
            plane.device(0, dx),
        )

    def along(h, i, n, incoming=False):
        dx = ACROSS[i]
        at, part, dy = ((0, None, 1), (0, None, -1), (-1, 0, 1), (1, 1, -1))[n]
        place = slot(h, at - dy if incoming else at, dx, part)
        src = source(h, 0) if (i == 0 and n < 2) else place
        if i == 0 and n < 2 and not incoming:
            place = slot(h, 0, 0)
        k = (h * 4 + i) * 4 + n
        return remote(src, place, y_send.at[k], y_recv.at[k], plane.device(dy, 0))

    def other(n, incoming):
        dx, dc = FRIENDS[n]
        return plane.friend(-dx if incoming else dx, dc)[2]

    def asking(head):
        return pl.ds(pl.multiple_of(lax.div(3 * head, 2) * 128, 128), ASK)

    def ask(n, incoming=False):
        return remote(
            queries.at[:, asking(other(n, False))],
            asked.at[other(n, True) if incoming else mine],
            q_send.at[n],
            q_recv.at[n],
            plane.friend_device(*FRIENDS[n]),
        )

    def tell(n, incoming=False):
        return remote(
            starts,
            begin.at[other(n, True) if incoming else mine],
            q_send.at[len(FRIENDS) + n],
            q_recv.at[len(FRIENDS) + n],
            plane.friend_device(*FRIENDS[n]),
        )

    def table(n, incoming=False):
        dy, dx = OTHERS[n]
        return remote(
            given.at[plane.chip(dy, dx)],
            held.at[plane.chip(-dy, -dx) if incoming else here],
            give.at[n],
            take.at[n],
            plane.device(dy, dx),
        )

    own_asked = pltpu.make_async_copy(
        queries.at[:, asking(mine)], asked.at[mine], sems.at[4]
    )
    own_begin = pltpu.make_async_copy(starts, begin.at[mine], sems.at[5])
    own_table = pltpu.make_async_copy(given.at[here], held.at[here], sems.at[6])

    project_keys()
    swap.start()
    for h in (0, 1):
        if h == 1:
            make_tables()
            own_begin.start()
            own_table.start()
            swap.wait_recv()
        keep(h).start()
        for n in range(3):
            across(h, n).start()
        along(h, 0, 0).start()
        along(h, 0, 1).start()
    project_queries()
    own_asked.start()
    for n in range(len(FRIENDS)):
        ask(n).start()
        tell(n).start()
    for n in range(3):
        i = (1, 2, 3)[n]
        for h in (0, 1):
            across(h, n, True).wait_recv()
            along(h, i, 0).start()
            along(h, i, 1).start()
    for n in range(len(OTHERS)):
        table(n).start()

    own_asked.wait()
    own_begin.wait()
    for n in range(len(FRIENDS)):
        ask(n, True).wait_recv()
        tell(n, True).wait_recv()
    for h in (0, 1):
        keep(h).wait()

    lane = lax.broadcasted_iota(jnp.int32, (rows, 128), 1)
    low = lane < HEAD_SIZE
    upper = core == 1
    for which in range(SIDE):
        for side in (0, 1):
            begins[2 * which + side] = jnp.broadcast_to(
                begin[2 * which + side, 0:1, :], (rows, rows)
            ).T
            tiles = [
                asked[2 * which + side, :, i * 128 : (i + 1) * 128].astype(jnp.float32)
                for i in (0, 1)
            ]
            turned = [pltpu.roll(tile, HEAD_SIZE, axis=1) for tile in tiles]
            heads = (
                jnp.where(upper, turned[0], tiles[0]),
                jnp.where(upper, tiles[1], turned[0]),
                jnp.where(upper, turned[1], tiles[1]),
            )
            for n in range(HEADS):
                at = (n * 2 + side) * rows
                packed[which, at : at + rows, :] = jnp.where(low, heads[n], 0.0).astype(
                    jnp.bfloat16
                )
    peak[...] = jnp.full_like(peak, LOW)
    total[...] = jnp.zeros_like(total)
    both = 2 * HEADS * rows
    lane_number = lax.broadcasted_iota(jnp.int32, (1, 128), 1).astype(jnp.float32)
    row_number = lax.broadcasted_iota(jnp.int32, (rows, 128), 0).astype(jnp.float32)

    def member(which):
        flip = lax.rem(plane.x + which, 2)
        return jnp.where(flip == 0, plane.y, SIDE - 1 - plane.y) * SIDE + which

    def visit(which, chip):
        stream_chip = member(which)
        at = chip * (2 * rows)
        shift = (stream_chip * (2 * rows) - at).astype(jnp.float32)
        base = at.astype(jnp.float32)
        for side in (0, 1):
            first = begins[2 * which + side] - base
            last = row_number + (shift + side * rows)
            for j in range(KEYS // 128):
                key_number = lane_number + j * 128
                bias[side * rows : (side + 1) * rows, j * 128 : (j + 1) * 128] = jnp.where(
                    (key_number >= first) & (key_number <= last), 0.0, LOW
                )
        tile = store[pl.ds(chip, 2)].reshape(KEYS, 128)
        scores = lax.dot_general(
            packed[which], tile, (((1,), (1,)), ((), ())), preferred_element_type=jnp.float32
        )
        scores = (scores.reshape(HEADS, 2 * rows, KEYS) + bias[...][None]).reshape(both, KEYS)
        before = peak[which]
        now = jnp.maximum(before, jnp.max(scores, axis=1, keepdims=True))
        peak[which] = now
        fade = jnp.exp2((before - now) * SCALE)
        wide = jnp.concatenate([now] * (KEYS // 128), axis=1)
        probs = jnp.exp2((scores - wide) * SCALE).astype(jnp.bfloat16)
        value_lane = lax.broadcasted_iota(jnp.int32, (KEYS, 128), 1) >= HEAD_SIZE
        beside = jnp.where(value_lane, tile, jnp.ones_like(tile))
        total[which] = total[which] * fade + jnp.dot(
            probs, beside, preferred_element_type=jnp.float32
        )

    def answer(which):
        for side in (0, 1):
            high, turned = [], []
            for n in range(HEADS):
                at = (n * 2 + side) * rows
                sums_here = total[which, at : at + rows, :]
                high.append(sums_here / pltpu.roll(sums_here, HEAD_SIZE, axis=1))
                turned.append(pltpu.roll(high[n], HEAD_SIZE, axis=1))
            tiles = (
                jnp.where(upper, high[0], jnp.where(low, turned[0], high[1])),
                jnp.where(upper, jnp.where(low, turned[1], high[2]), turned[2]),
            )
            for i in (0, 1):
                done[2 * which + side, :, i * 128 : (i + 1) * 128] = tiles[i].astype(jnp.bfloat16)

    def reply(n, incoming=False):
        return remote(
            done.at[other(n, False)],
            replies.at[other(n, True) if incoming else mine],
            o_send.at[n],
            o_recv.at[n],
            plane.friend_device(*FRIENDS[n]),
        )

    own_reply = pltpu.make_async_copy(done.at[mine], replies.at[mine], sems.at[7])

    def phase(step, carry):
        @pl.when(step == 1)
        def _():
            for i in range(4):
                for n in (0, 1):
                    for h in (0, 1):
                        along(h, i, n, True).wait_recv()
                        along(h, i, n + 2).start()

        @pl.when(step == 3)
        def _():
            for i in range(4):
                for n in (2, 3):
                    for h in (0, 1):
                        along(h, i, n, True).wait_recv()

        dy = jnp.where(step == 0, 0, jnp.where(step == 1, SIDE - 1, step - 1))
        dy = jnp.where(step == 3, 2, dy)
        row = lax.rem(plane.y + dy, SIDE) * SIDE

        def one(t, carry):
            turn, part = lax.div(t, 2), lax.rem(t, 2)
            dx = jnp.where(turn == 0, 2, jnp.where(turn == 1, 1, jnp.where(turn == 2, 3, 0)))
            which = lax.rem(plane.x + dx, SIDE)
            chip = row + 2 * part

            @pl.when(chip <= member(which))
            def _():
                visit(which, chip)

            @pl.when((step == 3) & (part == 1))
            def _():
                answer(which)

            for column in range(SIDE):

                @pl.when((step == 3) & (part == 1) & (dx == column))
                def _():
                    for n, friend in enumerate(FRIENDS):
                        if friend[0] == column:
                            reply(n).start()
                    if column == 0:
                        own_reply.start()

            return carry

        return lax.fori_loop(0, 2 * SIDE, one, carry)

    lax.fori_loop(0, 4, phase, 0)

    for n in (0, 1):
        weight_copy(n, True).wait_recv()
        weight_copy(2 + n).start()
        weight_copy(5 + n).start()

    swap.wait_send()
    own_table.wait()
    for h in (0, 1):
        for n in range(3):
            across(h, n).wait_send()
        for i in range(4):
            for n in range(4):
                along(h, i, n).wait_send()
    for n in range(len(FRIENDS)):
        ask(n).wait_send()
        tell(n).wait_send()
    for n in range(len(OTHERS)):
        table(n, True).wait_recv()
        table(n).wait_send()
    own_reply.wait()
    for n in range(len(FRIENDS)):
        reply(n, True).wait_recv()
        reply(n).wait_send()
    for p in range(KEY_VALUE_HEADS // 2):
        even, odd = replies[2 * p], replies[2 * p + 1]
        out[:, p * 384 : p * 384 + 128] = even[:, :128]
        out[:, p * 384 + 128 : p * 384 + 256] = jnp.where(
            low, even[:, 128:].astype(jnp.float32), odd[:, :128].astype(jnp.float32)
        ).astype(jnp.bfloat16)
        out[:, p * 384 + 256 : p * 384 + 384] = odd[:, 128:]


BLOCKS = 4
GROUPS = (
    ((0, 0), (2, 0), (0, -1), (0, 1)),
    ((-1, 0), (1, 0), (-1, -1), (-1, 1)),
    ((-1, 2), (1, 2), (1, -1), (1, 1)),
    ((0, 2), (2, 2), (2, -1), (2, 1)),
)
TWO = (0, 2)
ENDS = (-1, 1)


def experts_section(
    plane, weight_copy, own, residual, tables, out,
    rows_in, sums, weights, picked, made, hold_q, hold_r, hold_p, hold_d,
    g_send, g_recv, q_send, q_recv, r_send, r_recv, p_send, p_recv, d_send, d_recv, sem,
):
    rows, width = own.shape
    part_rows = rows // 2
    even = lax.rem(plane.y + plane.x, 2) == 0

    def turned(o, t):
        return jnp.where(even, t, o), jnp.where(even, o, t)

    def place(at):
        return plane.chip(*turned(*at))

    def device(o, t):
        return plane.device(*turned(o, t))

    def part(n):
        return pl.ds(n * part_rows, part_rows)

    def gather(k, src, dst, to):
        return remote(src, dst, g_send.at[k], g_recv.at[k], to)

    def emit(n, incoming=False):
        d = (1, -1)[n]
        at = (0, -d) if incoming else (0, 0)
        return gather(n, own, rows_in.at[place(at)], device(d, 0))

    def pass_on(n, incoming=False):
        at = (2, 0) if incoming else (0, ENDS[n])
        ref = rows_in.at[place(at), part(n)]
        return gather(2 + n, ref, ref, device(0, -ENDS[n]))

    def spread(group, j, n, incoming=False):
        d = (1, -1)[n]
        if group == 0:
            at = (-d, TWO[j]) if incoming else (TWO[j], 0)
            to = device(0, d)
        else:
            at = (ENDS[j], -d) if incoming else (0, ENDS[j])
            to = device(d, 0)
        ref = rows_in.at[place(at)]
        src = own if at == (0, 0) else ref
        return gather(4 + group * 8 + j * 4 + n, src, ref, to)

    def relay(group, j, n, incoming=False):
        if group == 0:
            at = (TWO[j], 2) if incoming else (ENDS[n], TWO[j])
            to = device(-ENDS[n], 0)
        else:
            at = (2, ENDS[j]) if incoming else (ENDS[j], ENDS[n])
            to = device(0, -ENDS[n])
        ref = rows_in.at[place(at), part(n)]
        return gather(4 + group * 8 + j * 4 + 2 + n, ref, ref, to)

    mine = pltpu.make_async_copy(own, rows_in.at[place((0, 0))], sem)
    for n in (0, 1):
        emit(n).start()
    for n in (0, 1):
        spread(0, 0, n).start()
    mine.start()
    for j in (0, 1):
        emit(j, True).wait_recv()
        pass_on(j).start()
        for n in (0, 1):
            spread(1, j, n).start()
    for n in (0, 1):
        pass_on(n, True).wait_recv()
    for n in (0, 1):
        spread(0, 1, n).start()
    for n in (2, 3):
        weight_copy(n, True).wait_recv()
    weight_copy(7).start()
    mine.wait()
    for n in (4, 5, 6, 7):
        weight_copy(n, True).wait_recv()

    def far(group, j):
        return (TWO[j], 2) if group == 0 else (2, ENDS[j])

    def near(group, j, side):
        return (ENDS[side], TWO[j]) if group == 0 else (ENDS[j], ENDS[side])

    def line(group, along_first):
        return (lambda d: device(d, 0)) if (group == 0) == along_first else (lambda d: device(0, d))

    def give_far(group, j, n):
        k = group * 4 + j * 2 + n
        return remote(
            sums.at[place(far(group, j)), part(n)],
            hold_q.at[k],
            q_send.at[k],
            q_recv.at[k],
            line(group, False)(ENDS[n]),
        )

    def give_near(group, j, side, late):
        k = group * 4 + j * 2 + side
        span = part(side if late else 1 - side)
        return remote(
            sums.at[place(near(group, j, side)), span],
            hold_r.at[k, span],
            r_send.at[2 * k + late],
            r_recv.at[2 * k + late],
            line(group, True)(ENDS[side]),
        )

    def give_across(n):
        return remote(
            sums.at[place((2, 0)), part(n)],
            hold_p.at[n],
            p_send.at[n],
            p_recv.at[n],
            device(ENDS[n], 0),
        )

    def give_back(side, late):
        span = part(side if late else 1 - side)
        return remote(
            sums.at[place((0, ENDS[side])), span],
            hold_d.at[side, span],
            d_send.at[2 * side + late],
            d_recv.at[2 * side + late],
            device(0, ENDS[side]),
        )

    PAIRS = [(0, 1), (1, 0), (1, 1), (0, 0)]
    slot = lax.broadcasted_iota(jnp.int32, (SLOTS, rows), 0).astype(jnp.float32)

    def group_step(g, carry):
        for when, j in ((1, 0), (2, 1)):

            @pl.when(g == when)
            def _():
                for n in (0, 1):
                    for group in (0, 1):
                        spread(group, j, n, True).wait_recv()
                        relay(group, j, n).start()

        @pl.when(g == 3)
        def _():
            for group, j in PAIRS:
                for n in (0, 1):
                    relay(group, j, n, True).wait_recv()
            for group, j in PAIRS:
                for side in (0, 1):
                    give_near(group, j, side, 0).start()

        ids = []
        for j in range(BLOCKS):
            at = place(GROUPS[3][j])
            for k in range(3):
                at = jnp.where(g == k, place(GROUPS[k][j]), at)
            ids.append(at)

        def hits(j, e):
            return tables[ids[j], 2 + e : 3 + e, :] == slot

        def choice(j):
            both = jnp.concatenate([hits(j, 0), hits(j, 1)], axis=0)
            return jnp.where(both, 1.0, 0.0).astype(jnp.bfloat16)

        for j in range(BLOCKS):
            picked[j] = jnp.dot(
                choice(j), rows_in[ids[j]], preferred_element_type=jnp.float32
            ).astype(jnp.bfloat16)
        for e in (0, 1):
            chosen = picked[:, e * SLOTS : (e + 1) * SLOTS, :].reshape(BLOCKS * SLOTS, width)
            gate = jnp.dot(chosen, weights[e, 0], preferred_element_type=jnp.float32)
            up = jnp.dot(chosen, weights[e, 1], preferred_element_type=jnp.float32)
            units = (gate / (1.0 + jnp.exp(-gate)) * up).astype(jnp.bfloat16)
            result = lax.dot_general(
                units, weights[e, 2], (((1,), (1,)), ((), ())), preferred_element_type=jnp.float32
            )
            for j in range(BLOCKS):
                gain = jnp.sum(
                    jnp.where(hits(j, e), tables[ids[j], e : e + 1, :], 0.0),
                    axis=1,
                    keepdims=True,
                )
                made[j, e * SLOTS : (e + 1) * SLOTS, :] = (
                    result[j * SLOTS : (j + 1) * SLOTS, :] * gain
                ).astype(jnp.bfloat16)
        for j in range(BLOCKS):
            sums[ids[j]] = lax.dot_general(
                choice(j), made[j], (((0,), (0,)), ((), ())), preferred_element_type=jnp.float32
            ).astype(jnp.bfloat16)
        return carry

    lax.fori_loop(0, len(GROUPS), group_step, 0)

    for group, j in PAIRS:
        for n in (0, 1):
            give_far(group, j, n).start()

    def add(at, held):
        sums[at] = (sums[at].astype(jnp.float32) + held.astype(jnp.float32)).astype(jnp.bfloat16)

    def relay_sums(group, j):
        for side in (0, 1):
            k = group * 4 + j * 2 + side
            give_far(group, j, side).wait_recv()
            add((place(near(group, j, side)), part(side)), hold_q[k])
            give_near(group, j, side, 1).start()

    def total(group, j):
        for side in (0, 1):
            for late in (0, 1):
                give_near(group, j, side, late).wait_recv()
        at = place((TWO[j], 0) if group == 0 else (0, ENDS[j]))
        k = group * 4 + j * 2
        return at, (
            sums[at].astype(jnp.float32)
            + hold_r[k].astype(jnp.float32)
            + hold_r[k + 1].astype(jnp.float32)
        )

    for group, j in PAIRS[:3]:
        relay_sums(group, j)
    at, value = total(0, 1)
    sums[at] = value.astype(jnp.bfloat16)
    for n in (0, 1):
        give_across(n).start()
    relay_sums(0, 0)
    for side in (0, 1):
        at, value = total(1, side)
        sums[at] = value.astype(jnp.bfloat16)
        give_back(side, 0).start()
    for side in (0, 1):
        give_across(side).wait_recv()
        add((place((0, ENDS[side])), part(side)), hold_p[side])
        give_back(side, 1).start()
    _, value = total(0, 0)
    out_sum = value + residual[...]
    for side in (0, 1):
        for late in (0, 1):
            give_back(side, late).wait_recv()
    out[...] = (
        out_sum + hold_d[0].astype(jnp.float32) + hold_d[1].astype(jnp.float32)
    ).astype(out.dtype)

    for n in (0, 1):
        emit(n).wait_send()
        pass_on(n).wait_send()
        give_across(n).wait_send()
        for late in (0, 1):
            give_back(n, late).wait_send()
    for n in range(8):
        weight_copy(n).wait_send()
    for group, j in PAIRS:
        for n in (0, 1):
            spread(group, j, n).wait_send()
            relay(group, j, n).wait_send()
            give_far(group, j, n).wait_send()
            for late in (0, 1):
                give_near(group, j, n, late).wait_send()


def normed(values, gain):
    mean_square = jnp.mean(values * values, axis=1, keepdims=True)
    return (values * lax.rsqrt(mean_square + epsilon) * gain[None]).astype(jnp.bfloat16)


def rotation_tables(plane, prompt_start, cosine, sine):
    rows = prompt_start.shape[1]
    half = HEAD_SIZE // 2
    lane = lax.broadcasted_iota(jnp.int32, (rows, 128), 1)
    begin = jnp.broadcast_to(prompt_start[...].astype(jnp.float32), (rows, rows)).T
    first = (plane.chip(0, 0) * 2 + plane.core) * rows
    position = first + lax.broadcasted_iota(jnp.int32, (rows, 128), 0)
    power = lax.rem(lane, half).astype(jnp.float32) / half
    angle = (position.astype(jnp.float32) - begin) * jnp.exp(power * -math.log(10000.0))
    cosine[...] = jnp.cos(angle)
    sine[...] = jnp.where(lax.rem(lane, HEAD_SIZE) < half, -jnp.sin(angle), jnp.sin(angle))


def layer_kernel(
    hidden, attn_gain, wq, wk, wv, wo, prompt_start, ffn_gain, routes, route_weights,
    first,
    out, key_cache, value_cache,
    query_w, key_w, value_w, output_w, own_in, residual, cosine, sine,
    queries, pairs, starts, given, attention, tables,
    near, store, asked, begin, begins, packed, peak, total, bias, done, replies,
    rows_in, sums, weights, picked, made, hold_q, hold_r, hold_p, hold_d,
    *sems,
):
    attention_sems, expert_sems, (w_send, w_recv, load_sems, row_sem) = (
        sems[:11],
        sems[11:21],
        sems[21:],
    )
    plane = Plane()
    core = plane.core
    rows, width = hidden.shape
    arrived = greet(plane)

    def lanes(r):
        return pl.ds(r * 128, 128)

    def weight_copy(n, incoming=False):
        half = width // 2
        e = 1 - core if incoming and n >= 4 else core
        if n < 2:
            src, dst = first, weights.at[e, :, :, lanes(1 + n)]
            to = plane.level((1, -1)[n])
        elif n < 4:
            span = pl.ds((n - 2) * half, half)
            src = weights.at[e, :, span, lanes(n - 1)]
            dst = weights.at[e, :, span, lanes(3)]
            to = plane.level((1, -1)[n - 2])
        else:
            dst = weights.at[e, :, :, lanes(n - 4)]
            src = first if n == 4 else dst
            to = plane.partner()
        return remote(src, dst, w_send.at[n], w_recv.at[n], to)

    loads = [
        pltpu.make_async_copy(src, dst, load_sems.at[n])
        for n, (src, dst) in enumerate(
            (
                (wk, key_w),
                (wv, value_w),
                (wq, query_w),
                (wo, output_w),
                (first, weights.at[core, :, :, lanes(0)]),
            )
        )
    ]
    for load in loads[:2]:
        load.start()
    own_in[...] = normed(hidden[...].astype(jnp.float32), attn_gain[...])
    rotation_tables(plane, prompt_start, cosine, sine)
    arrived()
    for n in (0, 1, 4):
        weight_copy(n).start()

    lane = lax.broadcasted_iota(jnp.int32, (rows, 128), 1)
    first_half = lax.rem(lane, HEAD_SIZE) < HEAD_SIZE // 2

    def rotated(tile):
        other = jnp.where(
            first_half,
            pltpu.roll(tile, 128 - HEAD_SIZE // 2, axis=1),
            pltpu.roll(tile, HEAD_SIZE // 2, axis=1),
        )
        return tile * cosine[...] + other * sine[...]

    def project_keys():
        for load in loads[2:]:
            load.start()
        starts[...] = jnp.broadcast_to(prompt_start[...].astype(jnp.float32), starts.shape)
        loads[0].wait()
        keys = jnp.dot(own_in[...], key_w[...], preferred_element_type=jnp.float32)
        loads[1].wait()
        values = jnp.dot(own_in[...], value_w[...], preferred_element_type=jnp.float32)
        value_cache[...] = values.astype(jnp.bfloat16)
        low = lane < HEAD_SIZE
        for p in range(KEY_VALUE_HEADS // 2):
            at = slice(p * 128, (p + 1) * 128)
            key, value = rotated(keys[:, at]), values[:, at]
            key_cache[:, at] = key.astype(jnp.bfloat16)
            sides = (
                jnp.where(low, key, pltpu.roll(value, HEAD_SIZE, axis=1)),
                jnp.where(low, pltpu.roll(key, HEAD_SIZE, axis=1), value),
            )
            for c in (0, 1):
                to = (c * SIDE + p) * 128
                pairs[:, to : to + 128] = sides[c].astype(jnp.bfloat16)

    def project_queries():
        loads[2].wait()
        for c in range(3):
            part = jnp.dot(
                own_in[...],
                query_w[:, c * 512 : (c + 1) * 512],
                preferred_element_type=jnp.float32,
            )
            for p in range(4):
                at = c * 512 + p * 128
                queries[:, at : at + 128] = rotated(part[:, p * 128 : (p + 1) * 128]).astype(
                    jnp.bfloat16
                )

    def make_tables():
        expert = lax.broadcasted_iota(jnp.int32, (EXPERTS, rows), 0)
        gains = jnp.zeros((EXPERTS, rows), jnp.float32)
        named = jnp.zeros((EXPERTS, rows), jnp.float32)
        for j in range(TOP):
            hit = routes[j : j + 1, :] == expert
            gains = gains + jnp.where(hit, route_weights[j : j + 1, :], 0.0)
            named = named + jnp.where(hit, 1.0, 0.0)
        earlier = lax.broadcasted_iota(jnp.int32, (rows, rows), 0) < lax.broadcasted_iota(
            jnp.int32, (rows, rows), 1
        )
        ranks = jnp.dot(
            named.astype(jnp.bfloat16),
            jnp.where(earlier, 1.0, 0.0).astype(jnp.bfloat16),
            preferred_element_type=jnp.float32,
        )
        ranks = jnp.where(named > 0.0, ranks, -1.0)
        given[...] = jnp.zeros_like(given)
        for c in range(CHIPS):
            given[c, 0:2, :] = gains[2 * c : 2 * c + 2, :]
            given[c, 2:4, :] = ranks[2 * c : 2 * c + 2, :]

    attention_section(
        plane, weight_copy, project_keys, project_queries, make_tables,
        queries, pairs, starts, given, attention, tables,
        near, store, asked, begin, begins, packed, peak, total, bias, done, replies,
        *attention_sems,
    )

    loads[3].wait()
    for c in range(3):
        at = slice(c * 512, (c + 1) * 512)
        residual[:, at] = hidden[:, at].astype(jnp.float32) + jnp.dot(
            attention[...], output_w[:, at], preferred_element_type=jnp.float32
        )
    own_in[...] = normed(residual[...], ffn_gain[...])
    loads[4].wait()

    experts_section(
        plane, weight_copy, own_in, residual, tables, out,
        rows_in, sums, weights, picked, made, hold_q, hold_r, hold_p, hold_d,
        *expert_sems, row_sem,
    )


def run_layer(hidden, attn_gain, wq, wk, wv, wo, starts, ffn_gain, routes, gains, first):
    rows, width = hidden.shape
    cache = wk.shape[1]
    dma = pltpu.SemaphoreType.DMA
    vmem = pl.BlockSpec(memory_space=pltpu.VMEM)
    hbm = pl.BlockSpec(memory_space=pl.ANY)

    def brief(*shape):
        return pltpu.VMEM(shape, jnp.bfloat16)

    def full(*shape):
        return pltpu.VMEM(shape, jnp.float32)

    others = len(OTHERS)
    friends = len(FRIENDS)
    counts = (others, 6, 32, 2 * friends, friends)
    attention_sems = [dma((n,)) for n in counts for _ in (0, 1)] + [dma((8,))]
    expert_sems = [dma((n,)) for n in (20, 8, 16, 2, 4) for _ in (0, 1)]
    both = 2 * HEADS * rows
    return pl.pallas_call(
        layer_kernel,
        out_shape=(
            jax.ShapeDtypeStruct((rows, width), jnp.bfloat16),
            jax.ShapeDtypeStruct((rows, cache), jnp.bfloat16),
            jax.ShapeDtypeStruct((rows, cache), jnp.bfloat16),
        ),
        in_specs=[vmem, vmem, hbm, hbm, hbm, hbm] + [vmem] * 4 + [hbm],
        out_specs=(vmem,) * 3,
        scratch_shapes=[
            brief(*wq.shape),
            brief(*wk.shape),
            brief(*wv.shape),
            brief(*wo.shape),
            brief(rows, width),
            full(rows, width),
            full(rows, 128),
            full(rows, 128),
            brief(rows, width),
            brief(rows, 2 * cache),
            full(8, rows),
            full(CHIPS, 8, rows),
            brief(rows, width),
            full(CHIPS, 8, rows),
            brief(rows, 512),
            brief(CHIPS, 2 * rows, 128),
            brief(KEY_VALUE_HEADS, rows, ASK),
            full(KEY_VALUE_HEADS, 8, rows),
            full(KEY_VALUE_HEADS, rows, rows),
            brief(SIDE, both, 128),
            full(SIDE, both, 128),
            full(SIDE, both, 128),
            full(2 * rows, KEYS),
            brief(KEY_VALUE_HEADS, rows, ASK),
            brief(KEY_VALUE_HEADS, rows, ASK),
            brief(CHIPS, rows, width),
            brief(CHIPS, rows, width),
            brief(2, 3, width, FF),
            brief(BLOCKS, 2 * SLOTS, width),
            brief(BLOCKS, 2 * SLOTS, width),
            brief(8, rows // 2, width),
            brief(8, rows, width),
            brief(2, rows // 2, width),
            brief(2, rows, width),
            *attention_sems,
            *expert_sems,
            dma((8,)),
            dma((8,)),
            dma((5,)),
            dma,
        ],
        compiler_params=pltpu.CompilerParams(
            collective_id=0, has_side_effects=True, vmem_limit_bytes=63 << 20
        ),
        name="layer",
    )(
        hidden, attn_gain, wq, wk, wv, wo, starts, ffn_gain, routes, gains, first
    )


def publish(*results):
    def kernel(*refs):
        for src, dst in zip(refs[: len(results)], refs[len(results) :]):
            dst[...] = src[...]

    vmem = pl.BlockSpec(memory_space=pltpu.VMEM)
    return pl.pallas_call(
        kernel,
        out_shape=tuple(jax.ShapeDtypeStruct(r.shape, r.dtype) for r in results),
        in_specs=[vmem] * len(results),
        out_specs=(vmem,) * len(results),
        name="publish",
    )(*results)


def shards(
    hidden,
    attn_gain,
    query_weight,
    key_matrix,
    value_matrix,
    output_weight,
    prompt_start,
    ffn_gain,
    routes,
    route_weights,
    expert_weights,
):
    results = run_layer(
        hidden,
        attn_gain,
        query_weight,
        key_matrix,
        value_matrix,
        output_weight,
        prompt_start[None],
        ffn_gain,
        routes.T,
        route_weights.T,
        expert_weights[0],
    )
    return publish(*results)


def solution(mesh):
    in_specs = (
        P(("req", "exp"), None),
        P(),
        P(),
        P(),
        P(),
        P(),
        P(("req", "exp")),
        P(),
        P(("req", "exp"), None),
        P(("req", "exp"), None),
        P("exp", None, None, "req"),
    )
    out_specs = (P(("req", "exp"), None), P(("req", "exp"), None), P(("req", "exp"), None))
    return jax.shard_map(shards, mesh=mesh, in_specs=in_specs, out_specs=out_specs, check_vma=False)
```

```python
import math

import jax
import jax.numpy as jnp
from jax import lax
from jax.experimental import pallas as pl
from jax.experimental.pallas import tpu as pltpu
from jax.sharding import PartitionSpec as P

QUERY_HEADS = 24
KEY_VALUE_HEADS = 8
HEAD_SIZE = 64
TOP = 8
SIDE = 4
CHIPS = SIDE * SIDE
EXPERTS = 32
SLOTS = 64
FF = 512


epsilon = 1e-05


class Plane:
    def __init__(self):
        me = lax.axis_index("exp")
        self.core = lax.rem(me, 2)
        chip = lax.div(me, 2)
        self.y = lax.div(chip, SIDE)
        self.x = lax.rem(chip, SIDE)

    def chip(self, dy, dx):
        return lax.rem(self.y + dy + SIDE, SIDE) * SIDE + lax.rem(self.x + dx + SIDE, SIDE)

    def device(self, dy, dx):
        return {"exp": self.chip(dy, dx) * 2 + self.core}

    def level(self, dz):
        return {"req": lax.rem(lax.axis_index("req") + dz + SIDE, SIDE)}

    def partner(self):
        return {"exp": self.chip(0, 0) * 2 + 1 - self.core}

    def friend(self, dx, dc):
        x = lax.rem(self.x + dx + SIDE, SIDE)
        y = self.y if dx % 2 == 0 else SIDE - 1 - self.y
        core = 1 - self.core if dc else self.core
        return y * SIDE + x, core, 2 * x + core

    def friend_device(self, dx, dc):
        chip, core, _ = self.friend(dx, dc)
        return {"exp": chip * 2 + core}


FRIENDS = tuple((dx, dc) for dx in range(SIDE) for dc in (0, 1) if dx or dc)
OTHERS = tuple((dy, dx) for dy in range(SIDE) for dx in range(SIDE) if dy or dx)


def greet(plane):
    barrier = pltpu.get_barrier_semaphore()
    devices = [plane.device(dy, dx) for dy, dx in OTHERS]
    devices += [plane.friend_device(dx, 1) for dx in range(SIDE)]
    devices += [plane.level(1), plane.level(-1)]
    for device in devices:
        pl.semaphore_signal(
            barrier, inc=1, device_id=device, device_id_type=pl.DeviceIdType.MESH
        )
    return lambda: pl.semaphore_wait(barrier, len(devices))


def remote(src, dst, send, recv, device):
    return pltpu.make_async_remote_copy(
        src_ref=src,
        dst_ref=dst,
        send_sem=send,
        recv_sem=recv,
        device_id=device,
        device_id_type=pl.DeviceIdType.MESH,
    )


KEYS = 512
HEADS = QUERY_HEADS // KEY_VALUE_HEADS
ASK = 256
LOW = -1e30
SCALE = HEAD_SIZE**-0.5 * 1.4426950408889634
ACROSS = (0, -1, 1, 2)


def attention_section(
    plane, weight_copy, project_keys, project_queries, make_tables,
    queries, pairs, starts, given, out, held,
    near, store, asked, begin, begins, packed, peak, total, bias, done, replies,
    give, take, x_send, x_recv, y_send, y_recv, q_send, q_recv, o_send, o_recv, sems,
):
    core = plane.core
    here = plane.chip(0, 0)
    rows = queries.shape[0]
    mine = 2 * plane.x + core

    def lanes(at, size):
        return pl.ds(pl.multiple_of(at * size, size), size)

    swap = remote(
        pairs.at[:, lanes(1 - core, 512)], near, sems.at[0], sems.at[1], plane.partner()
    )

    def source(h, dx):
        x = lax.rem(plane.x + dx + SIDE, SIDE)
        if h == 0:
            return pairs.at[:, lanes(SIDE * core + x, 128)]
        return near.at[:, lanes(x, 128)]

    def slot(h, dy, dx, part=None):
        low = (core if h == 0 else 1 - core) * rows
        size = rows
        if part is not None:
            size = rows // 2
            low = low + part * size
        return store.at[plane.chip(dy, dx), pl.ds(pl.multiple_of(low, size), size)]

    def keep(h):
        return pltpu.make_async_copy(source(h, 0), slot(h, 0, 0), sems.at[2 + h])

    def across(h, n, incoming=False):
        dx = (1, -1, 2)[n]
        return remote(
            source(h, dx),
            slot(h, 0, -dx if incoming else 0),
            x_send.at[3 * h + n],
            x_recv.at[3 * h + n],
            plane.device(0, dx),
        )

    def along(h, i, n, incoming=False):
        dx = ACROSS[i]
        at, part, dy = ((0, None, 1), (0, None, -1), (-1, 0, 1), (1, 1, -1))[n]
        place = slot(h, at - dy if incoming else at, dx, part)
        src = source(h, 0) if (i == 0 and n < 2) else place
        if i == 0 and n < 2 and not incoming:
            place = slot(h, 0, 0)
        k = (h * 4 + i) * 4 + n
        return remote(src, place, y_send.at[k], y_recv.at[k], plane.device(dy, 0))

    def other(n, incoming):
        dx, dc = FRIENDS[n]
        return plane.friend(-dx if incoming else dx, dc)[2]

    def asking(head):
        return pl.ds(pl.multiple_of(lax.div(3 * head, 2) * 128, 128), ASK)

    def ask(n, incoming=False):
        return remote(
            queries.at[:, asking(other(n, False))],
            asked.at[other(n, True) if incoming else mine],
            q_send.at[n],
            q_recv.at[n],
            plane.friend_device(*FRIENDS[n]),
        )

    def tell(n, incoming=False):
        return remote(
            starts,
            begin.at[other(n, True) if incoming else mine],
            q_send.at[len(FRIENDS) + n],
            q_recv.at[len(FRIENDS) + n],
            plane.friend_device(*FRIENDS[n]),
        )

    def table(n, incoming=False):
        dy, dx = OTHERS[n]
        return remote(
            given.at[plane.chip(dy, dx)],
            held.at[plane.chip(-dy, -dx) if incoming else here],
            give.at[n],
            take.at[n],
            plane.device(dy, dx),
        )

    own_asked = pltpu.make_async_copy(
        queries.at[:, asking(mine)], asked.at[mine], sems.at[4]
    )
    own_begin = pltpu.make_async_copy(starts, begin.at[mine], sems.at[5])
    own_table = pltpu.make_async_copy(given.at[here], held.at[here], sems.at[6])

    project_keys()
    swap.start()
    for h in (0, 1):
        if h == 1:
            make_tables()
            own_begin.start()
            own_table.start()
            swap.wait_recv()
        keep(h).start()
        for n in range(3):
            across(h, n).start()
        along(h, 0, 0).start()
        along(h, 0, 1).start()
    project_queries(0)
    for n in range(3):
        i = (1, 2, 3)[n]
        for h in (0, 1):
            across(h, n, True).wait_recv()
            along(h, i, 0).start()
            along(h, i, 1).start()
    project_queries(1)
    project_queries(2)
    own_asked.start()
    for n in range(len(FRIENDS)):
        ask(n).start()
        tell(n).start()
    for n in range(len(OTHERS)):
        table(n).start()

    own_asked.wait()
    own_begin.wait()
    for n in range(len(FRIENDS)):
        ask(n, True).wait_recv()
        tell(n, True).wait_recv()
    for h in (0, 1):
        keep(h).wait()

    lane = lax.broadcasted_iota(jnp.int32, (rows, 128), 1)
    low = lane < HEAD_SIZE
    upper = core == 1
    for which in range(SIDE):
        for side in (0, 1):
            begins[2 * which + side] = jnp.broadcast_to(
                begin[2 * which + side, 0:1, :], (rows, rows)
            ).T
            tiles = [
                asked[2 * which + side, :, i * 128 : (i + 1) * 128].astype(jnp.float32)
                for i in (0, 1)
            ]
            turned = [pltpu.roll(tile, HEAD_SIZE, axis=1) for tile in tiles]
            heads = (
                jnp.where(upper, turned[0], tiles[0]),
                jnp.where(upper, tiles[1], turned[0]),
                jnp.where(upper, turned[1], tiles[1]),
            )
            for n in range(HEADS):
                at = (n * 2 + side) * rows
                packed[which, at : at + rows, :] = jnp.where(low, heads[n], 0.0).astype(
                    jnp.bfloat16
                )
    peak[...] = jnp.full_like(peak, LOW)
    total[...] = jnp.zeros_like(total)
    both = 2 * HEADS * rows
    lane_number = lax.broadcasted_iota(jnp.int32, (1, 128), 1).astype(jnp.float32)
    row_number = lax.broadcasted_iota(jnp.int32, (rows, 128), 0).astype(jnp.float32)

    def member(which):
        flip = lax.rem(plane.x + which, 2)
        return jnp.where(flip == 0, plane.y, SIDE - 1 - plane.y) * SIDE + which

    def visit(which, chip):
        stream_chip = member(which)
        at = chip * (2 * rows)
        shift = (stream_chip * (2 * rows) - at).astype(jnp.float32)
        base = at.astype(jnp.float32)
        for side in (0, 1):
            first = begins[2 * which + side] - base
            last = row_number + (shift + side * rows)
            for j in range(KEYS // 128):
                key_number = lane_number + j * 128
                bias[side * rows : (side + 1) * rows, j * 128 : (j + 1) * 128] = jnp.where(
                    (key_number >= first) & (key_number <= last), 0.0, LOW
                )
        tile = store[pl.ds(chip, 2)].reshape(KEYS, 128)
        scores = lax.dot_general(
            packed[which], tile, (((1,), (1,)), ((), ())), preferred_element_type=jnp.float32
        )
        scores = (scores.reshape(HEADS, 2 * rows, KEYS) + bias[...][None]).reshape(both, KEYS)
        before = peak[which]
        now = jnp.maximum(before, jnp.max(scores, axis=1, keepdims=True))
        peak[which] = now
        fade = jnp.exp2((before - now) * SCALE)
        wide = jnp.concatenate([now] * (KEYS // 128), axis=1)
        probs = jnp.exp2((scores - wide) * SCALE).astype(jnp.bfloat16)
        value_lane = lax.broadcasted_iota(jnp.int32, (KEYS, 128), 1) >= HEAD_SIZE
        beside = jnp.where(value_lane, tile, jnp.ones_like(tile))
        total[which] = total[which] * fade + jnp.dot(
            probs, beside, preferred_element_type=jnp.float32
        )

    def answer(which):
        for side in (0, 1):
            high, turned = [], []
            for n in range(HEADS):
                at = (n * 2 + side) * rows
                sums_here = total[which, at : at + rows, :]
                high.append(sums_here / pltpu.roll(sums_here, HEAD_SIZE, axis=1))
                turned.append(pltpu.roll(high[n], HEAD_SIZE, axis=1))
            tiles = (
                jnp.where(upper, high[0], jnp.where(low, turned[0], high[1])),
                jnp.where(upper, jnp.where(low, turned[1], high[2]), turned[2]),
            )
            for i in (0, 1):
                done[2 * which + side, :, i * 128 : (i + 1) * 128] = tiles[i].astype(jnp.bfloat16)

    def reply(n, incoming=False):
        return remote(
            done.at[other(n, False)],
            replies.at[other(n, True) if incoming else mine],
            o_send.at[n],
            o_recv.at[n],
            plane.friend_device(*FRIENDS[n]),
        )

    own_reply = pltpu.make_async_copy(done.at[mine], replies.at[mine], sems.at[7])

    def phase(step, carry):
        @pl.when(step == 1)
        def _():
            for i in range(4):
                for n in (0, 1):
                    for h in (0, 1):
                        along(h, i, n, True).wait_recv()
                        along(h, i, n + 2).start()

        @pl.when(step == 3)
        def _():
            for i in range(4):
                for n in (2, 3):
                    for h in (0, 1):
                        along(h, i, n, True).wait_recv()

        dy = jnp.where(step == 0, 0, jnp.where(step == 1, SIDE - 1, step - 1))
        dy = jnp.where(step == 3, 2, dy)
        row = lax.rem(plane.y + dy, SIDE) * SIDE

        def one(t, carry):
            turn, part = lax.div(t, 2), lax.rem(t, 2)
            dx = jnp.where(turn == 0, 2, jnp.where(turn == 1, 1, jnp.where(turn == 2, 3, 0)))
            which = lax.rem(plane.x + dx, SIDE)
            chip = row + 2 * part

            @pl.when(chip <= member(which))
            def _():
                visit(which, chip)

            @pl.when((step == 3) & (part == 1))
            def _():
                answer(which)

            for column in range(SIDE):

                @pl.when((step == 3) & (part == 1) & (dx == column))
                def _():
                    for n, friend in enumerate(FRIENDS):
                        if friend[0] == column:
                            reply(n).start()
                    if column == 0:
                        own_reply.start()

            return carry

        return lax.fori_loop(0, 2 * SIDE, one, carry)

    lax.fori_loop(0, 4, phase, 0)

    for n in (0, 1):
        weight_copy(n, True).wait_recv()
        weight_copy(2 + n).start()
        weight_copy(5 + n).start()

    swap.wait_send()
    own_table.wait()
    for h in (0, 1):
        for n in range(3):
            across(h, n).wait_send()
        for i in range(4):
            for n in range(4):
                along(h, i, n).wait_send()
    for n in range(len(FRIENDS)):
        ask(n).wait_send()
        tell(n).wait_send()
    for n in range(len(OTHERS)):
        table(n, True).wait_recv()
        table(n).wait_send()
    own_reply.wait()
    for n in range(len(FRIENDS)):
        reply(n, True).wait_recv()
        reply(n).wait_send()
    for p in range(KEY_VALUE_HEADS // 2):
        even, odd = replies[2 * p], replies[2 * p + 1]
        out[:, p * 384 : p * 384 + 128] = even[:, :128]
        out[:, p * 384 + 128 : p * 384 + 256] = jnp.where(
            low, even[:, 128:].astype(jnp.float32), odd[:, :128].astype(jnp.float32)
        ).astype(jnp.bfloat16)
        out[:, p * 384 + 256 : p * 384 + 384] = odd[:, 128:]


BLOCKS = 4
GROUPS = (
    ((0, 0), (2, 0), (0, -1), (0, 1)),
    ((-1, 0), (1, 0), (-1, -1), (-1, 1)),
    ((-1, 2), (1, 2), (1, -1), (1, 1)),
    ((0, 2), (2, 2), (2, -1), (2, 1)),
)
TWO = (0, 2)
ENDS = (-1, 1)


def experts_section(
    plane, weight_copy, own, residual, tables, out,
    rows_in, sums, weights, picked, made, hold_q, hold_r, hold_p, hold_d,
    g_send, g_recv, q_send, q_recv, r_send, r_recv, p_send, p_recv, d_send, d_recv, sem,
):
    rows, width = own.shape
    part_rows = rows // 2
    even = lax.rem(plane.y + plane.x, 2) == 0

    def turned(o, t):
        return jnp.where(even, t, o), jnp.where(even, o, t)

    def place(at):
        return plane.chip(*turned(*at))

    def device(o, t):
        return plane.device(*turned(o, t))

    def part(n):
        return pl.ds(n * part_rows, part_rows)

    def gather(k, src, dst, to):
        return remote(src, dst, g_send.at[k], g_recv.at[k], to)

    def emit(n, incoming=False):
        d = (1, -1)[n]
        at = (0, -d) if incoming else (0, 0)
        return gather(n, own, rows_in.at[place(at)], device(d, 0))

    def pass_on(n, incoming=False):
        at = (2, 0) if incoming else (0, ENDS[n])
        ref = rows_in.at[place(at), part(n)]
        return gather(2 + n, ref, ref, device(0, -ENDS[n]))

    def spread(group, j, n, incoming=False):
        d = (1, -1)[n]
        if group == 0:
            at = (-d, TWO[j]) if incoming else (TWO[j], 0)
            to = device(0, d)
        else:
            at = (ENDS[j], -d) if incoming else (0, ENDS[j])
            to = device(d, 0)
        ref = rows_in.at[place(at)]
        src = own if at == (0, 0) else ref
        return gather(4 + group * 8 + j * 4 + n, src, ref, to)

    def relay(group, j, n, incoming=False):
        if group == 0:
            at = (TWO[j], 2) if incoming else (ENDS[n], TWO[j])
            to = device(-ENDS[n], 0)
        else:
            at = (2, ENDS[j]) if incoming else (ENDS[j], ENDS[n])
            to = device(0, -ENDS[n])
        ref = rows_in.at[place(at), part(n)]
        return gather(4 + group * 8 + j * 4 + 2 + n, ref, ref, to)

    mine = pltpu.make_async_copy(own, rows_in.at[place((0, 0))], sem)
    for n in (0, 1):
        emit(n).start()
    for n in (0, 1):
        spread(0, 0, n).start()
    mine.start()
    for j in (0, 1):
        emit(j, True).wait_recv()
        pass_on(j).start()
        for n in (0, 1):
            spread(1, j, n).start()
    for n in (0, 1):
        pass_on(n, True).wait_recv()
    for n in (0, 1):
        spread(0, 1, n).start()
    for n in (2, 3):
        weight_copy(n, True).wait_recv()
    weight_copy(7).start()
    mine.wait()
    for n in (4, 5, 6, 7):
        weight_copy(n, True).wait_recv()

    def far(group, j):
        return (TWO[j], 2) if group == 0 else (2, ENDS[j])

    def near(group, j, side):
        return (ENDS[side], TWO[j]) if group == 0 else (ENDS[j], ENDS[side])

    def line(group, along_first):
        return (lambda d: device(d, 0)) if (group == 0) == along_first else (lambda d: device(0, d))

    def give_far(group, j, n):
        k = group * 4 + j * 2 + n
        return remote(
            sums.at[place(far(group, j)), part(n)],
            hold_q.at[k],
            q_send.at[k],
            q_recv.at[k],
            line(group, False)(ENDS[n]),
        )

    def give_near(group, j, side, late):
        k = group * 4 + j * 2 + side
        span = part(side if late else 1 - side)
        return remote(
            sums.at[place(near(group, j, side)), span],
            hold_r.at[k, span],
            r_send.at[2 * k + late],
            r_recv.at[2 * k + late],
            line(group, True)(ENDS[side]),
        )

    def give_across(n):
        return remote(
            sums.at[place((2, 0)), part(n)],
            hold_p.at[n],
            p_send.at[n],
            p_recv.at[n],
            device(ENDS[n], 0),
        )

    def give_back(side, late):
        span = part(side if late else 1 - side)
        return remote(
            sums.at[place((0, ENDS[side])), span],
            hold_d.at[side, span],
            d_send.at[2 * side + late],
            d_recv.at[2 * side + late],
            device(0, ENDS[side]),
        )

    PAIRS = [(0, 1), (1, 0), (1, 1), (0, 0)]
    slot = lax.broadcasted_iota(jnp.int32, (SLOTS, rows), 0).astype(jnp.float32)

    def group_step(g, carry):
        for when, j in ((1, 0), (2, 1)):

            @pl.when(g == when)
            def _():
                for n in (0, 1):
                    for group in (0, 1):
                        spread(group, j, n, True).wait_recv()
                        relay(group, j, n).start()

        @pl.when(g == 3)
        def _():
            for group, j in PAIRS:
                for n in (0, 1):
                    relay(group, j, n, True).wait_recv()
            for group, j in PAIRS:
                for side in (0, 1):
                    give_near(group, j, side, 0).start()

        ids = []
        for j in range(BLOCKS):
            at = place(GROUPS[3][j])
            for k in range(3):
                at = jnp.where(g == k, place(GROUPS[k][j]), at)
            ids.append(at)

        def hits(j, e):
            return tables[ids[j], 2 + e : 3 + e, :] == slot

        def choice(j):
            both = jnp.concatenate([hits(j, 0), hits(j, 1)], axis=0)
            return jnp.where(both, 1.0, 0.0).astype(jnp.bfloat16)

        for j in range(BLOCKS):
            picked[j] = jnp.dot(
                choice(j), rows_in[ids[j]], preferred_element_type=jnp.float32
            ).astype(jnp.bfloat16)
        for e in (0, 1):
            chosen = picked[:, e * SLOTS : (e + 1) * SLOTS, :].reshape(BLOCKS * SLOTS, width)
            gate = jnp.dot(chosen, weights[e, 0], preferred_element_type=jnp.float32)
            up = jnp.dot(chosen, weights[e, 1], preferred_element_type=jnp.float32)
            units = (gate / (1.0 + jnp.exp(-gate)) * up).astype(jnp.bfloat16)
            result = lax.dot_general(
                units, weights[e, 2], (((1,), (1,)), ((), ())), preferred_element_type=jnp.float32
            )
            for j in range(BLOCKS):
                gain = jnp.sum(
                    jnp.where(hits(j, e), tables[ids[j], e : e + 1, :], 0.0),
                    axis=1,
                    keepdims=True,
                )
                made[j, e * SLOTS : (e + 1) * SLOTS, :] = (
                    result[j * SLOTS : (j + 1) * SLOTS, :] * gain
                ).astype(jnp.bfloat16)
        for j in range(BLOCKS):
            sums[ids[j]] = lax.dot_general(
                choice(j), made[j], (((0,), (0,)), ((), ())), preferred_element_type=jnp.float32
            ).astype(jnp.bfloat16)
        return carry

    lax.fori_loop(0, len(GROUPS), group_step, 0)

    for group, j in PAIRS:
        for n in (0, 1):
            give_far(group, j, n).start()

    def add(at, held):
        sums[at] = (sums[at].astype(jnp.float32) + held.astype(jnp.float32)).astype(jnp.bfloat16)

    def relay_sums(group, j):
        for side in (0, 1):
            k = group * 4 + j * 2 + side
            give_far(group, j, side).wait_recv()
            add((place(near(group, j, side)), part(side)), hold_q[k])
            give_near(group, j, side, 1).start()

    def total(group, j):
        for side in (0, 1):
            for late in (0, 1):
                give_near(group, j, side, late).wait_recv()
        at = place((TWO[j], 0) if group == 0 else (0, ENDS[j]))
        k = group * 4 + j * 2
        return at, (
            sums[at].astype(jnp.float32)
            + hold_r[k].astype(jnp.float32)
            + hold_r[k + 1].astype(jnp.float32)
        )

    for group, j in PAIRS[:3]:
        relay_sums(group, j)
    at, value = total(0, 1)
    sums[at] = value.astype(jnp.bfloat16)
    for n in (0, 1):
        give_across(n).start()
    relay_sums(0, 0)
    for side in (0, 1):
        at, value = total(1, side)
        sums[at] = value.astype(jnp.bfloat16)
        give_back(side, 0).start()
    for side in (0, 1):
        give_across(side).wait_recv()
        add((place((0, ENDS[side])), part(side)), hold_p[side])
        give_back(side, 1).start()
    _, value = total(0, 0)
    out_sum = value + residual[...]
    for side in (0, 1):
        for late in (0, 1):
            give_back(side, late).wait_recv()
    out[...] = (
        out_sum + hold_d[0].astype(jnp.float32) + hold_d[1].astype(jnp.float32)
    ).astype(out.dtype)

    for n in (0, 1):
        emit(n).wait_send()
        pass_on(n).wait_send()
        give_across(n).wait_send()
        for late in (0, 1):
            give_back(n, late).wait_send()
    for n in range(8):
        weight_copy(n).wait_send()
    for group, j in PAIRS:
        for n in (0, 1):
            spread(group, j, n).wait_send()
            relay(group, j, n).wait_send()
            give_far(group, j, n).wait_send()
            for late in (0, 1):
                give_near(group, j, n, late).wait_send()


def normed(values, gain):
    mean_square = jnp.mean(values * values, axis=1, keepdims=True)
    return (values * lax.rsqrt(mean_square + epsilon) * gain[None]).astype(jnp.bfloat16)


def rotation_tables(plane, prompt_start, cosine, sine):
    rows = prompt_start.shape[1]
    half = HEAD_SIZE // 2
    lane = lax.broadcasted_iota(jnp.int32, (rows, 128), 1)
    begin = jnp.broadcast_to(prompt_start[...].astype(jnp.float32), (rows, rows)).T
    first = (plane.chip(0, 0) * 2 + plane.core) * rows
    position = first + lax.broadcasted_iota(jnp.int32, (rows, 128), 0)
    power = lax.rem(lane, half).astype(jnp.float32) / half
    angle = (position.astype(jnp.float32) - begin) * jnp.exp(power * -math.log(10000.0))
    cosine[...] = jnp.cos(angle)
    sine[...] = jnp.where(lax.rem(lane, HEAD_SIZE) < half, -jnp.sin(angle), jnp.sin(angle))


def layer_kernel(
    hidden, attn_gain, wq, wk, wv, wo, prompt_start, ffn_gain, routes, route_weights,
    first,
    out, key_cache, value_cache,
    query_w, key_w, value_w, output_w, own_in, residual, cosine, sine,
    queries, pairs, starts, given, attention, tables,
    near, store, asked, begin, begins, packed, peak, total, bias, done, replies,
    rows_in, sums, weights, picked, made, hold_q, hold_r, hold_p, hold_d,
    *sems,
):
    attention_sems, expert_sems, (w_send, w_recv, load_sems, row_sem) = (
        sems[:11],
        sems[11:21],
        sems[21:],
    )
    plane = Plane()
    core = plane.core
    rows, width = hidden.shape
    arrived = greet(plane)

    def lanes(r):
        return pl.ds(r * 128, 128)

    def weight_copy(n, incoming=False):
        half = width // 2
        e = 1 - core if incoming and n >= 4 else core
        if n < 2:
            src, dst = first, weights.at[e, :, :, lanes(1 + n)]
            to = plane.level((1, -1)[n])
        elif n < 4:
            span = pl.ds((n - 2) * half, half)
            src = weights.at[e, :, span, lanes(n - 1)]
            dst = weights.at[e, :, span, lanes(3)]
            to = plane.level((1, -1)[n - 2])
        else:
            dst = weights.at[e, :, :, lanes(n - 4)]
            src = first if n == 4 else dst
            to = plane.partner()
        return remote(src, dst, w_send.at[n], w_recv.at[n], to)

    loads = [
        pltpu.make_async_copy(src, dst, load_sems.at[n])
        for n, (src, dst) in enumerate(
            (
                (wk, key_w),
                (wv, value_w),
                (wq, query_w),
                (wo, output_w),
                (first, weights.at[core, :, :, lanes(0)]),
            )
        )
    ]
    for load in loads[:2]:
        load.start()
    own_in[...] = normed(hidden[...].astype(jnp.float32), attn_gain[...])
    rotation_tables(plane, prompt_start, cosine, sine)
    arrived()
    for n in (0, 1, 4):
        weight_copy(n).start()

    lane = lax.broadcasted_iota(jnp.int32, (rows, 128), 1)
    first_half = lax.rem(lane, HEAD_SIZE) < HEAD_SIZE // 2

    def rotated(tile):
        other = jnp.where(
            first_half,
            pltpu.roll(tile, 128 - HEAD_SIZE // 2, axis=1),
            pltpu.roll(tile, HEAD_SIZE // 2, axis=1),
        )
        return tile * cosine[...] + other * sine[...]

    def project_keys():
        for load in loads[2:]:
            load.start()
        starts[...] = jnp.broadcast_to(prompt_start[...].astype(jnp.float32), starts.shape)
        loads[0].wait()
        keys = jnp.dot(own_in[...], key_w[...], preferred_element_type=jnp.float32)
        loads[1].wait()
        values = jnp.dot(own_in[...], value_w[...], preferred_element_type=jnp.float32)
        value_cache[...] = values.astype(jnp.bfloat16)
        low = lane < HEAD_SIZE
        for p in range(KEY_VALUE_HEADS // 2):
            at = slice(p * 128, (p + 1) * 128)
            key, value = rotated(keys[:, at]), values[:, at]
            key_cache[:, at] = key.astype(jnp.bfloat16)
            sides = (
                jnp.where(low, key, pltpu.roll(value, HEAD_SIZE, axis=1)),
                jnp.where(low, pltpu.roll(key, HEAD_SIZE, axis=1), value),
            )
            for c in (0, 1):
                to = (c * SIDE + p) * 128
                pairs[:, to : to + 128] = sides[c].astype(jnp.bfloat16)

    def project_queries(c):
        if c == 0:
            loads[2].wait()
        part = jnp.dot(
            own_in[...],
            query_w[:, c * 512 : (c + 1) * 512],
            preferred_element_type=jnp.float32,
        )
        for p in range(4):
            at = c * 512 + p * 128
            queries[:, at : at + 128] = rotated(part[:, p * 128 : (p + 1) * 128]).astype(
                jnp.bfloat16
            )

    def make_tables():
        expert = lax.broadcasted_iota(jnp.int32, (EXPERTS, rows), 0)
        gains = jnp.zeros((EXPERTS, rows), jnp.float32)
        named = jnp.zeros((EXPERTS, rows), jnp.float32)
        for j in range(TOP):
            hit = routes[j : j + 1, :] == expert
            gains = gains + jnp.where(hit, route_weights[j : j + 1, :], 0.0)
            named = named + jnp.where(hit, 1.0, 0.0)
        earlier = lax.broadcasted_iota(jnp.int32, (rows, rows), 0) < lax.broadcasted_iota(
            jnp.int32, (rows, rows), 1
        )
        ranks = jnp.dot(
            named.astype(jnp.bfloat16),
            jnp.where(earlier, 1.0, 0.0).astype(jnp.bfloat16),
            preferred_element_type=jnp.float32,
        )
        ranks = jnp.where(named > 0.0, ranks, -1.0)
        given[...] = jnp.zeros_like(given)
        for c in range(CHIPS):
            given[c, 0:2, :] = gains[2 * c : 2 * c + 2, :]
            given[c, 2:4, :] = ranks[2 * c : 2 * c + 2, :]

    attention_section(
        plane, weight_copy, project_keys, project_queries, make_tables,
        queries, pairs, starts, given, attention, tables,
        near, store, asked, begin, begins, packed, peak, total, bias, done, replies,
        *attention_sems,
    )

    loads[3].wait()
    for c in range(3):
        at = slice(c * 512, (c + 1) * 512)
        residual[:, at] = hidden[:, at].astype(jnp.float32) + jnp.dot(
            attention[...], output_w[:, at], preferred_element_type=jnp.float32
        )
    own_in[...] = normed(residual[...], ffn_gain[...])
    loads[4].wait()

    experts_section(
        plane, weight_copy, own_in, residual, tables, out,
        rows_in, sums, weights, picked, made, hold_q, hold_r, hold_p, hold_d,
        *expert_sems, row_sem,
    )


def run_layer(hidden, attn_gain, wq, wk, wv, wo, starts, ffn_gain, routes, gains, first):
    rows, width = hidden.shape
    cache = wk.shape[1]
    dma = pltpu.SemaphoreType.DMA
    vmem = pl.BlockSpec(memory_space=pltpu.VMEM)
    hbm = pl.BlockSpec(memory_space=pl.ANY)

    def brief(*shape):
        return pltpu.VMEM(shape, jnp.bfloat16)

    def full(*shape):
        return pltpu.VMEM(shape, jnp.float32)

    others = len(OTHERS)
    friends = len(FRIENDS)
    counts = (others, 6, 32, 2 * friends, friends)
    attention_sems = [dma((n,)) for n in counts for _ in (0, 1)] + [dma((8,))]
    expert_sems = [dma((n,)) for n in (20, 8, 16, 2, 4) for _ in (0, 1)]
    both = 2 * HEADS * rows
    return pl.pallas_call(
        layer_kernel,
        out_shape=(
            jax.ShapeDtypeStruct((rows, width), jnp.bfloat16),
            jax.ShapeDtypeStruct((rows, cache), jnp.bfloat16),
            jax.ShapeDtypeStruct((rows, cache), jnp.bfloat16),
        ),
        in_specs=[vmem, vmem, hbm, hbm, hbm, hbm] + [vmem] * 4 + [hbm],
        out_specs=(vmem,) * 3,
        scratch_shapes=[
            brief(*wq.shape),
            brief(*wk.shape),
            brief(*wv.shape),
            brief(*wo.shape),
            brief(rows, width),
            full(rows, width),
            full(rows, 128),
            full(rows, 128),
            brief(rows, width),
            brief(rows, 2 * cache),
            full(8, rows),
            full(CHIPS, 8, rows),
            brief(rows, width),
            full(CHIPS, 8, rows),
            brief(rows, 512),
            brief(CHIPS, 2 * rows, 128),
            brief(KEY_VALUE_HEADS, rows, ASK),
            full(KEY_VALUE_HEADS, 8, rows),
            full(KEY_VALUE_HEADS, rows, rows),
            brief(SIDE, both, 128),
            full(SIDE, both, 128),
            full(SIDE, both, 128),
            full(2 * rows, KEYS),
            brief(KEY_VALUE_HEADS, rows, ASK),
            brief(KEY_VALUE_HEADS, rows, ASK),
            brief(CHIPS, rows, width),
            brief(CHIPS, rows, width),
            brief(2, 3, width, FF),
            brief(BLOCKS, 2 * SLOTS, width),
            brief(BLOCKS, 2 * SLOTS, width),
            brief(8, rows // 2, width),
            brief(8, rows, width),
            brief(2, rows // 2, width),
            brief(2, rows, width),
            *attention_sems,
            *expert_sems,
            dma((8,)),
            dma((8,)),
            dma((5,)),
            dma,
        ],
        compiler_params=pltpu.CompilerParams(
            collective_id=0, has_side_effects=True, vmem_limit_bytes=63 << 20
        ),
        name="layer",
    )(
        hidden, attn_gain, wq, wk, wv, wo, starts, ffn_gain, routes, gains, first
    )


def publish(*results):
    def kernel(*refs):
        for src, dst in zip(refs[: len(results)], refs[len(results) :]):
            dst[...] = src[...]

    vmem = pl.BlockSpec(memory_space=pltpu.VMEM)
    return pl.pallas_call(
        kernel,
        out_shape=tuple(jax.ShapeDtypeStruct(r.shape, r.dtype) for r in results),
        in_specs=[vmem] * len(results),
        out_specs=(vmem,) * len(results),
        name="publish",
    )(*results)


def shards(
    hidden,
    attn_gain,
    query_weight,
    key_matrix,
    value_matrix,
    output_weight,
    prompt_start,
    ffn_gain,
    routes,
    route_weights,
    expert_weights,
):
    results = run_layer(
        hidden,
        attn_gain,
        query_weight,
        key_matrix,
        value_matrix,
        output_weight,
        prompt_start[None],
        ffn_gain,
        routes.T,
        route_weights.T,
        expert_weights[0],
    )
    return publish(*results)


def solution(mesh):
    in_specs = (
        P(("req", "exp"), None),
        P(),
        P(),
        P(),
        P(),
        P(),
        P(("req", "exp")),
        P(),
        P(("req", "exp"), None),
        P(("req", "exp"), None),
        P("exp", None, None, "req"),
    )
    out_specs = (P(("req", "exp"), None), P(("req", "exp"), None), P(("req", "exp"), None))
    return jax.shard_map(shards, mesh=mesh, in_specs=in_specs, out_specs=out_specs, check_vma=False)
```

```python
import math

import jax
import jax.numpy as jnp
from jax import lax
from jax.experimental import pallas as pl
from jax.experimental.pallas import tpu as pltpu
from jax.sharding import PartitionSpec as P

QUERY_HEADS = 24
KEY_VALUE_HEADS = 8
HEAD_SIZE = 64
TOP = 8
SIDE = 4
CHIPS = SIDE * SIDE
EXPERTS = 32
SLOTS = 64
FF = 512


epsilon = 1e-05


class Plane:
    def __init__(self):
        me = lax.axis_index("exp")
        self.core = lax.rem(me, 2)
        chip = lax.div(me, 2)
        self.y = lax.div(chip, SIDE)
        self.x = lax.rem(chip, SIDE)

    def chip(self, dy, dx):
        return lax.rem(self.y + dy + SIDE, SIDE) * SIDE + lax.rem(self.x + dx + SIDE, SIDE)

    def device(self, dy, dx):
        return {"exp": self.chip(dy, dx) * 2 + self.core}

    def level(self, dz):
        return {"req": lax.rem(lax.axis_index("req") + dz + SIDE, SIDE)}

    def partner(self):
        return {"exp": self.chip(0, 0) * 2 + 1 - self.core}

    def friend(self, dx, dc):
        x = lax.rem(self.x + dx + SIDE, SIDE)
        y = self.y if dx % 2 == 0 else SIDE - 1 - self.y
        core = 1 - self.core if dc else self.core
        return y * SIDE + x, core, 2 * x + core

    def friend_device(self, dx, dc):
        chip, core, _ = self.friend(dx, dc)
        return {"exp": chip * 2 + core}


FRIENDS = tuple((dx, dc) for dx in range(SIDE) for dc in (0, 1) if dx or dc)
OTHERS = tuple((dy, dx) for dy in range(SIDE) for dx in range(SIDE) if dy or dx)


def greet(plane):
    barrier = pltpu.get_barrier_semaphore()
    devices = [plane.device(dy, dx) for dy, dx in OTHERS]
    devices += [plane.friend_device(dx, 1) for dx in range(SIDE)]
    devices += [plane.level(1), plane.level(-1)]
    for device in devices:
        pl.semaphore_signal(
            barrier, inc=1, device_id=device, device_id_type=pl.DeviceIdType.MESH
        )
    return lambda: pl.semaphore_wait(barrier, len(devices))


def remote(src, dst, send, recv, device):
    return pltpu.make_async_remote_copy(
        src_ref=src,
        dst_ref=dst,
        send_sem=send,
        recv_sem=recv,
        device_id=device,
        device_id_type=pl.DeviceIdType.MESH,
    )


KEYS = 512
HEADS = QUERY_HEADS // KEY_VALUE_HEADS
ASK = 256
LOW = -1e30
SCALE = HEAD_SIZE**-0.5 * 1.4426950408889634
ACROSS = (0, -1, 1, 2)


def attention_section(
    plane, weight_copy, project_keys, project_queries, make_tables,
    queries, pairs, starts, given, out, held,
    near, store, asked, begin, begins, packed, peak, total, bias, done, replies,
    give, take, x_send, x_recv, y_send, y_recv, q_send, q_recv, o_send, o_recv, sems,
):
    core = plane.core
    here = plane.chip(0, 0)
    rows = queries.shape[0]
    mine = 2 * plane.x + core

    def lanes(at, size):
        return pl.ds(pl.multiple_of(at * size, size), size)

    swap = remote(
        pairs.at[:, lanes(1 - core, 512)], near, sems.at[0], sems.at[1], plane.partner()
    )

    def source(h, dx):
        x = lax.rem(plane.x + dx + SIDE, SIDE)
        if h == 0:
            return pairs.at[:, lanes(SIDE * core + x, 128)]
        return near.at[:, lanes(x, 128)]

    def slot(h, dy, dx, part=None):
        low = (core if h == 0 else 1 - core) * rows
        size = rows
        if part is not None:
            size = rows // 2
            low = low + part * size
        return store.at[plane.chip(dy, dx), pl.ds(pl.multiple_of(low, size), size)]

    def keep(h):
        return pltpu.make_async_copy(source(h, 0), slot(h, 0, 0), sems.at[2 + h])

    def across(h, n, incoming=False):
        dx = (1, -1, 2)[n]
        return remote(
            source(h, dx),
            slot(h, 0, -dx if incoming else 0),
            x_send.at[3 * h + n],
            x_recv.at[3 * h + n],
            plane.device(0, dx),
        )

    def along(h, i, n, incoming=False):
        dx = ACROSS[i]
        at, part, dy = ((0, None, 1), (0, None, -1), (-1, 0, 1), (1, 1, -1))[n]
        place = slot(h, at - dy if incoming else at, dx, part)
        src = source(h, 0) if (i == 0 and n < 2) else place
        if i == 0 and n < 2 and not incoming:
            place = slot(h, 0, 0)
        k = (h * 4 + i) * 4 + n
        return remote(src, place, y_send.at[k], y_recv.at[k], plane.device(dy, 0))

    def other(n, incoming):
        dx, dc = FRIENDS[n]
        return plane.friend(-dx if incoming else dx, dc)[2]

    def asking(head):
        return pl.ds(pl.multiple_of(lax.div(3 * head, 2) * 128, 128), ASK)

    def ask(n, incoming=False):
        return remote(
            queries.at[:, asking(other(n, False))],
            asked.at[other(n, True) if incoming else mine],
            q_send.at[n],
            q_recv.at[n],
            plane.friend_device(*FRIENDS[n]),
        )

    def tell(n, incoming=False):
        return remote(
            starts,
            begin.at[other(n, True) if incoming else mine],
            q_send.at[len(FRIENDS) + n],
            q_recv.at[len(FRIENDS) + n],
            plane.friend_device(*FRIENDS[n]),
        )

    def table(n, incoming=False):
        dy, dx = OTHERS[n]
        return remote(
            given.at[plane.chip(dy, dx)],
            held.at[plane.chip(-dy, -dx) if incoming else here],
            give.at[n],
            take.at[n],
            plane.device(dy, dx),
        )

    own_asked = pltpu.make_async_copy(
        queries.at[:, asking(mine)], asked.at[mine], sems.at[4]
    )
    own_begin = pltpu.make_async_copy(starts, begin.at[mine], sems.at[5])
    own_table = pltpu.make_async_copy(given.at[here], held.at[here], sems.at[6])

    project_queries()
    own_asked.start()
    own_begin.start()
    for n in range(len(FRIENDS)):
        ask(n).start()
        tell(n).start()
    project_keys()
    swap.start()
    for h in (0, 1):
        if h == 1:
            make_tables()
            own_table.start()
            swap.wait_recv()
        keep(h).start()
        for n in range(3):
            across(h, n).start()
        along(h, 0, 0).start()
        along(h, 0, 1).start()
    for n in range(3):
        i = (1, 2, 3)[n]
        for h in (0, 1):
            across(h, n, True).wait_recv()
            along(h, i, 0).start()
            along(h, i, 1).start()
    for n in range(len(OTHERS)):
        table(n).start()

    own_asked.wait()
    own_begin.wait()
    for n in range(len(FRIENDS)):
        ask(n, True).wait_recv()
        tell(n, True).wait_recv()
    for h in (0, 1):
        keep(h).wait()

    lane = lax.broadcasted_iota(jnp.int32, (rows, 128), 1)
    low = lane < HEAD_SIZE
    upper = core == 1
    for which in range(SIDE):
        for side in (0, 1):
            begins[2 * which + side] = jnp.broadcast_to(
                begin[2 * which + side, 0:1, :], (rows, rows)
            ).T
            tiles = [
                asked[2 * which + side, :, i * 128 : (i + 1) * 128].astype(jnp.float32)
                for i in (0, 1)
            ]
            turned = [pltpu.roll(tile, HEAD_SIZE, axis=1) for tile in tiles]
            heads = (
                jnp.where(upper, turned[0], tiles[0]),
                jnp.where(upper, tiles[1], turned[0]),
                jnp.where(upper, turned[1], tiles[1]),
            )
            for n in range(HEADS):
                at = (n * 2 + side) * rows
                packed[which, at : at + rows, :] = jnp.where(low, heads[n], 0.0).astype(
                    jnp.bfloat16
                )
    peak[...] = jnp.full_like(peak, LOW)
    total[...] = jnp.zeros_like(total)
    both = 2 * HEADS * rows
    lane_number = lax.broadcasted_iota(jnp.int32, (1, 128), 1).astype(jnp.float32)
    row_number = lax.broadcasted_iota(jnp.int32, (rows, 128), 0).astype(jnp.float32)

    def member(which):
        flip = lax.rem(plane.x + which, 2)
        return jnp.where(flip == 0, plane.y, SIDE - 1 - plane.y) * SIDE + which

    def visit(which, chip):
        stream_chip = member(which)
        at = chip * (2 * rows)
        shift = (stream_chip * (2 * rows) - at).astype(jnp.float32)
        base = at.astype(jnp.float32)
        for side in (0, 1):
            first = begins[2 * which + side] - base
            last = row_number + (shift + side * rows)
            for j in range(KEYS // 128):
                key_number = lane_number + j * 128
                bias[side * rows : (side + 1) * rows, j * 128 : (j + 1) * 128] = jnp.where(
                    (key_number >= first) & (key_number <= last), 0.0, LOW
                )
        tile = store[pl.ds(chip, 2)].reshape(KEYS, 128)
        scores = lax.dot_general(
            packed[which], tile, (((1,), (1,)), ((), ())), preferred_element_type=jnp.float32
        )
        scores = (scores.reshape(HEADS, 2 * rows, KEYS) + bias[...][None]).reshape(both, KEYS)
        before = peak[which]
        now = jnp.maximum(before, jnp.max(scores, axis=1, keepdims=True))
        peak[which] = now
        fade = jnp.exp2((before - now) * SCALE)
        wide = jnp.concatenate([now] * (KEYS // 128), axis=1)
        probs = jnp.exp2((scores - wide) * SCALE).astype(jnp.bfloat16)
        value_lane = lax.broadcasted_iota(jnp.int32, (KEYS, 128), 1) >= HEAD_SIZE
        beside = jnp.where(value_lane, tile, jnp.ones_like(tile))
        total[which] = total[which] * fade + jnp.dot(
            probs, beside, preferred_element_type=jnp.float32
        )

    def answer(which):
        for side in (0, 1):
            high, turned = [], []
            for n in range(HEADS):
                at = (n * 2 + side) * rows
                sums_here = total[which, at : at + rows, :]
                high.append(sums_here / pltpu.roll(sums_here, HEAD_SIZE, axis=1))
                turned.append(pltpu.roll(high[n], HEAD_SIZE, axis=1))
            tiles = (
                jnp.where(upper, high[0], jnp.where(low, turned[0], high[1])),
                jnp.where(upper, jnp.where(low, turned[1], high[2]), turned[2]),
            )
            for i in (0, 1):
                done[2 * which + side, :, i * 128 : (i + 1) * 128] = tiles[i].astype(jnp.bfloat16)

    def reply(n, incoming=False):
        return remote(
            done.at[other(n, False)],
            replies.at[other(n, True) if incoming else mine],
            o_send.at[n],
            o_recv.at[n],
            plane.friend_device(*FRIENDS[n]),
        )

    own_reply = pltpu.make_async_copy(done.at[mine], replies.at[mine], sems.at[7])

    def phase(step, carry):
        @pl.when(step == 1)
        def _():
            for i in range(4):
                for n in (0, 1):
                    for h in (0, 1):
                        along(h, i, n, True).wait_recv()
                        along(h, i, n + 2).start()

        @pl.when(step == 3)
        def _():
            for i in range(4):
                for n in (2, 3):
                    for h in (0, 1):
                        along(h, i, n, True).wait_recv()

        dy = jnp.where(step == 0, 0, jnp.where(step == 1, SIDE - 1, step - 1))
        dy = jnp.where(step == 3, 2, dy)
        row = lax.rem(plane.y + dy, SIDE) * SIDE

        def one(t, carry):
            turn, part = lax.div(t, 2), lax.rem(t, 2)
            dx = jnp.where(turn == 0, 2, jnp.where(turn == 1, 1, jnp.where(turn == 2, 3, 0)))
            which = lax.rem(plane.x + dx, SIDE)
            chip = row + 2 * part

            @pl.when(chip <= member(which))
            def _():
                visit(which, chip)

            @pl.when((step == 3) & (part == 1))
            def _():
                answer(which)

            for column in range(SIDE):

                @pl.when((step == 3) & (part == 1) & (dx == column))
                def _():
                    for n, friend in enumerate(FRIENDS):
                        if friend[0] == column:
                            reply(n).start()
                    if column == 0:
                        own_reply.start()

            return carry

        return lax.fori_loop(0, 2 * SIDE, one, carry)

    lax.fori_loop(0, 4, phase, 0)

    for n in (0, 1):
        weight_copy(n, True).wait_recv()
        weight_copy(2 + n).start()
        weight_copy(5 + n).start()

    swap.wait_send()
    own_table.wait()
    for h in (0, 1):
        for n in range(3):
            across(h, n).wait_send()
        for i in range(4):
            for n in range(4):
                along(h, i, n).wait_send()
    for n in range(len(FRIENDS)):
        ask(n).wait_send()
        tell(n).wait_send()
    for n in range(len(OTHERS)):
        table(n, True).wait_recv()
        table(n).wait_send()
    own_reply.wait()
    for n in range(len(FRIENDS)):
        reply(n, True).wait_recv()
        reply(n).wait_send()
    for p in range(KEY_VALUE_HEADS // 2):
        even, odd = replies[2 * p], replies[2 * p + 1]
        out[:, p * 384 : p * 384 + 128] = even[:, :128]
        out[:, p * 384 + 128 : p * 384 + 256] = jnp.where(
            low, even[:, 128:].astype(jnp.float32), odd[:, :128].astype(jnp.float32)
        ).astype(jnp.bfloat16)
        out[:, p * 384 + 256 : p * 384 + 384] = odd[:, 128:]


BLOCKS = 4
GROUPS = (
    ((0, 0), (2, 0), (0, -1), (0, 1)),
    ((-1, 0), (1, 0), (-1, -1), (-1, 1)),
    ((-1, 2), (1, 2), (1, -1), (1, 1)),
    ((0, 2), (2, 2), (2, -1), (2, 1)),
)
TWO = (0, 2)
ENDS = (-1, 1)


def experts_section(
    plane, weight_copy, own, residual, tables, out,
    rows_in, sums, weights, picked, made, hold_q, hold_r, hold_p, hold_d,
    g_send, g_recv, q_send, q_recv, r_send, r_recv, p_send, p_recv, d_send, d_recv, sem,
):
    rows, width = own.shape
    part_rows = rows // 2
    even = lax.rem(plane.y + plane.x, 2) == 0

    def turned(o, t):
        return jnp.where(even, t, o), jnp.where(even, o, t)

    def place(at):
        return plane.chip(*turned(*at))

    def device(o, t):
        return plane.device(*turned(o, t))

    def part(n):
        return pl.ds(n * part_rows, part_rows)

    def gather(k, src, dst, to):
        return remote(src, dst, g_send.at[k], g_recv.at[k], to)

    def emit(n, incoming=False):
        d = (1, -1)[n]
        at = (0, -d) if incoming else (0, 0)
        return gather(n, own, rows_in.at[place(at)], device(d, 0))

    def pass_on(n, incoming=False):
        at = (2, 0) if incoming else (0, ENDS[n])
        ref = rows_in.at[place(at), part(n)]
        return gather(2 + n, ref, ref, device(0, -ENDS[n]))

    def spread(group, j, n, incoming=False):
        d = (1, -1)[n]
        if group == 0:
            at = (-d, TWO[j]) if incoming else (TWO[j], 0)
            to = device(0, d)
        else:
            at = (ENDS[j], -d) if incoming else (0, ENDS[j])
            to = device(d, 0)
        ref = rows_in.at[place(at)]
        src = own if at == (0, 0) else ref
        return gather(4 + group * 8 + j * 4 + n, src, ref, to)

    def relay(group, j, n, incoming=False):
        if group == 0:
            at = (TWO[j], 2) if incoming else (ENDS[n], TWO[j])
            to = device(-ENDS[n], 0)
        else:
            at = (2, ENDS[j]) if incoming else (ENDS[j], ENDS[n])
            to = device(0, -ENDS[n])
        ref = rows_in.at[place(at), part(n)]
        return gather(4 + group * 8 + j * 4 + 2 + n, ref, ref, to)

    mine = pltpu.make_async_copy(own, rows_in.at[place((0, 0))], sem)
    for n in (0, 1):
        emit(n).start()
    for n in (0, 1):
        spread(0, 0, n).start()
    mine.start()
    for j in (0, 1):
        emit(j, True).wait_recv()
        pass_on(j).start()
        for n in (0, 1):
            spread(1, j, n).start()
    for n in (0, 1):
        pass_on(n, True).wait_recv()
    for n in (0, 1):
        spread(0, 1, n).start()
    for n in (2, 3):
        weight_copy(n, True).wait_recv()
    weight_copy(7).start()
    mine.wait()
    for n in (4, 5, 6, 7):
        weight_copy(n, True).wait_recv()

    def far(group, j):
        return (TWO[j], 2) if group == 0 else (2, ENDS[j])

    def near(group, j, side):
        return (ENDS[side], TWO[j]) if group == 0 else (ENDS[j], ENDS[side])

    def line(group, along_first):
        return (lambda d: device(d, 0)) if (group == 0) == along_first else (lambda d: device(0, d))

    def give_far(group, j, n):
        k = group * 4 + j * 2 + n
        return remote(
            sums.at[place(far(group, j)), part(n)],
            hold_q.at[k],
            q_send.at[k],
            q_recv.at[k],
            line(group, False)(ENDS[n]),
        )

    def give_near(group, j, side, late):
        k = group * 4 + j * 2 + side
        span = part(side if late else 1 - side)
        return remote(
            sums.at[place(near(group, j, side)), span],
            hold_r.at[k, span],
            r_send.at[2 * k + late],
            r_recv.at[2 * k + late],
            line(group, True)(ENDS[side]),
        )

    def give_across(n):
        return remote(
            sums.at[place((2, 0)), part(n)],
            hold_p.at[n],
            p_send.at[n],
            p_recv.at[n],
            device(ENDS[n], 0),
        )

    def give_back(side, late):
        span = part(side if late else 1 - side)
        return remote(
            sums.at[place((0, ENDS[side])), span],
            hold_d.at[side, span],
            d_send.at[2 * side + late],
            d_recv.at[2 * side + late],
            device(0, ENDS[side]),
        )

    PAIRS = [(0, 1), (1, 0), (1, 1), (0, 0)]
    slot = lax.broadcasted_iota(jnp.int32, (SLOTS, rows), 0).astype(jnp.float32)

    def group_step(g, carry):
        for when, j in ((1, 0), (2, 1)):

            @pl.when(g == when)
            def _():
                for n in (0, 1):
                    for group in (0, 1):
                        spread(group, j, n, True).wait_recv()
                        relay(group, j, n).start()

        @pl.when(g == 3)
        def _():
            for group, j in PAIRS:
                for n in (0, 1):
                    relay(group, j, n, True).wait_recv()
            for group, j in PAIRS:
                for side in (0, 1):
                    give_near(group, j, side, 0).start()

        ids = []
        for j in range(BLOCKS):
            at = place(GROUPS[3][j])
            for k in range(3):
                at = jnp.where(g == k, place(GROUPS[k][j]), at)
            ids.append(at)

        def hits(j, e):
            return tables[ids[j], 2 + e : 3 + e, :] == slot

        def choice(j):
            both = jnp.concatenate([hits(j, 0), hits(j, 1)], axis=0)
            return jnp.where(both, 1.0, 0.0).astype(jnp.bfloat16)

        for j in range(BLOCKS):
            picked[j] = jnp.dot(
                choice(j), rows_in[ids[j]], preferred_element_type=jnp.float32
            ).astype(jnp.bfloat16)
        for e in (0, 1):
            chosen = picked[:, e * SLOTS : (e + 1) * SLOTS, :].reshape(BLOCKS * SLOTS, width)
            gate = jnp.dot(chosen, weights[e, 0], preferred_element_type=jnp.float32)
            up = jnp.dot(chosen, weights[e, 1], preferred_element_type=jnp.float32)
            units = (gate / (1.0 + jnp.exp(-gate)) * up).astype(jnp.bfloat16)
            result = lax.dot_general(
                units, weights[e, 2], (((1,), (1,)), ((), ())), preferred_element_type=jnp.float32
            )
            for j in range(BLOCKS):
                gain = jnp.sum(
                    jnp.where(hits(j, e), tables[ids[j], e : e + 1, :], 0.0),
                    axis=1,
                    keepdims=True,
                )
                made[j, e * SLOTS : (e + 1) * SLOTS, :] = (
                    result[j * SLOTS : (j + 1) * SLOTS, :] * gain
                ).astype(jnp.bfloat16)
        for j in range(BLOCKS):
            sums[ids[j]] = lax.dot_general(
                choice(j), made[j], (((0,), (0,)), ((), ())), preferred_element_type=jnp.float32
            ).astype(jnp.bfloat16)
        return carry

    lax.fori_loop(0, len(GROUPS), group_step, 0)

    for group, j in PAIRS:
        for n in (0, 1):
            give_far(group, j, n).start()

    def add(at, held):
        sums[at] = (sums[at].astype(jnp.float32) + held.astype(jnp.float32)).astype(jnp.bfloat16)

    def relay_sums(group, j):
        for side in (0, 1):
            k = group * 4 + j * 2 + side
            give_far(group, j, side).wait_recv()
            add((place(near(group, j, side)), part(side)), hold_q[k])
            give_near(group, j, side, 1).start()

    def total(group, j):
        for side in (0, 1):
            for late in (0, 1):
                give_near(group, j, side, late).wait_recv()
        at = place((TWO[j], 0) if group == 0 else (0, ENDS[j]))
        k = group * 4 + j * 2
        return at, (
            sums[at].astype(jnp.float32)
            + hold_r[k].astype(jnp.float32)
            + hold_r[k + 1].astype(jnp.float32)
        )

    for group, j in PAIRS[:3]:
        relay_sums(group, j)
    at, value = total(0, 1)
    sums[at] = value.astype(jnp.bfloat16)
    for n in (0, 1):
        give_across(n).start()
    relay_sums(0, 0)
    for side in (0, 1):
        at, value = total(1, side)
        sums[at] = value.astype(jnp.bfloat16)
        give_back(side, 0).start()
    for side in (0, 1):
        give_across(side).wait_recv()
        add((place((0, ENDS[side])), part(side)), hold_p[side])
        give_back(side, 1).start()
    _, value = total(0, 0)
    out_sum = value + residual[...]
    for side in (0, 1):
        for late in (0, 1):
            give_back(side, late).wait_recv()
    out[...] = (
        out_sum + hold_d[0].astype(jnp.float32) + hold_d[1].astype(jnp.float32)
    ).astype(out.dtype)

    for n in (0, 1):
        emit(n).wait_send()
        pass_on(n).wait_send()
        give_across(n).wait_send()
        for late in (0, 1):
            give_back(n, late).wait_send()
    for n in range(8):
        weight_copy(n).wait_send()
    for group, j in PAIRS:
        for n in (0, 1):
            spread(group, j, n).wait_send()
            relay(group, j, n).wait_send()
            give_far(group, j, n).wait_send()
            for late in (0, 1):
                give_near(group, j, n, late).wait_send()


def normed(values, gain):
    mean_square = jnp.mean(values * values, axis=1, keepdims=True)
    return (values * lax.rsqrt(mean_square + epsilon) * gain[None]).astype(jnp.bfloat16)


def rotation_tables(plane, prompt_start, cosine, sine):
    rows = prompt_start.shape[1]
    half = HEAD_SIZE // 2
    lane = lax.broadcasted_iota(jnp.int32, (rows, 128), 1)
    begin = jnp.broadcast_to(prompt_start[...].astype(jnp.float32), (rows, rows)).T
    first = (plane.chip(0, 0) * 2 + plane.core) * rows
    position = first + lax.broadcasted_iota(jnp.int32, (rows, 128), 0)
    power = lax.rem(lane, half).astype(jnp.float32) / half
    angle = (position.astype(jnp.float32) - begin) * jnp.exp(power * -math.log(10000.0))
    cosine[...] = jnp.cos(angle)
    sine[...] = jnp.where(lax.rem(lane, HEAD_SIZE) < half, -jnp.sin(angle), jnp.sin(angle))


def layer_kernel(
    hidden, attn_gain, wq, wk, wv, wo, prompt_start, ffn_gain, routes, route_weights,
    first,
    out, key_cache, value_cache,
    query_w, key_w, value_w, output_w, own_in, residual, cosine, sine,
    queries, pairs, starts, given, attention, tables,
    near, store, asked, begin, begins, packed, peak, total, bias, done, replies,
    rows_in, sums, weights, picked, made, hold_q, hold_r, hold_p, hold_d,
    *sems,
):
    attention_sems, expert_sems, (w_send, w_recv, load_sems, row_sem) = (
        sems[:11],
        sems[11:21],
        sems[21:],
    )
    plane = Plane()
    core = plane.core
    rows, width = hidden.shape
    arrived = greet(plane)

    def lanes(r):
        return pl.ds(r * 128, 128)

    def weight_copy(n, incoming=False):
        half = width // 2
        e = 1 - core if incoming and n >= 4 else core
        if n < 2:
            src, dst = first, weights.at[e, :, :, lanes(1 + n)]
            to = plane.level((1, -1)[n])
        elif n < 4:
            span = pl.ds((n - 2) * half, half)
            src = weights.at[e, :, span, lanes(n - 1)]
            dst = weights.at[e, :, span, lanes(3)]
            to = plane.level((1, -1)[n - 2])
        else:
            dst = weights.at[e, :, :, lanes(n - 4)]
            src = first if n == 4 else dst
            to = plane.partner()
        return remote(src, dst, w_send.at[n], w_recv.at[n], to)

    loads = [
        pltpu.make_async_copy(src, dst, load_sems.at[n])
        for n, (src, dst) in enumerate(
            (
                (wk, key_w),
                (wv, value_w),
                (wq, query_w),
                (wo, output_w),
                (first, weights.at[core, :, :, lanes(0)]),
            )
        )
    ]
    for n in (2, 0, 1):
        loads[n].start()
    own_in[...] = normed(hidden[...].astype(jnp.float32), attn_gain[...])
    rotation_tables(plane, prompt_start, cosine, sine)
    arrived()
    for n in (0, 1, 4):
        weight_copy(n).start()

    lane = lax.broadcasted_iota(jnp.int32, (rows, 128), 1)
    first_half = lax.rem(lane, HEAD_SIZE) < HEAD_SIZE // 2

    def rotated(tile):
        other = jnp.where(
            first_half,
            pltpu.roll(tile, 128 - HEAD_SIZE // 2, axis=1),
            pltpu.roll(tile, HEAD_SIZE // 2, axis=1),
        )
        return tile * cosine[...] + other * sine[...]

    def project_keys():
        for load in loads[3:]:
            load.start()
        loads[0].wait()
        keys = jnp.dot(own_in[...], key_w[...], preferred_element_type=jnp.float32)
        loads[1].wait()
        values = jnp.dot(own_in[...], value_w[...], preferred_element_type=jnp.float32)
        value_cache[...] = values.astype(jnp.bfloat16)
        low = lane < HEAD_SIZE
        for p in range(KEY_VALUE_HEADS // 2):
            at = slice(p * 128, (p + 1) * 128)
            key, value = rotated(keys[:, at]), values[:, at]
            key_cache[:, at] = key.astype(jnp.bfloat16)
            sides = (
                jnp.where(low, key, pltpu.roll(value, HEAD_SIZE, axis=1)),
                jnp.where(low, pltpu.roll(key, HEAD_SIZE, axis=1), value),
            )
            for c in (0, 1):
                to = (c * SIDE + p) * 128
                pairs[:, to : to + 128] = sides[c].astype(jnp.bfloat16)

    def project_queries():
        starts[...] = jnp.broadcast_to(prompt_start[...].astype(jnp.float32), starts.shape)
        loads[2].wait()
        for c in range(3):
            part = jnp.dot(
                own_in[...],
                query_w[:, c * 512 : (c + 1) * 512],
                preferred_element_type=jnp.float32,
            )
            for p in range(4):
                at = c * 512 + p * 128
                queries[:, at : at + 128] = rotated(part[:, p * 128 : (p + 1) * 128]).astype(
                    jnp.bfloat16
                )

    def make_tables():
        expert = lax.broadcasted_iota(jnp.int32, (EXPERTS, rows), 0)
        gains = jnp.zeros((EXPERTS, rows), jnp.float32)
        named = jnp.zeros((EXPERTS, rows), jnp.float32)
        for j in range(TOP):
            hit = routes[j : j + 1, :] == expert
            gains = gains + jnp.where(hit, route_weights[j : j + 1, :], 0.0)
            named = named + jnp.where(hit, 1.0, 0.0)
        earlier = lax.broadcasted_iota(jnp.int32, (rows, rows), 0) < lax.broadcasted_iota(
            jnp.int32, (rows, rows), 1
        )
        ranks = jnp.dot(
            named.astype(jnp.bfloat16),
            jnp.where(earlier, 1.0, 0.0).astype(jnp.bfloat16),
            preferred_element_type=jnp.float32,
        )
        ranks = jnp.where(named > 0.0, ranks, -1.0)
        given[...] = jnp.zeros_like(given)
        for c in range(CHIPS):
            given[c, 0:2, :] = gains[2 * c : 2 * c + 2, :]
            given[c, 2:4, :] = ranks[2 * c : 2 * c + 2, :]

    attention_section(
        plane, weight_copy, project_keys, project_queries, make_tables,
        queries, pairs, starts, given, attention, tables,
        near, store, asked, begin, begins, packed, peak, total, bias, done, replies,
        *attention_sems,
    )

    loads[3].wait()
    for c in range(3):
        at = slice(c * 512, (c + 1) * 512)
        residual[:, at] = hidden[:, at].astype(jnp.float32) + jnp.dot(
            attention[...], output_w[:, at], preferred_element_type=jnp.float32
        )
    own_in[...] = normed(residual[...], ffn_gain[...])
    loads[4].wait()

    experts_section(
        plane, weight_copy, own_in, residual, tables, out,
        rows_in, sums, weights, picked, made, hold_q, hold_r, hold_p, hold_d,
        *expert_sems, row_sem,
    )


def run_layer(hidden, attn_gain, wq, wk, wv, wo, starts, ffn_gain, routes, gains, first):
    rows, width = hidden.shape
    cache = wk.shape[1]
    dma = pltpu.SemaphoreType.DMA
    vmem = pl.BlockSpec(memory_space=pltpu.VMEM)
    hbm = pl.BlockSpec(memory_space=pl.ANY)

    def brief(*shape):
        return pltpu.VMEM(shape, jnp.bfloat16)

    def full(*shape):
        return pltpu.VMEM(shape, jnp.float32)

    others = len(OTHERS)
    friends = len(FRIENDS)
    counts = (others, 6, 32, 2 * friends, friends)
    attention_sems = [dma((n,)) for n in counts for _ in (0, 1)] + [dma((8,))]
    expert_sems = [dma((n,)) for n in (20, 8, 16, 2, 4) for _ in (0, 1)]
    both = 2 * HEADS * rows
    return pl.pallas_call(
        layer_kernel,
        out_shape=(
            jax.ShapeDtypeStruct((rows, width), jnp.bfloat16),
            jax.ShapeDtypeStruct((rows, cache), jnp.bfloat16),
            jax.ShapeDtypeStruct((rows, cache), jnp.bfloat16),
        ),
        in_specs=[vmem, vmem, hbm, hbm, hbm, hbm] + [vmem] * 4 + [hbm],
        out_specs=(vmem,) * 3,
        scratch_shapes=[
            brief(*wq.shape),
            brief(*wk.shape),
            brief(*wv.shape),
            brief(*wo.shape),
            brief(rows, width),
            full(rows, width),
            full(rows, 128),
            full(rows, 128),
            brief(rows, width),
            brief(rows, 2 * cache),
            full(8, rows),
            full(CHIPS, 8, rows),
            brief(rows, width),
            full(CHIPS, 8, rows),
            brief(rows, 512),
            brief(CHIPS, 2 * rows, 128),
            brief(KEY_VALUE_HEADS, rows, ASK),
            full(KEY_VALUE_HEADS, 8, rows),
            full(KEY_VALUE_HEADS, rows, rows),
            brief(SIDE, both, 128),
            full(SIDE, both, 128),
            full(SIDE, both, 128),
            full(2 * rows, KEYS),
            brief(KEY_VALUE_HEADS, rows, ASK),
            brief(KEY_VALUE_HEADS, rows, ASK),
            brief(CHIPS, rows, width),
            brief(CHIPS, rows, width),
            brief(2, 3, width, FF),
            brief(BLOCKS, 2 * SLOTS, width),
            brief(BLOCKS, 2 * SLOTS, width),
            brief(8, rows // 2, width),
            brief(8, rows, width),
            brief(2, rows // 2, width),
            brief(2, rows, width),
            *attention_sems,
            *expert_sems,
            dma((8,)),
            dma((8,)),
            dma((5,)),
            dma,
        ],
        compiler_params=pltpu.CompilerParams(
            collective_id=0, has_side_effects=True, vmem_limit_bytes=63 << 20
        ),
        name="layer",
    )(
        hidden, attn_gain, wq, wk, wv, wo, starts, ffn_gain, routes, gains, first
    )


def publish(*results):
    def kernel(*refs):
        for src, dst in zip(refs[: len(results)], refs[len(results) :]):
            dst[...] = src[...]

    vmem = pl.BlockSpec(memory_space=pltpu.VMEM)
    return pl.pallas_call(
        kernel,
        out_shape=tuple(jax.ShapeDtypeStruct(r.shape, r.dtype) for r in results),
        in_specs=[vmem] * len(results),
        out_specs=(vmem,) * len(results),
        name="publish",
    )(*results)


def shards(
    hidden,
    attn_gain,
    query_weight,
    key_matrix,
    value_matrix,
    output_weight,
    prompt_start,
    ffn_gain,
    routes,
    route_weights,
    expert_weights,
):
    results = run_layer(
        hidden,
        attn_gain,
        query_weight,
        key_matrix,
        value_matrix,
        output_weight,
        prompt_start[None],
        ffn_gain,
        routes.T,
        route_weights.T,
        expert_weights[0],
    )
    return publish(*results)


def solution(mesh):
    in_specs = (
        P(("req", "exp"), None),
        P(),
        P(),
        P(),
        P(),
        P(),
        P(("req", "exp")),
        P(),
        P(("req", "exp"), None),
        P(("req", "exp"), None),
        P("exp", None, None, "req"),
    )
    out_specs = (P(("req", "exp"), None), P(("req", "exp"), None), P(("req", "exp"), None))
    return jax.shard_map(shards, mesh=mesh, in_specs=in_specs, out_specs=out_specs, check_vma=False)
```

```python
import math

import jax
import jax.numpy as jnp
from jax import lax
from jax.experimental import pallas as pl
from jax.experimental.pallas import tpu as pltpu
from jax.sharding import PartitionSpec as P

QUERY_HEADS = 24
KEY_VALUE_HEADS = 8
HEAD_SIZE = 64
TOP = 8
SIDE = 4
CHIPS = SIDE * SIDE
EXPERTS = 32
SLOTS = 64
FF = 512


epsilon = 1e-05


class Plane:
    def __init__(self):
        me = lax.axis_index("exp")
        self.core = lax.rem(me, 2)
        chip = lax.div(me, 2)
        self.y = lax.div(chip, SIDE)
        self.x = lax.rem(chip, SIDE)

    def chip(self, dy, dx):
        return lax.rem(self.y + dy + SIDE, SIDE) * SIDE + lax.rem(self.x + dx + SIDE, SIDE)

    def device(self, dy, dx):
        return {"exp": self.chip(dy, dx) * 2 + self.core}

    def level(self, dz):
        return {"req": lax.rem(lax.axis_index("req") + dz + SIDE, SIDE)}

    def partner(self):
        return {"exp": self.chip(0, 0) * 2 + 1 - self.core}

    def friend(self, dx, dc):
        x = lax.rem(self.x + dx + SIDE, SIDE)
        y = self.y if dx % 2 == 0 else SIDE - 1 - self.y
        core = 1 - self.core if dc else self.core
        return y * SIDE + x, core, 2 * x + core

    def friend_device(self, dx, dc):
        chip, core, _ = self.friend(dx, dc)
        return {"exp": chip * 2 + core}


FRIENDS = tuple((dx, dc) for dx in range(SIDE) for dc in (0, 1) if dx or dc)
OTHERS = tuple((dy, dx) for dy in range(SIDE) for dx in range(SIDE) if dy or dx)


def greet(plane):
    barrier = pltpu.get_barrier_semaphore()
    devices = [plane.device(dy, dx) for dy, dx in OTHERS]
    devices += [plane.friend_device(dx, 1) for dx in range(SIDE)]
    devices += [plane.level(1), plane.level(-1)]
    for device in devices:
        pl.semaphore_signal(
            barrier, inc=1, device_id=device, device_id_type=pl.DeviceIdType.MESH
        )
    return lambda: pl.semaphore_wait(barrier, len(devices))


def remote(src, dst, send, recv, device):
    return pltpu.make_async_remote_copy(
        src_ref=src,
        dst_ref=dst,
        send_sem=send,
        recv_sem=recv,
        device_id=device,
        device_id_type=pl.DeviceIdType.MESH,
    )


KEYS = 512
HEADS = QUERY_HEADS // KEY_VALUE_HEADS
ASK = 256
LOW = -1e30
SCALE = HEAD_SIZE**-0.5 * 1.4426950408889634
ACROSS = (0, -1, 1, 2)


def attention_section(
    plane, weight_copy, project_keys, project_queries, make_tables,
    queries, pairs, starts, given, out, held,
    near, store, asked, begin, begins, packed, peak, total, bias, done, replies,
    give, take, x_send, x_recv, y_send, y_recv, q_send, q_recv, o_send, o_recv, sems,
):
    core = plane.core
    here = plane.chip(0, 0)
    rows = queries.shape[0]
    mine = 2 * plane.x + core

    def lanes(at, size):
        return pl.ds(pl.multiple_of(at * size, size), size)

    swap = remote(
        pairs.at[:, lanes(1 - core, 512)], near, sems.at[0], sems.at[1], plane.partner()
    )

    def source(h, dx):
        x = lax.rem(plane.x + dx + SIDE, SIDE)
        if h == 0:
            return pairs.at[:, lanes(SIDE * core + x, 128)]
        return near.at[:, lanes(x, 128)]

    def slot(h, dy, dx, part=None):
        low = (core if h == 0 else 1 - core) * rows
        size = rows
        if part is not None:
            size = rows // 2
            low = low + part * size
        return store.at[plane.chip(dy, dx), pl.ds(pl.multiple_of(low, size), size)]

    def keep(h):
        return pltpu.make_async_copy(source(h, 0), slot(h, 0, 0), sems.at[2 + h])

    def across(h, n, incoming=False):
        dx = (1, -1, 2)[n]
        return remote(
            source(h, dx),
            slot(h, 0, -dx if incoming else 0),
            x_send.at[3 * h + n],
            x_recv.at[3 * h + n],
            plane.device(0, dx),
        )

    def along(h, i, n, incoming=False):
        dx = ACROSS[i]
        at, part, dy = ((0, None, 1), (0, None, -1), (-1, 0, 1), (1, 1, -1))[n]
        place = slot(h, at - dy if incoming else at, dx, part)
        src = source(h, 0) if (i == 0 and n < 2) else place
        if i == 0 and n < 2 and not incoming:
            place = slot(h, 0, 0)
        k = (h * 4 + i) * 4 + n
        return remote(src, place, y_send.at[k], y_recv.at[k], plane.device(dy, 0))

    def other(n, incoming):
        dx, dc = FRIENDS[n]
        return plane.friend(-dx if incoming else dx, dc)[2]

    def asking(head):
        return pl.ds(pl.multiple_of(lax.div(3 * head, 2) * 128, 128), ASK)

    def ask(n, incoming=False):
        return remote(
            queries.at[:, asking(other(n, False))],
            asked.at[other(n, True) if incoming else mine],
            q_send.at[n],
            q_recv.at[n],
            plane.friend_device(*FRIENDS[n]),
        )

    def tell(n, incoming=False):
        return remote(
            starts,
            begin.at[other(n, True) if incoming else mine],
            q_send.at[len(FRIENDS) + n],
            q_recv.at[len(FRIENDS) + n],
            plane.friend_device(*FRIENDS[n]),
        )

    def table(n, incoming=False):
        dy, dx = OTHERS[n]
        return remote(
            given.at[plane.chip(dy, dx)],
            held.at[plane.chip(-dy, -dx) if incoming else here],
            give.at[n],
            take.at[n],
            plane.device(dy, dx),
        )

    own_asked = pltpu.make_async_copy(
        queries.at[:, asking(mine)], asked.at[mine], sems.at[4]
    )
    own_begin = pltpu.make_async_copy(starts, begin.at[mine], sems.at[5])
    own_table = pltpu.make_async_copy(given.at[here], held.at[here], sems.at[6])

    project_queries()
    own_asked.start()
    own_begin.start()
    for n in range(len(FRIENDS)):
        ask(n).start()
        tell(n).start()
    project_keys()
    swap.start()
    for h in (0, 1):
        if h == 1:
            make_tables()
            own_table.start()
            swap.wait_recv()
        keep(h).start()
        for n in range(3):
            across(h, n).start()
        along(h, 0, 0).start()
        along(h, 0, 1).start()
    own_asked.wait()
    own_begin.wait()
    for n in range(len(FRIENDS)):
        ask(n, True).wait_recv()
        tell(n, True).wait_recv()

    lane = lax.broadcasted_iota(jnp.int32, (rows, 128), 1)
    low = lane < HEAD_SIZE
    upper = core == 1
    for which in range(SIDE):
        for side in (0, 1):
            begins[2 * which + side] = jnp.broadcast_to(
                begin[2 * which + side, 0:1, :], (rows, rows)
            ).T
            tiles = [
                asked[2 * which + side, :, i * 128 : (i + 1) * 128].astype(jnp.float32)
                for i in (0, 1)
            ]
            turned = [pltpu.roll(tile, HEAD_SIZE, axis=1) for tile in tiles]
            heads = (
                jnp.where(upper, turned[0], tiles[0]),
                jnp.where(upper, tiles[1], turned[0]),
                jnp.where(upper, turned[1], tiles[1]),
            )
            for n in range(HEADS):
                at = (n * 2 + side) * rows
                packed[which, at : at + rows, :] = jnp.where(low, heads[n], 0.0).astype(
                    jnp.bfloat16
                )
    peak[...] = jnp.full_like(peak, LOW)
    total[...] = jnp.zeros_like(total)
    for n in range(3):
        i = (1, 2, 3)[n]
        for h in (0, 1):
            across(h, n, True).wait_recv()
            along(h, i, 0).start()
            along(h, i, 1).start()
    for n in range(len(OTHERS)):
        table(n).start()

    for h in (0, 1):
        keep(h).wait()

    both = 2 * HEADS * rows
    lane_number = lax.broadcasted_iota(jnp.int32, (1, 128), 1).astype(jnp.float32)
    row_number = lax.broadcasted_iota(jnp.int32, (rows, 128), 0).astype(jnp.float32)

    def member(which):
        flip = lax.rem(plane.x + which, 2)
        return jnp.where(flip == 0, plane.y, SIDE - 1 - plane.y) * SIDE + which

    def visit(which, chip):
        stream_chip = member(which)
        at = chip * (2 * rows)
        shift = (stream_chip * (2 * rows) - at).astype(jnp.float32)
        base = at.astype(jnp.float32)
        for side in (0, 1):
            first = begins[2 * which + side] - base
            last = row_number + (shift + side * rows)
            for j in range(KEYS // 128):
                key_number = lane_number + j * 128
                bias[side * rows : (side + 1) * rows, j * 128 : (j + 1) * 128] = jnp.where(
                    (key_number >= first) & (key_number <= last), 0.0, LOW
                )
        tile = store[pl.ds(chip, 2)].reshape(KEYS, 128)
        scores = lax.dot_general(
            packed[which], tile, (((1,), (1,)), ((), ())), preferred_element_type=jnp.float32
        )
        scores = (scores.reshape(HEADS, 2 * rows, KEYS) + bias[...][None]).reshape(both, KEYS)
        before = peak[which]
        now = jnp.maximum(before, jnp.max(scores, axis=1, keepdims=True))
        peak[which] = now
        fade = jnp.exp2((before - now) * SCALE)
        wide = jnp.concatenate([now] * (KEYS // 128), axis=1)
        probs = jnp.exp2((scores - wide) * SCALE).astype(jnp.bfloat16)
        value_lane = lax.broadcasted_iota(jnp.int32, (KEYS, 128), 1) >= HEAD_SIZE
        beside = jnp.where(value_lane, tile, jnp.ones_like(tile))
        total[which] = total[which] * fade + jnp.dot(
            probs, beside, preferred_element_type=jnp.float32
        )

    def answer(which):
        for side in (0, 1):
            high, turned = [], []
            for n in range(HEADS):
                at = (n * 2 + side) * rows
                sums_here = total[which, at : at + rows, :]
                high.append(sums_here / pltpu.roll(sums_here, HEAD_SIZE, axis=1))
                turned.append(pltpu.roll(high[n], HEAD_SIZE, axis=1))
            tiles = (
                jnp.where(upper, high[0], jnp.where(low, turned[0], high[1])),
                jnp.where(upper, jnp.where(low, turned[1], high[2]), turned[2]),
            )
            for i in (0, 1):
                done[2 * which + side, :, i * 128 : (i + 1) * 128] = tiles[i].astype(jnp.bfloat16)

    def reply(n, incoming=False):
        return remote(
            done.at[other(n, False)],
            replies.at[other(n, True) if incoming else mine],
            o_send.at[n],
            o_recv.at[n],
            plane.friend_device(*FRIENDS[n]),
        )

    own_reply = pltpu.make_async_copy(done.at[mine], replies.at[mine], sems.at[7])

    def phase(step, carry):
        @pl.when(step == 1)
        def _():
            for i in range(4):
                for n in (0, 1):
                    for h in (0, 1):
                        along(h, i, n, True).wait_recv()
                        along(h, i, n + 2).start()

        @pl.when(step == 3)
        def _():
            for i in range(4):
                for n in (2, 3):
                    for h in (0, 1):
                        along(h, i, n, True).wait_recv()

        dy = jnp.where(step == 0, 0, jnp.where(step == 1, SIDE - 1, step - 1))
        dy = jnp.where(step == 3, 2, dy)
        row = lax.rem(plane.y + dy, SIDE) * SIDE

        def one(t, carry):
            turn, part = lax.div(t, 2), lax.rem(t, 2)
            dx = jnp.where(turn == 0, 2, jnp.where(turn == 1, 1, jnp.where(turn == 2, 3, 0)))
            which = lax.rem(plane.x + dx, SIDE)
            chip = row + 2 * part

            @pl.when(chip <= member(which))
            def _():
                visit(which, chip)

            @pl.when((step == 3) & (part == 1))
            def _():
                answer(which)

            for column in range(SIDE):

                @pl.when((step == 3) & (part == 1) & (dx == column))
                def _():
                    for n, friend in enumerate(FRIENDS):
                        if friend[0] == column:
                            reply(n).start()
                    if column == 0:
                        own_reply.start()

            return carry

        return lax.fori_loop(0, 2 * SIDE, one, carry)

    lax.fori_loop(0, 4, phase, 0)

    for n in (0, 1):
        weight_copy(n, True).wait_recv()
        weight_copy(2 + n).start()
        weight_copy(5 + n).start()

    swap.wait_send()
    own_table.wait()
    for h in (0, 1):
        for n in range(3):
            across(h, n).wait_send()
        for i in range(4):
            for n in range(4):
                along(h, i, n).wait_send()
    for n in range(len(FRIENDS)):
        ask(n).wait_send()
        tell(n).wait_send()
    for n in range(len(OTHERS)):
        table(n, True).wait_recv()
        table(n).wait_send()
    own_reply.wait()
    for n in range(len(FRIENDS)):
        reply(n, True).wait_recv()
        reply(n).wait_send()
    for p in range(KEY_VALUE_HEADS // 2):
        even, odd = replies[2 * p], replies[2 * p + 1]
        out[:, p * 384 : p * 384 + 128] = even[:, :128]
        out[:, p * 384 + 128 : p * 384 + 256] = jnp.where(
            low, even[:, 128:].astype(jnp.float32), odd[:, :128].astype(jnp.float32)
        ).astype(jnp.bfloat16)
        out[:, p * 384 + 256 : p * 384 + 384] = odd[:, 128:]


BLOCKS = 4
GROUPS = (
    ((0, 0), (2, 0), (0, -1), (0, 1)),
    ((-1, 0), (1, 0), (-1, -1), (-1, 1)),
    ((-1, 2), (1, 2), (1, -1), (1, 1)),
    ((0, 2), (2, 2), (2, -1), (2, 1)),
)
TWO = (0, 2)
ENDS = (-1, 1)


def experts_section(
    plane, weight_copy, own, residual, tables, out,
    rows_in, sums, weights, picked, made, hold_q, hold_r, hold_p, hold_d,
    g_send, g_recv, q_send, q_recv, r_send, r_recv, p_send, p_recv, d_send, d_recv, sem,
):
    rows, width = own.shape
    part_rows = rows // 2
    even = lax.rem(plane.y + plane.x, 2) == 0

    def turned(o, t):
        return jnp.where(even, t, o), jnp.where(even, o, t)

    def place(at):
        return plane.chip(*turned(*at))

    def device(o, t):
        return plane.device(*turned(o, t))

    def part(n):
        return pl.ds(n * part_rows, part_rows)

    def gather(k, src, dst, to):
        return remote(src, dst, g_send.at[k], g_recv.at[k], to)

    def emit(n, incoming=False):
        d = (1, -1)[n]
        at = (0, -d) if incoming else (0, 0)
        return gather(n, own, rows_in.at[place(at)], device(d, 0))

    def pass_on(n, incoming=False):
        at = (2, 0) if incoming else (0, ENDS[n])
        ref = rows_in.at[place(at), part(n)]
        return gather(2 + n, ref, ref, device(0, -ENDS[n]))

    def spread(group, j, n, incoming=False):
        d = (1, -1)[n]
        if group == 0:
            at = (-d, TWO[j]) if incoming else (TWO[j], 0)
            to = device(0, d)
        else:
            at = (ENDS[j], -d) if incoming else (0, ENDS[j])
            to = device(d, 0)
        ref = rows_in.at[place(at)]
        src = own if at == (0, 0) else ref
        return gather(4 + group * 8 + j * 4 + n, src, ref, to)

    def relay(group, j, n, incoming=False):
        if group == 0:
            at = (TWO[j], 2) if incoming else (ENDS[n], TWO[j])
            to = device(-ENDS[n], 0)
        else:
            at = (2, ENDS[j]) if incoming else (ENDS[j], ENDS[n])
            to = device(0, -ENDS[n])
        ref = rows_in.at[place(at), part(n)]
        return gather(4 + group * 8 + j * 4 + 2 + n, ref, ref, to)

    mine = pltpu.make_async_copy(own, rows_in.at[place((0, 0))], sem)
    for n in (0, 1):
        emit(n).start()
    for n in (0, 1):
        spread(0, 0, n).start()
    mine.start()
    for j in (0, 1):
        emit(j, True).wait_recv()
        pass_on(j).start()
        for n in (0, 1):
            spread(1, j, n).start()
    for n in (0, 1):
        pass_on(n, True).wait_recv()
    for n in (0, 1):
        spread(0, 1, n).start()
    for n in (2, 3):
        weight_copy(n, True).wait_recv()
    weight_copy(7).start()
    mine.wait()
    for n in (4, 5, 6, 7):
        weight_copy(n, True).wait_recv()

    def far(group, j):
        return (TWO[j], 2) if group == 0 else (2, ENDS[j])

    def near(group, j, side):
        return (ENDS[side], TWO[j]) if group == 0 else (ENDS[j], ENDS[side])

    def line(group, along_first):
        return (lambda d: device(d, 0)) if (group == 0) == along_first else (lambda d: device(0, d))

    def give_far(group, j, n):
        k = group * 4 + j * 2 + n
        return remote(
            sums.at[place(far(group, j)), part(n)],
            hold_q.at[k],
            q_send.at[k],
            q_recv.at[k],
            line(group, False)(ENDS[n]),
        )

    def give_near(group, j, side, late):
        k = group * 4 + j * 2 + side
        span = part(side if late else 1 - side)
        return remote(
            sums.at[place(near(group, j, side)), span],
            hold_r.at[k, span],
            r_send.at[2 * k + late],
            r_recv.at[2 * k + late],
            line(group, True)(ENDS[side]),
        )

    def give_across(n):
        return remote(
            sums.at[place((2, 0)), part(n)],
            hold_p.at[n],
            p_send.at[n],
            p_recv.at[n],
            device(ENDS[n], 0),
        )

    def give_back(side, late):
        span = part(side if late else 1 - side)
        return remote(
            sums.at[place((0, ENDS[side])), span],
            hold_d.at[side, span],
            d_send.at[2 * side + late],
            d_recv.at[2 * side + late],
            device(0, ENDS[side]),
        )

    PAIRS = [(0, 1), (1, 0), (1, 1), (0, 0)]
    slot = lax.broadcasted_iota(jnp.int32, (SLOTS, rows), 0).astype(jnp.float32)

    def group_step(g, carry):
        for when, j in ((1, 0), (2, 1)):

            @pl.when(g == when)
            def _():
                for n in (0, 1):
                    for group in (0, 1):
                        spread(group, j, n, True).wait_recv()
                        relay(group, j, n).start()

        @pl.when(g == 3)
        def _():
            for group, j in PAIRS:
                for n in (0, 1):
                    relay(group, j, n, True).wait_recv()
            for group, j in PAIRS:
                for side in (0, 1):
                    give_near(group, j, side, 0).start()

        ids = []
        for j in range(BLOCKS):
            at = place(GROUPS[3][j])
            for k in range(3):
                at = jnp.where(g == k, place(GROUPS[k][j]), at)
            ids.append(at)

        def hits(j, e):
            return tables[ids[j], 2 + e : 3 + e, :] == slot

        def choice(j):
            both = jnp.concatenate([hits(j, 0), hits(j, 1)], axis=0)
            return jnp.where(both, 1.0, 0.0).astype(jnp.bfloat16)

        for j in range(BLOCKS):
            picked[j] = jnp.dot(
                choice(j), rows_in[ids[j]], preferred_element_type=jnp.float32
            ).astype(jnp.bfloat16)
        for e in (0, 1):
            chosen = picked[:, e * SLOTS : (e + 1) * SLOTS, :].reshape(BLOCKS * SLOTS, width)
            gate = jnp.dot(chosen, weights[e, 0], preferred_element_type=jnp.float32)
            up = jnp.dot(chosen, weights[e, 1], preferred_element_type=jnp.float32)
            units = (gate / (1.0 + jnp.exp(-gate)) * up).astype(jnp.bfloat16)
            result = lax.dot_general(
                units, weights[e, 2], (((1,), (1,)), ((), ())), preferred_element_type=jnp.float32
            )
            for j in range(BLOCKS):
                gain = jnp.sum(
                    jnp.where(hits(j, e), tables[ids[j], e : e + 1, :], 0.0),
                    axis=1,
                    keepdims=True,
                )
                made[j, e * SLOTS : (e + 1) * SLOTS, :] = (
                    result[j * SLOTS : (j + 1) * SLOTS, :] * gain
                ).astype(jnp.bfloat16)
        for j in range(BLOCKS):
            sums[ids[j]] = lax.dot_general(
                choice(j), made[j], (((0,), (0,)), ((), ())), preferred_element_type=jnp.float32
            ).astype(jnp.bfloat16)
        return carry

    lax.fori_loop(0, len(GROUPS), group_step, 0)

    for group, j in PAIRS:
        for n in (0, 1):
            give_far(group, j, n).start()

    def add(at, held):
        sums[at] = (sums[at].astype(jnp.float32) + held.astype(jnp.float32)).astype(jnp.bfloat16)

    def relay_sums(group, j):
        for side in (0, 1):
            k = group * 4 + j * 2 + side
            give_far(group, j, side).wait_recv()
            add((place(near(group, j, side)), part(side)), hold_q[k])
            give_near(group, j, side, 1).start()

    def total(group, j):
        for side in (0, 1):
            for late in (0, 1):
                give_near(group, j, side, late).wait_recv()
        at = place((TWO[j], 0) if group == 0 else (0, ENDS[j]))
        k = group * 4 + j * 2
        return at, (
            sums[at].astype(jnp.float32)
            + hold_r[k].astype(jnp.float32)
            + hold_r[k + 1].astype(jnp.float32)
        )

    for group, j in PAIRS[:3]:
        relay_sums(group, j)
    at, value = total(0, 1)
    sums[at] = value.astype(jnp.bfloat16)
    for n in (0, 1):
        give_across(n).start()
    relay_sums(0, 0)
    for side in (0, 1):
        at, value = total(1, side)
        sums[at] = value.astype(jnp.bfloat16)
        give_back(side, 0).start()
    for side in (0, 1):
        give_across(side).wait_recv()
        add((place((0, ENDS[side])), part(side)), hold_p[side])
        give_back(side, 1).start()
    _, value = total(0, 0)
    out_sum = value + residual[...]
    for side in (0, 1):
        for late in (0, 1):
            give_back(side, late).wait_recv()
    out[...] = (
        out_sum + hold_d[0].astype(jnp.float32) + hold_d[1].astype(jnp.float32)
    ).astype(out.dtype)

    for n in (0, 1):
        emit(n).wait_send()
        pass_on(n).wait_send()
        give_across(n).wait_send()
        for late in (0, 1):
            give_back(n, late).wait_send()
    for n in range(8):
        weight_copy(n).wait_send()
    for group, j in PAIRS:
        for n in (0, 1):
            spread(group, j, n).wait_send()
            relay(group, j, n).wait_send()
            give_far(group, j, n).wait_send()
            for late in (0, 1):
                give_near(group, j, n, late).wait_send()


def normed(values, gain):
    mean_square = jnp.mean(values * values, axis=1, keepdims=True)
    return (values * lax.rsqrt(mean_square + epsilon) * gain[None]).astype(jnp.bfloat16)


def rotation_tables(plane, prompt_start, cosine, sine):
    rows = prompt_start.shape[1]
    half = HEAD_SIZE // 2
    lane = lax.broadcasted_iota(jnp.int32, (rows, 128), 1)
    begin = jnp.broadcast_to(prompt_start[...].astype(jnp.float32), (rows, rows)).T
    first = (plane.chip(0, 0) * 2 + plane.core) * rows
    position = first + lax.broadcasted_iota(jnp.int32, (rows, 128), 0)
    power = lax.rem(lane, half).astype(jnp.float32) / half
    angle = (position.astype(jnp.float32) - begin) * jnp.exp(power * -math.log(10000.0))
    cosine[...] = jnp.cos(angle)
    sine[...] = jnp.where(lax.rem(lane, HEAD_SIZE) < half, -jnp.sin(angle), jnp.sin(angle))


def layer_kernel(
    hidden, attn_gain, wq, wk, wv, wo, prompt_start, ffn_gain, routes, route_weights,
    first,
    out, key_cache, value_cache,
    query_w, key_w, value_w, output_w, own_in, residual, cosine, sine,
    queries, pairs, starts, given, attention, tables,
    near, store, asked, begin, begins, packed, peak, total, bias, done, replies,
    rows_in, sums, weights, picked, made, hold_q, hold_r, hold_p, hold_d,
    *sems,
):
    attention_sems, expert_sems, (w_send, w_recv, load_sems, row_sem) = (
        sems[:11],
        sems[11:21],
        sems[21:],
    )
    plane = Plane()
    core = plane.core
    rows, width = hidden.shape
    arrived = greet(plane)

    def lanes(r):
        return pl.ds(r * 128, 128)

    def weight_copy(n, incoming=False):
        half = width // 2
        e = 1 - core if incoming and n >= 4 else core
        if n < 2:
            src, dst = first, weights.at[e, :, :, lanes(1 + n)]
            to = plane.level((1, -1)[n])
        elif n < 4:
            span = pl.ds((n - 2) * half, half)
            src = weights.at[e, :, span, lanes(n - 1)]
            dst = weights.at[e, :, span, lanes(3)]
            to = plane.level((1, -1)[n - 2])
        else:
            dst = weights.at[e, :, :, lanes(n - 4)]
            src = first if n == 4 else dst
            to = plane.partner()
        return remote(src, dst, w_send.at[n], w_recv.at[n], to)

    loads = [
        pltpu.make_async_copy(src, dst, load_sems.at[n])
        for n, (src, dst) in enumerate(
            (
                (wk, key_w),
                (wv, value_w),
                (wq, query_w),
                (wo, output_w),
                (first, weights.at[core, :, :, lanes(0)]),
            )
        )
    ]
    for n in (2, 0, 1):
        loads[n].start()
    own_in[...] = normed(hidden[...].astype(jnp.float32), attn_gain[...])
    rotation_tables(plane, prompt_start, cosine, sine)
    arrived()
    for n in (0, 1, 4):
        weight_copy(n).start()

    lane = lax.broadcasted_iota(jnp.int32, (rows, 128), 1)
    first_half = lax.rem(lane, HEAD_SIZE) < HEAD_SIZE // 2

    def rotated(tile):
        other = jnp.where(
            first_half,
            pltpu.roll(tile, 128 - HEAD_SIZE // 2, axis=1),
            pltpu.roll(tile, HEAD_SIZE // 2, axis=1),
        )
        return tile * cosine[...] + other * sine[...]

    def project_keys():
        for load in loads[3:]:
            load.start()
        loads[0].wait()
        keys = jnp.dot(own_in[...], key_w[...], preferred_element_type=jnp.float32)
        loads[1].wait()
        values = jnp.dot(own_in[...], value_w[...], preferred_element_type=jnp.float32)
        value_cache[...] = values.astype(jnp.bfloat16)
        low = lane < HEAD_SIZE
        for p in range(KEY_VALUE_HEADS // 2):
            at = slice(p * 128, (p + 1) * 128)
            key, value = rotated(keys[:, at]), values[:, at]
            key_cache[:, at] = key.astype(jnp.bfloat16)
            sides = (
                jnp.where(low, key, pltpu.roll(value, HEAD_SIZE, axis=1)),
                jnp.where(low, pltpu.roll(key, HEAD_SIZE, axis=1), value),
            )
            for c in (0, 1):
                to = (c * SIDE + p) * 128
                pairs[:, to : to + 128] = sides[c].astype(jnp.bfloat16)

    def project_queries():
        starts[...] = jnp.broadcast_to(prompt_start[...].astype(jnp.float32), starts.shape)
        loads[2].wait()
        for c in range(3):
            part = jnp.dot(
                own_in[...],
                query_w[:, c * 512 : (c + 1) * 512],
                preferred_element_type=jnp.float32,
            )
            for p in range(4):
                at = c * 512 + p * 128
                queries[:, at : at + 128] = rotated(part[:, p * 128 : (p + 1) * 128]).astype(
                    jnp.bfloat16
                )

    def make_tables():
        expert = lax.broadcasted_iota(jnp.int32, (EXPERTS, rows), 0)
        gains = jnp.zeros((EXPERTS, rows), jnp.float32)
        named = jnp.zeros((EXPERTS, rows), jnp.float32)
        for j in range(TOP):
            hit = routes[j : j + 1, :] == expert
            gains = gains + jnp.where(hit, route_weights[j : j + 1, :], 0.0)
            named = named + jnp.where(hit, 1.0, 0.0)
        earlier = lax.broadcasted_iota(jnp.int32, (rows, rows), 0) < lax.broadcasted_iota(
            jnp.int32, (rows, rows), 1
        )
        ranks = jnp.dot(
            named.astype(jnp.bfloat16),
            jnp.where(earlier, 1.0, 0.0).astype(jnp.bfloat16),
            preferred_element_type=jnp.float32,
        )
        ranks = jnp.where(named > 0.0, ranks, -1.0)
        given[...] = jnp.zeros_like(given)
        for c in range(CHIPS):
            given[c, 0:2, :] = gains[2 * c : 2 * c + 2, :]
            given[c, 2:4, :] = ranks[2 * c : 2 * c + 2, :]

    attention_section(
        plane, weight_copy, project_keys, project_queries, make_tables,
        queries, pairs, starts, given, attention, tables,
        near, store, asked, begin, begins, packed, peak, total, bias, done, replies,
        *attention_sems,
    )

    loads[3].wait()
    for c in range(3):
        at = slice(c * 512, (c + 1) * 512)
        residual[:, at] = hidden[:, at].astype(jnp.float32) + jnp.dot(
            attention[...], output_w[:, at], preferred_element_type=jnp.float32
        )
    own_in[...] = normed(residual[...], ffn_gain[...])
    loads[4].wait()

    experts_section(
        plane, weight_copy, own_in, residual, tables, out,
        rows_in, sums, weights, picked, made, hold_q, hold_r, hold_p, hold_d,
        *expert_sems, row_sem,
    )


def run_layer(hidden, attn_gain, wq, wk, wv, wo, starts, ffn_gain, routes, gains, first):
    rows, width = hidden.shape
    cache = wk.shape[1]
    dma = pltpu.SemaphoreType.DMA
    vmem = pl.BlockSpec(memory_space=pltpu.VMEM)
    hbm = pl.BlockSpec(memory_space=pl.ANY)

    def brief(*shape):
        return pltpu.VMEM(shape, jnp.bfloat16)

    def full(*shape):
        return pltpu.VMEM(shape, jnp.float32)

    others = len(OTHERS)
    friends = len(FRIENDS)
    counts = (others, 6, 32, 2 * friends, friends)
    attention_sems = [dma((n,)) for n in counts for _ in (0, 1)] + [dma((8,))]
    expert_sems = [dma((n,)) for n in (20, 8, 16, 2, 4) for _ in (0, 1)]
    both = 2 * HEADS * rows
    return pl.pallas_call(
        layer_kernel,
        out_shape=(
            jax.ShapeDtypeStruct((rows, width), jnp.bfloat16),
            jax.ShapeDtypeStruct((rows, cache), jnp.bfloat16),
            jax.ShapeDtypeStruct((rows, cache), jnp.bfloat16),
        ),
        in_specs=[vmem, vmem, hbm, hbm, hbm, hbm] + [vmem] * 4 + [hbm],
        out_specs=(vmem,) * 3,
        scratch_shapes=[
            brief(*wq.shape),
            brief(*wk.shape),
            brief(*wv.shape),
            brief(*wo.shape),
            brief(rows, width),
            full(rows, width),
            full(rows, 128),
            full(rows, 128),
            brief(rows, width),
            brief(rows, 2 * cache),
            full(8, rows),
            full(CHIPS, 8, rows),
            brief(rows, width),
            full(CHIPS, 8, rows),
            brief(rows, 512),
            brief(CHIPS, 2 * rows, 128),
            brief(KEY_VALUE_HEADS, rows, ASK),
            full(KEY_VALUE_HEADS, 8, rows),
            full(KEY_VALUE_HEADS, rows, rows),
            brief(SIDE, both, 128),
            full(SIDE, both, 128),
            full(SIDE, both, 128),
            full(2 * rows, KEYS),
            brief(KEY_VALUE_HEADS, rows, ASK),
            brief(KEY_VALUE_HEADS, rows, ASK),
            brief(CHIPS, rows, width),
            brief(CHIPS, rows, width),
            brief(2, 3, width, FF),
            brief(BLOCKS, 2 * SLOTS, width),
            brief(BLOCKS, 2 * SLOTS, width),
            brief(8, rows // 2, width),
            brief(8, rows, width),
            brief(2, rows // 2, width),
            brief(2, rows, width),
            *attention_sems,
            *expert_sems,
            dma((8,)),
            dma((8,)),
            dma((5,)),
            dma,
        ],
        compiler_params=pltpu.CompilerParams(
            collective_id=0, has_side_effects=True, vmem_limit_bytes=63 << 20
        ),
        name="layer",
    )(
        hidden, attn_gain, wq, wk, wv, wo, starts, ffn_gain, routes, gains, first
    )


def publish(*results):
    def kernel(*refs):
        for src, dst in zip(refs[: len(results)], refs[len(results) :]):
            dst[...] = src[...]

    vmem = pl.BlockSpec(memory_space=pltpu.VMEM)
    return pl.pallas_call(
        kernel,
        out_shape=tuple(jax.ShapeDtypeStruct(r.shape, r.dtype) for r in results),
        in_specs=[vmem] * len(results),
        out_specs=(vmem,) * len(results),
        name="publish",
    )(*results)


def shards(
    hidden,
    attn_gain,
    query_weight,
    key_matrix,
    value_matrix,
    output_weight,
    prompt_start,
    ffn_gain,
    routes,
    route_weights,
    expert_weights,
):
    results = run_layer(
        hidden,
        attn_gain,
        query_weight,
        key_matrix,
        value_matrix,
        output_weight,
        prompt_start[None],
        ffn_gain,
        routes.T,
        route_weights.T,
        expert_weights[0],
    )
    return publish(*results)


def solution(mesh):
    in_specs = (
        P(("req", "exp"), None),
        P(),
        P(),
        P(),
        P(),
        P(),
        P(("req", "exp")),
        P(),
        P(("req", "exp"), None),
        P(("req", "exp"), None),
        P("exp", None, None, "req"),
    )
    out_specs = (P(("req", "exp"), None), P(("req", "exp"), None), P(("req", "exp"), None))
    return jax.shard_map(shards, mesh=mesh, in_specs=in_specs, out_specs=out_specs, check_vma=False)
```
